512 devices in a mesh: py: 32 (over z_hi, y, core), pz: 16 (over x, z_lo).
Axes of the slice: x: 4, y: 4, z: 16 (z_hi: 4, z_lo: 4; z = z_hi * 4 + z_lo), core: 2. Of those that a mesh axis runs over, the one named last changes fastest.
Arguments:
- solution: float32 [256, 256, 512], P('py', 'pz'), may hold values from -6 to 6
- right_side: float32 [256, 256, 512], P('py', 'pz'), may hold values from -6 to 6
- span_index: int32 [256, 256, 512], P('py', 'pz'), may hold values from 0 to 7
- coef_table: float32 [8], replicated, may hold values from 0.5 to 2
- xaxis_bands: float32 [2, 7, 512], replicated, may hold values from -0.5 to 0.5
- yaxis_bands: float32 [2, 7, 256], P(None, None, 'py'), may hold values from -0.5 to 0.5
- zaxis_bands: float32 [2, 7, 256], P(None, None, 'pz'), may hold values from -0.5 to 0.5
- xaxis_vectors: float32 [512, 512], replicated, may hold values from -0.25 to 0.25
- yaxis_vectors: float32 [256, 256], replicated, may hold values from -0.375 to 0.375
- zaxis_vectors: float32 [256, 256], replicated, may hold values from -0.375 to 0.375
- xaxis_values: float32 [512], replicated, may hold values from 0.25 to 2
- yaxis_values: float32 [256], replicated, may hold values from 0.25 to 2
- zaxis_values: float32 [256], replicated, may hold values from 0.25 to 2
Outputs:
- updated: float32 [256, 256, 512], P('py', 'pz')
- residual: float32 [256, 256, 512], P('py', 'pz')
The draws below stay inside these ranges and needn't reach their ends.
All inputs are finite; a program needn't handle non-finite values.
Results may differ from the reference program's by a relative error of at most 0.0001.
Values sent between devices are 32-bit elements; how exact they have to be, the bound alone decides.
A program may use at most 64 MiB of HBM per device.

```python
import math
import jax
import jax.numpy as jnp
from jax import lax

NX = 512
TABLE = 8
ITERS = 2
NY = 256
NZ = 256


def set_ends(drawn, own_key, smallest, high):
    index_at = [jax.random.randint(jax.random.fold_in(own_key, axis), (), 0, length) for axis, length in enumerate(drawn.shape)]
    widest = drawn.shape.index(max(drawn.shape))
    neighbour = index_at[:widest] + [(index_at[widest] + 1) % drawn.shape[widest]] + index_at[widest + 1:]
    return drawn.at[tuple(index_at)].set(smallest).at[tuple(neighbour)].set(high)


def steps_of(stream_key, shape, cuts, least, largest):
    factor_of = 1.0
    for position, parts in cuts:
        draws = jax.random.uniform(jax.random.fold_in(jax.random.fold_in(stream_key, 6), position), (parts,), jnp.float32, least / len(cuts), largest / len(cuts))
        factor_of = factor_of * jnp.repeat(jnp.exp(draws), shape[position] // parts).reshape((-1,) + (1,) * (len(shape) - 1 - position))
    return factor_of


def centred(stream_key, dims, spread, limit, split=(), dtype=jnp.bfloat16):
    array = jax.random.normal(stream_key, dims, jnp.float32) * spread
    if len(split) > 0:
        array = steps_of(stream_key, dims, split, -0.22, 0.18) * array
    return jnp.clip(array, min=-limit, max=limit).astype(dtype)


def setup_inputs(seed: int = 0) -> dict:
    arg_keys = jax.random.split(jax.random.key(seed), 14)
    return {
        "solution": centred(arg_keys[0], (NY, NZ, NX), 1.0, 6.0, ((0, 32), (1, 16)), jnp.float32),
        "right_side": centred(arg_keys[1], (NY, NZ, NX), 1.0, 6.0, ((0, 32), (1, 16)), jnp.float32),
        "span_index": set_ends(jax.random.randint(arg_keys[2], (NY, NZ, NX), 0, TABLE), jax.random.fold_in(arg_keys[2], 1), 0, TABLE - 1).astype(jnp.int32),
        "coef_table": jnp.clip(jnp.exp(jax.random.uniform(arg_keys[3], (TABLE,), jnp.float32, math.log(0.5), math.log(2.0))), 0.5, 2.0),
        "xaxis_bands": jnp.clip(jax.random.uniform(arg_keys[4], (2, 7, NX), jnp.float32, -0.5, 0.5), -0.5, 0.5),
        "yaxis_bands": jnp.clip(jax.random.uniform(arg_keys[5], (2, 7, NY), jnp.float32, -0.5, 0.5) * steps_of(arg_keys[5], (2, 7, NY), ((2, 32),), -0.4, 0.0), -0.5, 0.5),
        "zaxis_bands": jnp.clip(jax.random.uniform(arg_keys[6], (2, 7, NZ), jnp.float32, -0.5, 0.5) * steps_of(arg_keys[6], (2, 7, NZ), ((2, 16),), -0.4, 0.0), -0.5, 0.5),
        "xaxis_vectors": centred(arg_keys[7], (NX, NX), NX ** -0.5, 0.25, (), jnp.float32),
        "yaxis_vectors": centred(arg_keys[8], (NY, NY), NY ** -0.5, 0.375, (), jnp.float32),
        "zaxis_vectors": centred(arg_keys[9], (NZ, NZ), NZ ** -0.5, 0.375, (), jnp.float32),
        "xaxis_values": jnp.clip(jnp.exp(jax.random.uniform(arg_keys[10], (NX,), jnp.float32, math.log(0.25), math.log(2.0))), 0.25, 2.0),
        "yaxis_values": jnp.clip(jnp.exp(jax.random.uniform(arg_keys[11], (NY,), jnp.float32, math.log(0.25), math.log(2.0))), 0.25, 2.0),
        "zaxis_values": jnp.clip(jnp.exp(jax.random.uniform(arg_keys[12], (NZ,), jnp.float32, math.log(0.25), math.log(2.0))), 0.25, 2.0),
    }


HIGH = lax.Precision.HIGHEST


def band_padded(padded, bands, axis):
    length = padded.shape[axis] - 6
    layout = [1, 1, 1]
    layout[axis] = length
    summed = None
    for offset in range(7):
        contrib = bands[offset].reshape(layout) * lax.slice_in_dim(padded, offset, offset + length, axis=axis)
        summed = contrib if summed is None else summed + contrib
    return summed


def band_apply(field, bands, axis):
    widths = [(0, 0), (0, 0), (0, 0)]
    widths[axis] = (3, 3)
    return band_padded(jnp.pad(field, widths), bands, axis)


def operate(field, coefficient, xaxis_bands, yaxis_bands, zaxis_bands):
    weighted = coefficient * field
    mass_part = band_apply(weighted, zaxis_bands[1], 1)
    stiff_part = band_apply(weighted, zaxis_bands[0], 1)
    mass_mass = band_apply(mass_part, yaxis_bands[1], 0)
    stiff_mass = band_apply(mass_part, yaxis_bands[0], 0)
    mass_stiff = band_apply(stiff_part, yaxis_bands[1], 0)
    return coefficient * (band_apply(mass_mass, xaxis_bands[0], 2) + band_apply(stiff_mass + mass_stiff, xaxis_bands[1], 2))


def reference(solution, right_side, span_index, coef_table, xaxis_bands, yaxis_bands, zaxis_bands, xaxis_vectors, yaxis_vectors, zaxis_vectors, xaxis_values, yaxis_values, zaxis_values):
    coefficient = coef_table[span_index]
    denominator = yaxis_values[:, None, None] + zaxis_values[None, :, None] + xaxis_values[None, None, :]
    updated = solution
    residual = right_side
    for iteration in range(ITERS):
        residual = right_side - operate(updated, coefficient, xaxis_bands, yaxis_bands, zaxis_bands)
        spectral = jnp.einsum('yzi,ij->yzj', residual, xaxis_vectors, precision=HIGH)
        spectral = jnp.einsum('izx,ij->jzx', spectral, yaxis_vectors, precision=HIGH)
        spectral = jnp.einsum('yix,ij->yjx', spectral, zaxis_vectors, precision=HIGH)
        spectral = spectral / denominator
        spectral = jnp.einsum('yjx,ij->yix', spectral, zaxis_vectors, precision=HIGH)
        spectral = jnp.einsum('jzx,ij->izx', spectral, yaxis_vectors, precision=HIGH)
        spectral = jnp.einsum('yzj,ij->yzi', spectral, xaxis_vectors, precision=HIGH)
        updated = updated + spectral
    return updated, residual
```

```python
import jax
import jax.numpy as jnp
from jax import lax
from jax.experimental import pallas as pl
from jax.experimental.pallas import tpu as pltpu
from jax.sharding import PartitionSpec as P

ITERS = 2
F32 = jnp.float32
BF16 = jnp.bfloat16
RING = (8, 7, 9, 6, 10, 5, 11, 4, 12, 3, 13, 2, 14, 1, 15)


def split(v):
    hi = v.astype(BF16)
    return hi, (v - hi.astype(F32)).astype(BF16)


def dot3(a, b, dims=((1,), (0,))):
    def one(p, q):
        return lax.dot_general(p, q, (dims, ((), ())), preferred_element_type=F32)

    return one(a[0], b[0]) + one(a[0], b[1]) + one(a[1], b[0])


def swap_blocks(v, sub, lane):
    far = pltpu.roll(pltpu.roll(v, 4, 0), 64, 1)
    v = jnp.where((sub // 4) == (lane // 64), v, far)
    for bit in (2, 1):
        width = 16 * bit
        s, l = (sub // bit) % 2, (lane // width) % 2
        down = pltpu.roll(pltpu.roll(v, bit, 0), 128 - width, 1)
        up = pltpu.roll(pltpu.roll(v, 8 - bit, 0), width, 1)
        v = jnp.where(s == l, v, jnp.where(s == 1, down, up))
    return v


def kernel(
    u_in, b_in, span_in, coef, xb, yb, zb, vx_in, vy_in, vz_in, xv, yv, zv,
    u_out, r_out,
    u, b, span, vx, vy, vz, c, r, zs, cs, hr, w, acc,
    s, ra, sb, rb, m, mb, rb2, sa2, ra2,
    bm_h, bm_l, vxt_h, vxt_l, vy_h, vy_l, vyt_h, vyt_l, vz_h, vz_l, den,
    load_sem, send_sem, recv_sem,
):
    py, pz = lax.axis_index("py"), lax.axis_index("pz")
    zh, yc = py // 8, py % 8
    x, zl = pz // 4, pz % 4
    g = yc * 4 + x
    q = zh * 4 + zl

    def device(py2, pz2):
        return {"py": py2, "pz": pz2}

    def group(g2):
        return device(zh * 8 + g2 // 4, (g2 % 4) * 4 + zl)

    def ring(q2):
        return device((q2 // 4) * 8 + yc, x * 4 + q2 % 4)

    def near(dy, dz):
        return device((py + 32 + dy) % 32, (pz + 16 + dz) % 16)

    loads = [
        pltpu.make_async_copy(src, dst, load_sem.at[i])
        for i, (src, dst) in enumerate(
            ((u_in, u), (span_in, span), (vx_in, vx), (vy_in, vy), (vz_in, vz), (b_in, b))
        )
    ]
    for load in loads:
        load.start()

    barrier = pltpu.get_barrier_semaphore()

    def greet(k, carry):
        pl.semaphore_signal(barrier, inc=1, device_id=group((g + k) % 32))
        return carry

    lax.fori_loop(1, 32, greet, 0)

    def greet_ring(k, carry):
        pl.semaphore_signal(barrier, inc=1, device_id=ring((q + k) % 16))
        return carry

    lax.fori_loop(1, 16, greet_ring, 0)
    sides = [(dy, dz) for dy in (-1, 0, 1) for dz in (-1, 0, 1) if dy or dz]
    for dy, dz in sides:
        pl.semaphore_signal(barrier, inc=1, device_id=near(dy, dz))

    cs[...] = jnp.zeros_like(cs)
    for it in range(ITERS):
        hr[it, pl.ds(208, 48), :] = jnp.zeros((48, 512), F32)

    loads[0].wait()
    loads[1].wait()

    def weigh(i, carry):
        rows = pl.ds(pl.multiple_of(i * 8, 8), 8)
        at = span[rows, :]
        v = jnp.full((8, 512), coef[0], F32)
        for e in range(1, 8):
            v = jnp.where(at == e, coef[e], v)
        c[rows, :] = v
        w[0, rows, :] = v * u[rows, :]
        return carry

    lax.fori_loop(0, 16, weigh, 0)
    pl.semaphore_wait(barrier, 31 + 15 + 8)

    sub = lax.broadcasted_iota(jnp.int32, (8, 128), 0)
    lane = lax.broadcasted_iota(jnp.int32, (8, 128), 1)

    def prepare():
        def coords(tile):
            if tile == 2:
                return lane // 16, lane % 16
            col = lane + tile * 128
            yy = jnp.where(col < 48, col // 16 - 3, 8 + (col - 48) // 16)
            zz = col % 16
            k = col - 96
            edge = col >= 96
            yy = jnp.where(edge, k % 8, yy)
            zz = jnp.where(edge, jnp.where(k < 24, k // 8 - 3, 16 + (k - 24) // 8), zz)
            k = col - 144
            corner = k >= 0
            cc = k % 16
            y3 = jnp.where(cc >= 6, 2, jnp.where(cc >= 3, 1, 0))
            z3 = cc - 3 * y3
            t = k // 16
            yy = jnp.where(corner, jnp.where(t < 2, y3 - 3, 8 + y3), yy)
            zz = jnp.where(corner, jnp.where(t % 2 == 0, z3 - 3, 16 + z3), zz)
            bad = (corner & (cc >= 9)) | (col >= 208)
            gy, gz = py * 8 + yy, pz * 16 + zz
            bad = bad | (gy < 0) | (gy > 255) | (gz < 0) | (gz > 255)
            return jnp.where(bad, 1000, yy), jnp.where(bad, 1000, zz)

        for tile in range(3):
            yy, zz = coords(tile)
            ez = {}
            for half in range(2):
                dz = zz - (half * 8 + sub) + 3
                for kind in range(2):
                    total = jnp.zeros((8, 128), F32)
                    for k in range(7):
                        column = jnp.zeros((8, 128), F32)
                        for row in range(8):
                            column = jnp.where(sub == row, zb[kind, k, half * 8 + row], column)
                        total = jnp.where(dz == k, column, total)
                    ez[kind, half] = total

            def rows_of(y, carry, yy=yy, ez=ez, tile=tile):
                dy = yy - y + 3
                ey = []
                for kind in range(2):
                    total = jnp.zeros((8, 128), F32)
                    for k in range(7):
                        total = jnp.where(dy == k, yb[kind, k, y], total)
                    ey.append(total)
                mass = [ey[1] * ez[1, half] for half in range(2)]
                stiff = [ey[0] * ez[1, half] + ey[1] * ez[0, half] for half in range(2)]
                for base, pair in ((0, mass), (128, stiff)):
                    hi, lo = split(jnp.concatenate(pair, axis=0))
                    at = pl.ds(pl.multiple_of(base + y * 16, 16), 16)
                    bm_h[at, tile * 128 : tile * 128 + 128] = hi
                    bm_l[at, tile * 128 : tile * 128 + 128] = lo
                return carry

            lax.fori_loop(0, 8, rows_of, 0)
        loads[2].wait()
        for i in range(4):
            cols = slice(i * 128, i * 128 + 128)
            hi, lo = split(jnp.transpose(vx[:, cols]))
            vxt_h[cols, :] = hi
            vxt_l[cols, :] = lo
        loads[3].wait()
        vy_h[...], vy_l[...] = split(vy[...])
        vyt_h[...], vyt_l[...] = split(jnp.transpose(vy[...]))
        loads[4].wait()
        for p in range(2):
            for e in range(2):
                for xx in range(4):
                    to = p * 128 + e * 64 + xx * 16
                    at = xx * 64 + (2 * p + e) * 16
                    hi, lo = split(vz[at : at + 16, :])
                    vz_h[to : to + 16, :] = hi
                    vz_l[to : to + 16, :] = lo
        column = jnp.transpose(jnp.broadcast_to(yv[...], (128, 256)))
        j = g * 16 + q
        row = lax.broadcasted_iota(jnp.int32, (1, 512), 1)
        mine = jnp.sum(jnp.where(row == j, xv[...], 0.0), axis=1, keepdims=True)
        for half in range(2):
            cols = slice(half * 128, half * 128 + 128)
            den[:, cols] = (column + zv[:, cols]) + mine
        loads[5].wait()

    def step(it, carry):
        for i in range(3):
            for side, first in enumerate((0, 13)):
                for t in range(4):
                    cols = slice(t * 128, t * 128 + 128)
                    full = w[it, :, cols].reshape(8, 16, 128)
                    zs[it, side, i * 8 : i * 8 + 8, cols] = full[:, first + i, :]
        for cy in range(2):
            for cz in range(2):
                for i in range(3):
                    row = (cy * 5 + i) * 16 + cz * 13
                    cs[it, cy * 2 + cz, i * 3 : i * 3 + 3, :] = w[it, row : row + 3, :]
        own = w.at[it]
        rims = (
            (own.at[80:128], 0, 48, near(1, 0)),
            (own.at[0:48], 48, 48, near(-1, 0)),
            (zs.at[it, 1], 96, 24, near(0, 1)),
            (zs.at[it, 0], 120, 24, near(0, -1)),
            (cs.at[it, 3], 144, 16, near(1, 1)),
            (cs.at[it, 2], 160, 16, near(1, -1)),
            (cs.at[it, 1], 176, 16, near(-1, 1)),
            (cs.at[it, 0], 192, 16, near(-1, -1)),
        )
        for src, first, count, where in rims:
            pltpu.make_async_remote_copy(
                src, hr.at[it, first : first + count], send_sem.at[it, 0], recv_sem.at[it, 0],
                device_id=where,
            ).start()

        pl.when(it == 0)(prepare)

        wide = split(w[it])
        acc[...] = dot3((bm_h[:, 256:384], bm_l[:, 256:384]), wide)
        pltpu.make_async_remote_copy(
            hr.at[it, 0:208], hr.at[it, 0:208], send_sem.at[it, 0], recv_sem.at[it, 0],
            device_id=near(1, 0),
        ).wait_recv()
        wide = split(hr[it])
        acc[...] += dot3((bm_h[:, 0:256], bm_l[:, 0:256]), wide)

        place = lax.broadcasted_iota(jnp.int32, (1, 512), 1)

        def along_x(i, carry):
            rows = pl.ds(pl.multiple_of(i * 8, 8), 8)
            more = pl.ds(pl.multiple_of(128 + i * 8, 8), 8)
            mass, stiff = acc[rows, :], acc[more, :]
            total = jnp.zeros((8, 512), F32)
            for k in range(7):
                d = k - 3
                inside = (place + d >= 0) & (place + d < 512)
                kx = jnp.where(inside, xb[0, k : k + 1, :], 0.0)
                mx = jnp.where(inside, xb[1, k : k + 1, :], 0.0)
                if d:
                    a = pltpu.roll(mass, (512 - d) % 512, 1)
                    e = pltpu.roll(stiff, (512 - d) % 512, 1)
                else:
                    a, e = mass, stiff
                total = total + (kx * a + mx * e)
            r[rows, :] = b[rows, :] - c[rows, :] * total
            return carry

        lax.fori_loop(0, 16, along_x, 0)

        wide = split(r[...])
        for i in range(4):
            rows = slice(i * 128, i * 128 + 128)
            s[it, rows, :] = dot3((vxt_h[rows, :], vxt_l[rows, :]), wide, ((1,), (1,)))

        def send_group(src, dst, stage):
            def one(k, carry):
                g2 = (g + k) % 32
                pltpu.make_async_remote_copy(
                    src.at[it, pl.ds(pl.multiple_of(g2 * 16, 16), 16)],
                    dst.at[it, pl.ds(pl.multiple_of(g * 16, 16), 16)],
                    send_sem.at[it, stage], recv_sem.at[it, stage], device_id=group(g2),
                ).start()
                return carry

            lax.fori_loop(1, 32, one, 0)
            mine = pl.ds(pl.multiple_of(g * 16, 16), 16)
            dst[it, mine, :] = src[it, mine, :]

        def wait_group(dst, stage):
            part = dst.at[it, 0 : 31 * 16]
            pltpu.make_async_remote_copy(
                part, part, send_sem.at[it, stage], recv_sem.at[it, stage],
                device_id=group((g + 1) % 32),
            ).wait_recv()

        def send_ring(src, dst, stage):
            for k in RING:
                q2 = (q + k) % 16
                pltpu.make_async_remote_copy(
                    src.at[it, q2], dst.at[it, q],
                    send_sem.at[it, stage], recv_sem.at[it, stage], device_id=ring(q2),
                ).start()
            dst[it, q] = src[it, q]

        def wait_ring(dst, stage):
            part = dst.at[it, 0:15]
            pltpu.make_async_remote_copy(
                part, part, send_sem.at[it, stage], recv_sem.at[it, stage],
                device_id=ring((q + 1) % 16),
            ).wait_recv()

        send_group(s, ra, 1)
        wait_group(ra, 1)
        for k in range(16):
            sb[it, k] = ra[it, pl.ds(k, 32, stride=16), :]
        send_ring(sb, rb, 2)
        wait_ring(rb, 2)

        def gather(i, carry):
            h, y4 = i // 4, i % 4
            rows = pl.ds(pl.multiple_of(y4 * 8, 8), 8)
            for p in range(2):
                a = swap_blocks(rb[it, h * 4 + 2 * p, rows, :], sub, lane)
                e = swap_blocks(rb[it, h * 4 + 2 * p + 1, rows, :], sub, lane)
                low = jnp.where(lane < 64, a, pltpu.roll(e, 64, 1))
                high = jnp.where(lane < 64, pltpu.roll(a, 64, 1), e)
                cols = slice(p * 128, p * 128 + 128)
                m[pl.ds(pl.multiple_of(i * 16, 8), 8), cols] = low
                m[pl.ds(pl.multiple_of(i * 16 + 8, 8), 8), cols] = high
            return carry

        lax.fori_loop(0, 16, gather, 0)
        vzs = (vz_h[...], vz_l[...])
        m[...] = dot3(split(m[...]), vzs)
        m[...] = dot3((vyt_h[...], vyt_l[...]), split(m[...])) / den[...]
        m[...] = dot3((vy_h[...], vy_l[...]), split(m[...]))
        m[...] = dot3(split(m[...]), vzs, ((1,), (1,)))

        def scatter(i, carry):
            h, y4 = i // 4, i % 4
            rows = pl.ds(pl.multiple_of(y4 * 8, 8), 8)
            for p in range(2):
                cols = slice(p * 128, p * 128 + 128)
                low = m[pl.ds(pl.multiple_of(i * 16, 8), 8), cols]
                high = m[pl.ds(pl.multiple_of(i * 16 + 8, 8), 8), cols]
                a = jnp.where(lane < 64, low, pltpu.roll(high, 64, 1))
                e = jnp.where(lane < 64, pltpu.roll(low, 64, 1), high)
                mb[it, h * 4 + 2 * p, rows, :] = swap_blocks(a, sub, lane)
                mb[it, h * 4 + 2 * p + 1, rows, :] = swap_blocks(e, sub, lane)
            return carry

        lax.fori_loop(0, 16, scatter, 0)
        send_ring(mb, rb2, 3)
        wait_ring(rb2, 3)
        for k in range(16):
            for h in range(4):
                rows = rb2[it, k, h * 8 : h * 8 + 8, :]
                sa2[it, pl.ds(h * 128 + k, 8, stride=16), :] = rows
        send_group(sa2, ra2, 4)
        wait_group(ra2, 4)
        wide = split(jnp.transpose(ra2[it]))
        u[...] += dot3(wide, (vxt_h[...], vxt_l[...]))

        @pl.when(it + 1 < ITERS)
        def _():
            w[ITERS - 1] = c[...] * u[...]

        return carry

    lax.fori_loop(0, ITERS, step, 0)
    u_out[...] = u[...]
    r_out[...] = r[...]

    for it in range(ITERS):
        sent = hr.at[it, 0:208]
        pltpu.make_async_remote_copy(
            sent, sent, send_sem.at[it, 0], recv_sem.at[it, 0], device_id=near(1, 0)
        ).wait_send()
        for stage, part in ((1, s.at[it, 0:496]), (2, sb.at[it, 0:15]), (3, mb.at[it, 0:15]), (4, sa2.at[it, 0:496])):
            pltpu.make_async_remote_copy(
                part, part, send_sem.at[it, stage], recv_sem.at[it, stage], device_id=near(1, 0)
            ).wait_send()


def shards(solution, right_side, span_index, coef_table, xaxis_bands, yaxis_bands, zaxis_bands,
           xaxis_vectors, yaxis_vectors, zaxis_vectors, xaxis_values, yaxis_values, zaxis_values):
    flat = (128, 512)
    hbm = pl.BlockSpec(memory_space=pl.ANY)
    vmem = pl.BlockSpec(memory_space=pltpu.VMEM)
    smem = pl.BlockSpec(memory_space=pltpu.SMEM)
    V = pltpu.VMEM
    big = V((ITERS, 512, 128), F32)
    ring = V((ITERS, 16, 32, 128), F32)
    scratch = [
        V(flat, F32), V(flat, F32), V(flat, jnp.int32), V((512, 512), F32), V((256, 256), F32), V((256, 256), F32),
        V(flat, F32), V(flat, F32), V((ITERS, 2, 24, 512), F32), V((ITERS, 4, 16, 512), F32),
        V((ITERS, 256, 512), F32), V((ITERS, 128, 512), F32), V((256, 512), F32),
        big, big, ring, ring, V((256, 256), F32), ring, ring, big, big,
        V((256, 384), BF16), V((256, 384), BF16), V((512, 512), BF16), V((512, 512), BF16),
        V((256, 256), BF16), V((256, 256), BF16), V((256, 256), BF16), V((256, 256), BF16),
        V((256, 256), BF16), V((256, 256), BF16), V((256, 256), F32),
        pltpu.SemaphoreType.DMA((6,)), pltpu.SemaphoreType.DMA((ITERS, 5)), pltpu.SemaphoreType.DMA((ITERS, 5)),
    ]
    updated, residual = pl.pallas_call(
        kernel,
        out_shape=(jax.ShapeDtypeStruct(flat, F32), jax.ShapeDtypeStruct(flat, F32)),
        in_specs=[hbm, hbm, hbm, smem, vmem, smem, smem, hbm, hbm, hbm, vmem, vmem, vmem],
        out_specs=(vmem, vmem),
        scratch_shapes=scratch,
        compiler_params=pltpu.CompilerParams(collective_id=0, has_side_effects=True),
        name="richardson",
    )(
        solution.reshape(flat), right_side.reshape(flat), span_index.reshape(flat), coef_table,
        xaxis_bands, yaxis_bands, zaxis_bands, xaxis_vectors, yaxis_vectors, zaxis_vectors,
        xaxis_values.reshape(1, 512), yaxis_values.reshape(1, 256), zaxis_values.reshape(1, 256),
    )
    return updated.reshape(solution.shape), residual.reshape(solution.shape)


def solution(mesh):
    grid = P("py", "pz", None)
    return jax.shard_map(
        shards,
        mesh=mesh,
        in_specs=(grid, grid, grid, P(), P(), P(None, None, "py"), P(None, None, "pz"), P(), P(), P(), P(), P(), P()),
        out_specs=(grid, grid),
        check_vma=False,
    )
```

```python
import jax
import jax.numpy as jnp
from jax import lax
from jax.experimental import pallas as pl
from jax.experimental.pallas import tpu as pltpu
from jax.sharding import PartitionSpec as P

ITERS = 2
F32 = jnp.float32
BF16 = jnp.bfloat16
RING = (8, 7, 9, 6, 10, 5, 11, 4, 12, 3, 13, 2, 14, 1, 15)


def split(v):
    hi = v.astype(BF16)
    return hi, (v - hi.astype(F32)).astype(BF16)


def dot3(a, b, dims=((1,), (0,))):
    def one(p, q):
        return lax.dot_general(p, q, (dims, ((), ())), preferred_element_type=F32)

    return one(a[0], b[0]) + one(a[0], b[1]) + one(a[1], b[0])


def swap_blocks(v, lane):
    v = pltpu.roll(v, 0, 1, stride=16, stride_axis=0)
    for bit in (1, 2, 4):
        v = jnp.where((lane // (16 * bit)) % 2 == 1, pltpu.roll(v, 8 - bit, 0), v)
    return pltpu.roll(v, 0, 1, stride=16, stride_axis=0)


def kernel(
    u_in, b_in, span_in, coef, xb_in, yb_in, zb_in, vx_in, vy_in, vz_in, xv_in, yv_in, zv_in,
    u_out, r_out,
    u, b, span, vx, vy, vz, xb, yb, zb, xv, yv, zv, c, r, zs, cs, hc, rl, hr, w, acc,
    s, ra, sb, rb, m, mb, rb2, sa2, ra2,
    bm_h, bm_l, vxt_h, vxt_l, vy_h, vy_l, vyt_h, vyt_l, vz_h, vz_l, den,
    kx_h, kx_l, mx_h, mx_l, load_sem, send_sem, recv_sem,
):
    py, pz = lax.axis_index("py"), lax.axis_index("pz")
    zh, yc = py // 8, py % 8
    x, zl = pz // 4, pz % 4
    g = yc * 4 + x
    q = zh * 4 + zl

    def device(py2, pz2):
        return {"py": py2, "pz": pz2}

    def group(g2):
        return device(zh * 8 + g2 // 4, (g2 % 4) * 4 + zl)

    def ring(q2):
        return device((q2 // 4) * 8 + yc, x * 4 + q2 % 4)

    def near(dy, dz):
        return device((py + 32 + dy) % 32, (pz + 16 + dz) % 16)

    loads = [
        pltpu.make_async_copy(src, dst, load_sem.at[i])
        for i, (src, dst) in enumerate(
            ((u_in, u), (span_in, span), (vx_in, vx), (vy_in, vy), (vz_in, vz), (b_in, b),
             (xb_in, xb), (yb_in, yb), (zb_in, zb), (xv_in, xv), (yv_in, yv), (zv_in, zv))
        )
    ]
    for load in loads:
        load.start()

    barrier = pltpu.get_barrier_semaphore()

    def greet(k, carry):
        pl.semaphore_signal(barrier, inc=1, device_id=group((g + k) % 32))
        return carry

    lax.fori_loop(1, 32, greet, 0)

    def greet_ring(k, carry):
        pl.semaphore_signal(barrier, inc=1, device_id=ring((q + k) % 16))
        return carry

    lax.fori_loop(1, 16, greet_ring, 0)
    sides = [(dy, dz) for dy in (-1, 0, 1) for dz in (-1, 0, 1) if dy or dz]
    for dy, dz in sides:
        pl.semaphore_signal(barrier, inc=1, device_id=near(dy, dz))
    top, bottom = yc == 7, yc == 0
    above, below = ((zh + 1) % 4) * 8, ((zh + 3) % 4) * 8

    @pl.when(bottom)
    def _():
        for k in range(3):
            pl.semaphore_signal(barrier, inc=1, device_id=device(below + 2 * k + 1, pz))

    @pl.when(top)
    def _():
        for k in range(1, 4):
            pl.semaphore_signal(barrier, inc=1, device_id=device(above + 2 * k, pz))

    cs[...] = jnp.zeros_like(cs)
    for it in range(ITERS):
        hr[it, pl.ds(144, 112), :] = jnp.zeros((112, 512), F32)

    loads[0].wait()
    loads[1].wait()

    def weigh(i, carry):
        rows = pl.ds(pl.multiple_of(i * 8, 8), 8)
        at = span[rows, :]
        v = jnp.full((8, 512), coef[0], F32)
        for e in range(1, 8):
            v = jnp.where(at == e, coef[e], v)
        c[rows, :] = v
        w[0, rows, :] = v * u[rows, :]
        return carry

    lax.fori_loop(0, 16, weigh, 0)
    pl.semaphore_wait(barrier, 31 + 15 + 8 + jnp.where(top | bottom, 0, 1))

    sub = lax.broadcasted_iota(jnp.int32, (8, 128), 0)
    lane = lax.broadcasted_iota(jnp.int32, (8, 128), 1)

    def prepare():
        def coords(tile):
            if tile == 2:
                return lane // 16, lane % 16
            col = lane + tile * 128
            yy = jnp.where(col < 48, col // 16 - 3, 8 + (col - 48) // 16)
            zz = col % 16
            k = col - 96
            edge = col >= 96
            yy = jnp.where(edge, k % 8, yy)
            zz = jnp.where(edge, jnp.where(k < 24, k // 8 - 3, 16 + (k - 24) // 8), zz)
            k = col - 144
            corner = k >= 0
            cc = k % 16
            y3 = jnp.where(cc >= 6, 2, jnp.where(cc >= 3, 1, 0))
            z3 = cc - 3 * y3
            t = k // 16
            yy = jnp.where(corner, jnp.where(t < 2, y3 - 3, 8 + y3), yy)
            zz = jnp.where(corner, jnp.where(t % 2 == 0, z3 - 3, 16 + z3), zz)
            bad = (corner & (cc >= 9)) | (col >= 208)
            gy, gz = py * 8 + yy, pz * 16 + zz
            bad = bad | (gy < 0) | (gy > 255) | (gz < 0) | (gz > 255)
            return jnp.where(bad, 1000, yy), jnp.where(bad, 1000, zz)

        for i in (6, 7, 8):
            loads[i].wait()
        pick = lax.broadcasted_iota(jnp.int32, (8, 16), 1) - lax.broadcasted_iota(jnp.int32, (8, 16), 0)
        columns = {
            (kind, k, half): jnp.sum(
                jnp.where(pick == half * 8, zb[k, kind : kind + 1, :], 0.0), axis=1, keepdims=True
            )
            for kind in range(2) for k in range(7) for half in range(2)
        }
        for tile in range(3):
            yy, zz = coords(tile)
            ez = {}
            for half in range(2):
                dz = zz - (half * 8 + sub) + 3
                for kind in range(2):
                    total = jnp.zeros((8, 128), F32)
                    for k in range(7):
                        total = jnp.where(dz == k, columns[kind, k, half], total)
                    ez[kind, half] = total
            for y in range(8):
                dy = yy - y + 3
                ey = []
                for kind in range(2):
                    total = jnp.zeros((8, 128), F32)
                    for k in range(7):
                        total = jnp.where(dy == k, yb[k, kind : kind + 1, y : y + 1], total)
                    ey.append(total)
                mass = [ey[1] * ez[1, half] for half in range(2)]
                stiff = [ey[0] * ez[1, half] + ey[1] * ez[0, half] for half in range(2)]
                for base, pair in ((0, mass), (128, stiff)):
                    hi, lo = split(jnp.concatenate(pair, axis=0))
                    at = slice(base + y * 16, base + y * 16 + 16)
                    bm_h[at, tile * 128 : tile * 128 + 128] = hi
                    bm_l[at, tile * 128 : tile * 128 + 128] = lo
        for kind, (big, small) in enumerate(((kx_h, kx_l), (mx_h, mx_l))):
            for i in range(4):
                for j in range(4):
                    at = (slice(j * 128, j * 128 + 128), slice(i * 128, i * 128 + 128))
                    if abs(i - j) > 1:
                        big[at] = jnp.zeros((128, 128), BF16)
                        small[at] = jnp.zeros((128, 128), BF16)
                        continue
                    for part in range(0, 128, 16):
                        shape = (16, 128)
                        k_of = (j - i) * 128 + part + 3 + lax.broadcasted_iota(jnp.int32, shape, 0)
                        k_of = k_of - lax.broadcasted_iota(jnp.int32, shape, 1)
                        total = jnp.zeros(shape, F32)
                        for k in range(7):
                            total = jnp.where(k_of == k, xb[k, kind : kind + 1, at[1]], total)
                        hi, lo = split(total)
                        big[j * 128 + part : j * 128 + part + 16, at[1]] = hi
                        small[j * 128 + part : j * 128 + part + 16, at[1]] = lo
        loads[2].wait()
        for i in range(4):
            cols = slice(i * 128, i * 128 + 128)
            hi, lo = split(jnp.transpose(vx[:, cols]))
            vxt_h[cols, :] = hi
            vxt_l[cols, :] = lo
        loads[3].wait()
        vy_h[...], vy_l[...] = split(vy[...])
        vyt_h[...], vyt_l[...] = split(jnp.transpose(vy[...]))
        loads[4].wait()
        for p in range(2):
            for e in range(2):
                for xx in range(4):
                    to = p * 128 + e * 64 + xx * 16
                    at = xx * 64 + (2 * p + e) * 16
                    hi, lo = split(vz[at : at + 16, :])
                    vz_h[to : to + 16, :] = hi
                    vz_l[to : to + 16, :] = lo
        for i in (9, 10, 11):
            loads[i].wait()
        column = jnp.transpose(jnp.broadcast_to(yv[...], (128, 256)))
        j = g * 16 + q
        row = lax.broadcasted_iota(jnp.int32, (1, 512), 1)
        mine = jnp.sum(jnp.where(row == j, xv[...], 0.0), axis=1, keepdims=True)
        for half in range(2):
            cols = slice(half * 128, half * 128 + 128)
            den[:, cols] = (column + zv[:, cols]) + mine
        loads[5].wait()

    def step(it, carry):
        for i in range(3):
            for side, first in enumerate((0, 13)):
                for t in range(4):
                    cols = slice(t * 128, t * 128 + 128)
                    full = w[it, :, cols].reshape(8, 16, 128)
                    zs[it, side, i * 8 : i * 8 + 8, cols] = full[:, first + i, :]
        for cy in range(2):
            for cz in range(2):
                for i in range(3):
                    row = (cy * 5 + i) * 16 + cz * 13
                    three = w[it, row : row + 3, :]
                    for t in range(4):
                        at = t * 9 + i * 3
                        cs[it, cy * 2 + cz, at : at + 3, :] = three[:, t * 128 : t * 128 + 128]
        own = w.at[it]

        def push(src, dst, stage, where, out=None):
            pltpu.make_async_remote_copy(
                src, dst, send_sem.at[it, stage if out is None else out], recv_sem.at[it, stage], device_id=where
            ).start()

        quarter = [slice(k * 128, k * 128 + 128) for k in range(4)]

        @pl.when(top)
        def _():
            for k in range(3):
                push(own.at[80:128, quarter[k]], rl.at[it], 5, device(zh * 8 + 2 * k + 1, pz))
            push(own.at[80:128, quarter[3]], hr.at[it, 0:48, quarter[3]], 0, near(1, 0), 5)

        @pl.when(bottom)
        def _():
            for k in range(1, 4):
                push(own.at[0:48, quarter[k]], rl.at[it], 5, device(zh * 8 + 2 * k, pz))
            push(own.at[0:48, quarter[0]], hr.at[it, 48:96, quarter[0]], 0, near(-1, 0), 5)

        push(cs.at[it, 3], hc.at[it, 0], 6, near(1, 1))
        push(cs.at[it, 2], hc.at[it, 1], 6, near(1, -1))
        push(cs.at[it, 1], hc.at[it, 2], 6, near(-1, 1))
        push(cs.at[it, 0], hc.at[it, 3], 6, near(-1, -1))

        @pl.when(jnp.logical_not(top))
        def _():
            push(own.at[80:128], hr.at[it, 0:48], 0, near(1, 0))

        @pl.when(jnp.logical_not(bottom))
        def _():
            push(own.at[0:48], hr.at[it, 48:96], 0, near(-1, 0))

        push(zs.at[it, 1], hr.at[it, 96:120], 0, near(0, 1))
        push(zs.at[it, 0], hr.at[it, 120:144], 0, near(0, -1))

        @pl.when(jnp.logical_not(top | bottom))
        def _():
            pltpu.make_async_remote_copy(
                rl.at[it], rl.at[it], send_sem.at[it, 5], recv_sem.at[it, 5], device_id=near(1, 0)
            ).wait_recv()
            odd = yc % 2 == 1
            first = pl.multiple_of(jnp.where(odd, 0, 48), 8)
            cols = pl.ds(pl.multiple_of((yc // 2) * 128, 128), 128)
            push(rl.at[it], hr.at[it, pl.ds(first, 48), cols], 0,
                 device(jnp.where(odd, above, below + 7), pz), 7)

        pl.when(it == 0)(prepare)

        wide = split(w[it])
        acc[...] = dot3((bm_h[:, 256:384], bm_l[:, 256:384]), wide)
        pltpu.make_async_remote_copy(
            hr.at[it, 0:144], hr.at[it, 0:144], send_sem.at[it, 0], recv_sem.at[it, 0],
            device_id=near(1, 0),
        ).wait_recv()
        pltpu.make_async_remote_copy(
            hc.at[it], hc.at[it], send_sem.at[it, 6], recv_sem.at[it, 6], device_id=near(1, 0)
        ).wait_recv()
        for corner in range(4):
            for t in range(4):
                at = 144 + corner * 16
                hr[it, at : at + 9, quarter[t]] = hc[it, corner, t * 9 : t * 9 + 9, :]
        wide = split(hr[it])
        acc[...] += dot3((bm_h[:, 0:256], bm_l[:, 0:256]), wide)

        total = dot3(split(acc[0:128, :]), (kx_h[...], kx_l[...]))
        total = total + dot3(split(acc[128:256, :]), (mx_h[...], mx_l[...]))
        r[...] = b[...] - c[...] * total

        @pl.when(it == ITERS - 1)
        def _():
            pltpu.make_async_copy(r, r_out, load_sem.at[12]).start()

        turned = [r[((8 - i) % 8) * 16 : ((8 - i) % 8) * 16 + 16, :] for i in range(8)]
        wide = split(jnp.concatenate(turned, axis=0))
        for i in range(4):
            rows = slice(i * 128, i * 128 + 128)
            s[it, rows, :] = dot3((vxt_h[rows, :], vxt_l[rows, :]), wide, ((1,), (1,)))

        def send_group(src, dst, stage, place=lambda g2: g2):
            def one(k, carry):
                g2 = (g + k) % 32
                pltpu.make_async_remote_copy(
                    src.at[it, pl.ds(pl.multiple_of(place(g2) * 16, 16), 16)],
                    dst.at[it, pl.ds(pl.multiple_of(g * 16, 16), 16)],
                    send_sem.at[it, stage], recv_sem.at[it, stage], device_id=group(g2),
                ).start()
                return carry

            lax.fori_loop(1, 32, one, 0)
            mine = pl.ds(pl.multiple_of(g * 16, 16), 16)
            dst[it, mine, :] = src[it, pl.ds(pl.multiple_of(place(g) * 16, 16), 16), :]

        def wait_group(dst, stage):
            part = dst.at[it, 0 : 31 * 16]
            pltpu.make_async_remote_copy(
                part, part, send_sem.at[it, stage], recv_sem.at[it, stage],
                device_id=group((g + 1) % 32),
            ).wait_recv()

        def send_ring(src, dst, stage):
            for k in RING:
                q2 = (q + k) % 16
                pltpu.make_async_remote_copy(
                    src.at[it, q2], dst.at[it, q],
                    send_sem.at[it, stage], recv_sem.at[it, stage], device_id=ring(q2),
                ).start()
            dst[it, q] = src[it, q]

        def wait_ring(dst, stage):
            part = dst.at[it, 0:15]
            pltpu.make_async_remote_copy(
                part, part, send_sem.at[it, stage], recv_sem.at[it, stage],
                device_id=ring((q + 1) % 16),
            ).wait_recv()

        send_group(s, ra, 1)
        wait_group(ra, 1)
        for k in range(16):
            sb[it, k] = ra[it, pl.ds(k, 32, stride=16), :]
        send_ring(sb, rb, 2)
        wait_ring(rb, 2)

        for i in range(16):
            h, y4 = i // 4, i % 4
            rows = slice(y4 * 8, y4 * 8 + 8)
            for p in range(2):
                a = swap_blocks(rb[it, h * 4 + 2 * p, rows, :], lane)
                e = swap_blocks(rb[it, h * 4 + 2 * p + 1, rows, :], lane)
                cols = quarter[p]
                m[i * 16 : i * 16 + 8, cols] = jnp.where(lane < 64, a, pltpu.roll(e, 64, 1))
                m[i * 16 + 8 : i * 16 + 16, cols] = jnp.where(lane < 64, pltpu.roll(a, 64, 1), e)
        vzs = (vz_h[...], vz_l[...])
        m[...] = dot3(split(m[...]), vzs)
        m[...] = dot3((vyt_h[...], vyt_l[...]), split(m[...])) / den[...]
        m[...] = dot3((vy_h[...], vy_l[...]), split(m[...]))
        m[...] = dot3(split(m[...]), vzs, ((1,), (1,)))

        for i in range(16):
            h, y4 = i // 4, i % 4
            rows = slice(y4 * 8, y4 * 8 + 8)
            for p in range(2):
                cols = quarter[p]
                low = m[i * 16 : i * 16 + 8, cols]
                high = m[i * 16 + 8 : i * 16 + 16, cols]
                a = jnp.where(lane < 64, low, pltpu.roll(high, 64, 1))
                e = jnp.where(lane < 64, pltpu.roll(low, 64, 1), high)
                mb[it, h * 4 + 2 * p, rows, :] = swap_blocks(a, lane)
                mb[it, h * 4 + 2 * p + 1, rows, :] = swap_blocks(e, lane)
        send_ring(mb, rb2, 3)
        wait_ring(rb2, 3)
        for k in range(16):
            for h in range(4):
                rows = rb2[it, k, h * 8 : h * 8 + 8, :]
                sa2[it, pl.ds(h * 128 + k, 8, stride=16), :] = rows
        send_group(sa2, ra2, 4, lambda g2: (g2 // 8) * 8 + (8 - g2 % 8) % 8)
        wait_group(ra2, 4)
        wide = split(jnp.transpose(ra2[it]))
        u[...] += dot3(wide, (vxt_h[...], vxt_l[...]))

        @pl.when(it + 1 < ITERS)
        def _():
            w[ITERS - 1] = c[...] * u[...]

        return carry

    lax.fori_loop(0, ITERS, step, 0)
    last = pltpu.make_async_copy(u, u_out, load_sem.at[13])
    last.start()
    for it in range(ITERS):
        @pl.when(jnp.logical_not(top | bottom))
        def _(it=it):
            pltpu.make_async_remote_copy(
                hr.at[it, 0:144], hr.at[it, 0:144], send_sem.at[it, 0], recv_sem.at[it, 0], device_id=near(1, 0)
            ).wait_send()
            pltpu.make_async_remote_copy(
                rl.at[it], rl.at[it], send_sem.at[it, 7], recv_sem.at[it, 0], device_id=near(1, 0)
            ).wait_send()

        @pl.when(top | bottom)
        def _(it=it):
            for stage, part in ((0, hr.at[it, 0:96]), (5, hr.at[it, 0:48])):
                pltpu.make_async_remote_copy(
                    part, part, send_sem.at[it, stage], recv_sem.at[it, stage], device_id=near(1, 0)
                ).wait_send()

        for stage, part in (
            (6, hc.at[it]),
            (1, s.at[it, 0:496]), (2, sb.at[it, 0:15]), (3, mb.at[it, 0:15]), (4, sa2.at[it, 0:496])):
            pltpu.make_async_remote_copy(
                part, part, send_sem.at[it, stage], recv_sem.at[it, stage], device_id=near(1, 0)
            ).wait_send()
    last.wait()
    pltpu.make_async_copy(r, r_out, load_sem.at[12]).wait()


def finish(u_in, r_in, u_out, r_out):
    u_out[...] = u_in[...]
    r_out[...] = r_in[...]


def shards(solution, right_side, span_index, coef_table, xaxis_bands, yaxis_bands, zaxis_bands,
           xaxis_vectors, yaxis_vectors, zaxis_vectors, xaxis_values, yaxis_values, zaxis_values):
    flat = (128, 512)
    hbm = pl.BlockSpec(memory_space=pl.ANY)
    vmem = pl.BlockSpec(memory_space=pltpu.VMEM)
    smem = pl.BlockSpec(memory_space=pltpu.SMEM)
    V = pltpu.VMEM
    big = V((ITERS, 512, 128), F32)
    ring = V((ITERS, 16, 32, 128), F32)
    scratch = [
        V(flat, F32), V(flat, F32), V(flat, jnp.int32), V((512, 512), F32), V((256, 256), F32), V((256, 256), F32),
        V((7, 2, 512), F32), V((7, 2, 8), F32), V((7, 2, 16), F32), V((1, 512), F32), V((1, 256), F32), V((1, 256), F32),
        V(flat, F32), V(flat, F32), V((ITERS, 2, 24, 512), F32), V((ITERS, 4, 40, 128), F32),
        V((ITERS, 4, 40, 128), F32), V((ITERS, 48, 128), F32),
        V((ITERS, 256, 512), F32), V((ITERS, 128, 512), F32), V((256, 512), F32),
        big, big, ring, ring, V((256, 256), F32), ring, ring, big, big,
        V((256, 384), BF16), V((256, 384), BF16), V((512, 512), BF16), V((512, 512), BF16),
        V((256, 256), BF16), V((256, 256), BF16), V((256, 256), BF16), V((256, 256), BF16),
        V((256, 256), BF16), V((256, 256), BF16), V((256, 256), F32),
        V((512, 512), BF16), V((512, 512), BF16), V((512, 512), BF16), V((512, 512), BF16),
        pltpu.SemaphoreType.DMA((14,)), pltpu.SemaphoreType.DMA((ITERS, 8)), pltpu.SemaphoreType.DMA((ITERS, 8)),
    ]
    updated, residual = pl.pallas_call(
        kernel,
        out_shape=(jax.ShapeDtypeStruct(flat, F32), jax.ShapeDtypeStruct(flat, F32)),
        in_specs=[hbm, hbm, hbm, smem] + [hbm] * 9,
        out_specs=(hbm, hbm),
        scratch_shapes=scratch,
        compiler_params=pltpu.CompilerParams(collective_id=0, has_side_effects=True),
        name="richardson",
    )(
        solution.reshape(flat), right_side.reshape(flat), span_index.reshape(flat), coef_table,
        jnp.swapaxes(xaxis_bands, 0, 1), jnp.swapaxes(yaxis_bands, 0, 1), jnp.swapaxes(zaxis_bands, 0, 1),
        xaxis_vectors, yaxis_vectors, zaxis_vectors,
        xaxis_values.reshape(1, 512), yaxis_values.reshape(1, 256), zaxis_values.reshape(1, 256),
    )
    updated, residual = pl.pallas_call(
        finish,
        out_shape=(jax.ShapeDtypeStruct(flat, F32), jax.ShapeDtypeStruct(flat, F32)),
        in_specs=[vmem, vmem],
        out_specs=(vmem, vmem),
        name="finish",
    )(updated, residual)
    return updated.reshape(solution.shape), residual.reshape(solution.shape)


def solution(mesh):
    grid = P("py", "pz", None)
    return jax.shard_map(
        shards,
        mesh=mesh,
        in_specs=(grid, grid, grid, P(), P(), P(None, None, "py"), P(None, None, "pz"), P(), P(), P(), P(), P(), P()),
        out_specs=(grid, grid),
        check_vma=False,
    )
```

```python
import jax
import jax.numpy as jnp
from jax import lax
from jax.experimental import pallas as pl
from jax.experimental.pallas import tpu as pltpu
from jax.sharding import PartitionSpec as P

ITERS = 2
F32 = jnp.float32
BF16 = jnp.bfloat16
PLACES = ((2, 3), (4, 5), (6, 1), (0, 7))
RING = (8, 7, 9, 6, 10, 5, 11, 4, 12, 3, 13, 2, 14, 1, 15)


def split(v):
    hi = v.astype(BF16)
    return hi, (v - hi.astype(F32)).astype(BF16)


def dot3(a, b, dims=((1,), (0,))):
    def one(p, q):
        return lax.dot_general(p, q, (dims, ((), ())), preferred_element_type=F32)

    return one(a[0], b[0]) + one(a[0], b[1]) + one(a[1], b[0])


def swap_blocks(v, lane):
    v = pltpu.roll(v, 0, 1, stride=16, stride_axis=0)
    for bit in (1, 2, 4):
        v = jnp.where((lane // (16 * bit)) % 2 == 1, pltpu.roll(v, 8 - bit, 0), v)
    return pltpu.roll(v, 0, 1, stride=16, stride_axis=0)


def kernel(
    u_in, b_in, span_in, coef, xb_in, yb_in, zb_in, vx_in, vy_in, vz_in, xv_in, yv_in, zv_in,
    u_out, r_out,
    u, b, span, vx, vy, vz, xb, yb, zb, xv, yv, zv, c, r, zs, cs, hc, rl, hr, w, acc,
    s, ra, sb, rb, m, mb, rb2, sa2, ra2,
    bm_h, bm_l, vxt_h, vxt_l, vy_h, vy_l, vyt_h, vyt_l, vz_h, vz_l, den,
    kx_h, kx_l, mx_h, mx_l, load_sem, send_sem, recv_sem,
):
    py, pz = lax.axis_index("py"), lax.axis_index("pz")
    zh, yc = py // 8, py % 8
    x, zl = pz // 4, pz % 4
    top, bottom = yc == 7, yc == 0
    edge = top | bottom
    place = jnp.where(top, 7, jnp.where(bottom, 6, jnp.where(yc == 1, 5, yc - 2)))
    g = place * 4 + x
    q = zh * 4 + zl

    def device(py2, pz2):
        return {"py": py2, "pz": pz2}

    def group(g2):
        p = g2 // 4
        yc2 = jnp.where(p == 7, 7, jnp.where(p == 6, 0, jnp.where(p == 5, 1, p + 2)))
        return device(zh * 8 + yc2, (g2 % 4) * 4 + zl)

    def ring(q2):
        return device((q2 // 4) * 8 + yc, x * 4 + q2 % 4)

    def near(dy, dz):
        return device((py + 32 + dy) % 32, (pz + 16 + dz) % 16)

    loads = [
        pltpu.make_async_copy(src, dst, load_sem.at[i])
        for i, (src, dst) in enumerate(
            ((u_in, u), (span_in, span), (vx_in, vx), (vy_in, vy), (vz_in, vz), (b_in, b),
             (xb_in, xb), (yb_in, yb), (zb_in, zb), (xv_in, xv), (yv_in, yv), (zv_in, zv))
        )
    ]
    loads[0].start()
    loads[1].start()
    barrier = pltpu.get_barrier_semaphore()

    def greet(k, carry):
        pl.semaphore_signal(barrier, inc=1, device_id=group((g + k) % 32))
        return carry

    lax.fori_loop(1, 32, greet, 0)

    def greet_ring(k, carry):
        pl.semaphore_signal(barrier, inc=1, device_id=ring((q + k) % 16))
        return carry

    lax.fori_loop(1, 16, greet_ring, 0)
    sides = [(dy, dz) for dy in (-1, 0, 1) for dz in (-1, 0, 1) if dy or dz]
    for dy, dz in sides:
        pl.semaphore_signal(barrier, inc=1, device_id=near(dy, dz))
    above, below = ((zh + 1) % 4) * 8, ((zh + 3) % 4) * 8

    @pl.when(bottom)
    def _():
        for k in range(3):
            pl.semaphore_signal(barrier, inc=1, device_id=device(below + 2 * k + 1, pz))

    @pl.when(top)
    def _():
        for k in range(1, 4):
            pl.semaphore_signal(barrier, inc=1, device_id=device(above + 2 * k, pz))

    for load in loads[2:]:
        load.start()
    cs[...] = jnp.zeros_like(cs)
    for it in range(ITERS):
        hr[it, pl.ds(144, 112), :] = jnp.zeros((112, 512), F32)

    loads[0].wait()
    loads[1].wait()

    def weigh(i, carry):
        rows = pl.ds(pl.multiple_of(i * 8, 8), 8)
        at = span[rows, :]
        v = jnp.full((8, 512), coef[0], F32)
        for e in range(1, 8):
            v = jnp.where(at == e, coef[e], v)
        c[rows, :] = v
        w[0, rows, :] = v * u[rows, :]
        return carry

    lax.fori_loop(0, 16, weigh, 0)
    pl.semaphore_wait(barrier, 31 + 15 + 8 + jnp.where(top | bottom, 0, 1))

    sub = lax.broadcasted_iota(jnp.int32, (8, 128), 0)
    lane = lax.broadcasted_iota(jnp.int32, (8, 128), 1)

    def prepare():
        def coords(tile):
            if tile == 2:
                return lane // 16, lane % 16
            col = lane + tile * 128
            yy = jnp.where(col < 48, col // 16 - 3, 8 + (col - 48) // 16)
            zz = col % 16
            k = col - 96
            edge = col >= 96
            yy = jnp.where(edge, k % 8, yy)
            zz = jnp.where(edge, jnp.where(k < 24, k // 8 - 3, 16 + (k - 24) // 8), zz)
            k = col - 144
            corner = k >= 0
            cc = k % 16
            y3 = jnp.where(cc >= 6, 2, jnp.where(cc >= 3, 1, 0))
            z3 = cc - 3 * y3
            t = k // 16
            yy = jnp.where(corner, jnp.where(t < 2, y3 - 3, 8 + y3), yy)
            zz = jnp.where(corner, jnp.where(t % 2 == 0, z3 - 3, 16 + z3), zz)
            bad = (corner & (cc >= 9)) | (col >= 208)
            gy, gz = py * 8 + yy, pz * 16 + zz
            bad = bad | (gy < 0) | (gy > 255) | (gz < 0) | (gz > 255)
            return jnp.where(bad, 1000, yy), jnp.where(bad, 1000, zz)

        for i in (6, 7, 8):
            loads[i].wait()
        pick = lax.broadcasted_iota(jnp.int32, (8, 16), 1) - lax.broadcasted_iota(jnp.int32, (8, 16), 0)
        columns = {
            (kind, k, half): jnp.sum(
                jnp.where(pick == half * 8, zb[k, kind : kind + 1, :], 0.0), axis=1, keepdims=True
            )
            for kind in range(2) for k in range(7) for half in range(2)
        }
        for tile in range(3):
            yy, zz = coords(tile)
            ez = {}
            for half in range(2):
                dz = zz - (half * 8 + sub) + 3
                for kind in range(2):
                    total = jnp.zeros((8, 128), F32)
                    for k in range(7):
                        total = jnp.where(dz == k, columns[kind, k, half], total)
                    ez[kind, half] = total
            for y in range(8):
                dy = yy - y + 3
                ey = []
                for kind in range(2):
                    total = jnp.zeros((8, 128), F32)
                    for k in range(7):
                        total = jnp.where(dy == k, yb[k, kind : kind + 1, y : y + 1], total)
                    ey.append(total)
                mass = [ey[1] * ez[1, half] for half in range(2)]
                stiff = [ey[0] * ez[1, half] + ey[1] * ez[0, half] for half in range(2)]
                for base, pair in ((0, mass), (128, stiff)):
                    hi, lo = split(jnp.concatenate(pair, axis=0))
                    at = slice(base + y * 16, base + y * 16 + 16)
                    bm_h[at, tile * 128 : tile * 128 + 128] = hi
                    bm_l[at, tile * 128 : tile * 128 + 128] = lo
        for kind, (big, small) in enumerate(((kx_h, kx_l), (mx_h, mx_l))):
            for i in range(4):
                for j in range(4):
                    at = (slice(j * 128, j * 128 + 128), slice(i * 128, i * 128 + 128))
                    if abs(i - j) > 1:
                        big[at] = jnp.zeros((128, 128), BF16)
                        small[at] = jnp.zeros((128, 128), BF16)
                        continue
                    for part in range(0, 128, 16):
                        shape = (16, 128)
                        k_of = (j - i) * 128 + part + 3 + lax.broadcasted_iota(jnp.int32, shape, 0)
                        k_of = k_of - lax.broadcasted_iota(jnp.int32, shape, 1)
                        total = jnp.zeros(shape, F32)
                        for k in range(7):
                            total = jnp.where(k_of == k, xb[k, kind : kind + 1, at[1]], total)
                        hi, lo = split(total)
                        big[j * 128 + part : j * 128 + part + 16, at[1]] = hi
                        small[j * 128 + part : j * 128 + part + 16, at[1]] = lo
        loads[2].wait()
        for i in range(4):
            cols = slice(i * 128, i * 128 + 128)
            hi, lo = split(jnp.transpose(vx[:, cols]))
            vxt_h[cols, :] = hi
            vxt_l[cols, :] = lo
        loads[3].wait()
        vy_h[...], vy_l[...] = split(vy[...])
        vyt_h[...], vyt_l[...] = split(jnp.transpose(vy[...]))
        loads[4].wait()
        for p in range(2):
            for e in range(2):
                for xx in range(4):
                    to = p * 128 + e * 64 + xx * 16
                    at = xx * 64 + (2 * p + e) * 16
                    hi, lo = split(vz[at : at + 16, :])
                    vz_h[to : to + 16, :] = hi
                    vz_l[to : to + 16, :] = lo
        for i in (9, 10, 11):
            loads[i].wait()
        column = jnp.transpose(jnp.broadcast_to(yv[...], (128, 256)))
        j = g * 16 + q
        row = lax.broadcasted_iota(jnp.int32, (1, 512), 1)
        mine = jnp.sum(jnp.where(row == j, xv[...], 0.0), axis=1, keepdims=True)
        for half in range(2):
            cols = slice(half * 128, half * 128 + 128)
            den[:, cols] = (column + zv[:, cols]) + mine
        loads[5].wait()

    quarter = [slice(k * 128, k * 128 + 128) for k in range(4)]

    def push(it, src, dst, stage, where, out=None):
        pltpu.make_async_remote_copy(
            src, dst, send_sem.at[it, stage if out is None else out], recv_sem.at[it, stage], device_id=where
        ).start()

    def rims(it):
        for i in range(3):
            for side, first in enumerate((0, 13)):
                for t in range(4):
                    cols = slice(t * 128, t * 128 + 128)
                    full = w[it, :, cols].reshape(8, 16, 128)
                    zs[it, side, i * 8 : i * 8 + 8, cols] = full[:, first + i, :]
        for cy in range(2):
            for cz in range(2):
                for i in range(3):
                    row = (cy * 5 + i) * 16 + cz * 13
                    three = w[it, row : row + 3, :]
                    for t in range(4):
                        at = t * 9 + i * 3
                        cs[it, cy * 2 + cz, at : at + 3, :] = three[:, t * 128 : t * 128 + 128]
        own = w.at[it]

        @pl.when(top)
        def _():
            for k in range(3):
                push(it, own.at[80:128, quarter[k]], rl.at[it], 5, device(zh * 8 + 2 * k + 1, pz))
            push(it, own.at[80:128, quarter[3]], hr.at[it, 0:48, quarter[3]], 0, near(1, 0), 5)

        @pl.when(bottom)
        def _():
            for k in range(1, 4):
                push(it, own.at[0:48, quarter[k]], rl.at[it], 5, device(zh * 8 + 2 * k, pz))
            push(it, own.at[0:48, quarter[0]], hr.at[it, 48:96, quarter[0]], 0, near(-1, 0), 5)

        push(it, cs.at[it, 3], hc.at[it, 0], 6, near(1, 1))
        push(it, cs.at[it, 2], hc.at[it, 1], 6, near(1, -1))
        push(it, cs.at[it, 1], hc.at[it, 2], 6, near(-1, 1))
        push(it, cs.at[it, 0], hc.at[it, 3], 6, near(-1, -1))

        @pl.when(jnp.logical_not(top))
        def _():
            push(it, own.at[80:128], hr.at[it, 0:48], 0, near(1, 0))

        @pl.when(jnp.logical_not(bottom))
        def _():
            push(it, own.at[0:48], hr.at[it, 48:96], 0, near(-1, 0))

        push(it, zs.at[it, 1], hr.at[it, 96:120], 0, near(0, 1))
        push(it, zs.at[it, 0], hr.at[it, 120:144], 0, near(0, -1))

    def relay(it):
        @pl.when(jnp.logical_not(top | bottom))
        def _():
            pltpu.make_async_remote_copy(
                rl.at[it], rl.at[it], send_sem.at[it, 5], recv_sem.at[it, 5], device_id=near(1, 0)
            ).wait_recv()
            odd = yc % 2 == 1
            first = pl.multiple_of(jnp.where(odd, 0, 48), 8)
            cols = pl.ds(pl.multiple_of((yc // 2) * 128, 128), 128)
            push(it, rl.at[it], hr.at[it, pl.ds(first, 48), cols], 0,
                 device(jnp.where(odd, above, below + 7), pz), 7)

    rims(0)
    relay(0)
    prepare()

    def step(it, carry):
        wide = split(w[it])
        acc[...] = dot3((bm_h[:, 256:384], bm_l[:, 256:384]), wide)
        pltpu.make_async_remote_copy(
            hr.at[it, 0:144], hr.at[it, 0:144], send_sem.at[it, 0], recv_sem.at[it, 0],
            device_id=near(1, 0),
        ).wait_recv()
        pltpu.make_async_remote_copy(
            hc.at[it], hc.at[it], send_sem.at[it, 6], recv_sem.at[it, 6], device_id=near(1, 0)
        ).wait_recv()
        for corner in range(4):
            for t in range(4):
                at = 144 + corner * 16
                hr[it, at : at + 9, quarter[t]] = hc[it, corner, t * 9 : t * 9 + 9, :]
        wide = split(hr[it])
        acc[...] += dot3((bm_h[:, 0:256], bm_l[:, 0:256]), wide)

        total = dot3(split(acc[0:128, :]), (kx_h[...], kx_l[...]))
        total = total + dot3(split(acc[128:256, :]), (mx_h[...], mx_l[...]))
        r[...] = b[...] - c[...] * total

        @pl.when(it == ITERS - 1)
        def _():
            pltpu.make_async_copy(r, r_out, load_sem.at[12]).start()

        turned = [r[((8 - i) % 8) * 16 : ((8 - i) % 8) * 16 + 16, :] for i in range(8)]
        wide = split(jnp.concatenate(turned, axis=0))
        for i in range(4):
            rows = slice(i * 128, i * 128 + 128)
            s[it, rows, :] = dot3((vxt_h[rows, :], vxt_l[rows, :]), wide, ((1,), (1,)))

        def wait_rows(part, stage):
            pltpu.make_async_remote_copy(
                part, part, send_sem.at[it, 0], recv_sem.at[it, stage], device_id=near(1, 0)
            ).wait_recv()

        def send_ring(src, dst, rows, send, stage):
            for k in RING:
                q2 = (q + k) % 16
                pltpu.make_async_remote_copy(
                    src.at[it, q2, rows], dst.at[it, q, rows],
                    send_sem.at[it, send], recv_sem.at[it, stage], device_id=ring(q2),
                ).start()
            dst[it, q, rows] = src[it, q, rows]

        def block(i):
            return pl.ds(pl.multiple_of(i * 16, 16), 16)

        def send_block(k, carry):
            g2 = (g + k) % 32
            pltpu.make_async_remote_copy(
                s.at[it, block(g2)], ra.at[it, block(g)],
                send_sem.at[it, 1], recv_sem.at[it, jnp.where(edge, 8, 1)], device_id=group(g2),
            ).start()
            return carry

        lax.fori_loop(1, 32, send_block, 0)
        ra[it, block(g), :] = s[it, block(g), :]
        pl.when(edge)(lambda: wait_rows(ra.at[it, 0 : 24 * 16], 1))
        pl.when(jnp.logical_not(edge))(lambda: wait_rows(ra.at[it, 0 : 23 * 16], 1))
        for k in range(16):
            sb[it, k, 0:24] = ra[it, pl.ds(k, 24, stride=16), :]
        send_ring(sb, rb, slice(0, 24), 2, 2)
        pl.when(edge)(lambda: wait_rows(ra.at[it, 0 : 7 * 16], 8))
        pl.when(jnp.logical_not(edge))(lambda: wait_rows(ra.at[it, 0 : 8 * 16], 8))
        for k in range(16):
            sb[it, k, 24:32] = ra[it, pl.ds(24 * 16 + k, 8, stride=16), :]
        send_ring(sb, rb, slice(24, 32), 2, 2)
        wait_rows(rb.at[it, 0:15], 2)

        for h in range(4):
            for t in range(4):
                rows = slice(t * 8, t * 8 + 8)
                one, two = ((h * 8 + yy) * 8 for yy in PLACES[t])
                for p in range(2):
                    a = swap_blocks(rb[it, h * 4 + 2 * p, rows, :], lane)
                    e = swap_blocks(rb[it, h * 4 + 2 * p + 1, rows, :], lane)
                    m[one : one + 8, quarter[p]] = jnp.where(lane < 64, a, pltpu.roll(e, 64, 1))
                    m[two : two + 8, quarter[p]] = jnp.where(lane < 64, pltpu.roll(a, 64, 1), e)
        vzs = (vz_h[...], vz_l[...])
        m[...] = dot3(split(m[...]), vzs)
        m[...] = dot3((vyt_h[...], vyt_l[...]), split(m[...])) / den[...]
        m[...] = dot3((vy_h[...], vy_l[...]), split(m[...]))
        m[...] = dot3(split(m[...]), vzs, ((1,), (1,)))

        for t in (3, 0, 1, 2):
            rows = slice(t * 8, t * 8 + 8)
            for h in range(4):
                one, two = ((h * 8 + yy) * 8 for yy in PLACES[t])
                for p in range(2):
                    low, high = m[one : one + 8, quarter[p]], m[two : two + 8, quarter[p]]
                    a = jnp.where(lane < 64, low, pltpu.roll(high, 64, 1))
                    e = jnp.where(lane < 64, pltpu.roll(low, 64, 1), high)
                    mb[it, h * 4 + 2 * p, rows, :] = swap_blocks(a, lane)
                    mb[it, h * 4 + 2 * p + 1, rows, :] = swap_blocks(e, lane)
            send_ring(mb, rb2, rows, 3, 9 + t)
        for t in (3, 0, 1, 2):
            wait_rows(rb2.at[it, 0:15, 0:8], 9 + t)
            for k in range(16):
                sa2[it, pl.ds(t * 128 + k, 8, stride=16), :] = rb2[it, k, t * 8 : t * 8 + 8, :]
            for i in range(8):
                row = (g + i) % 8
                g2 = t * 8 + row
                src = block(t * 8 + (8 - row) % 8)

                @pl.when(g2 != g)
                def _(g2=g2, src=src):
                    pltpu.make_async_remote_copy(
                        sa2.at[it, src], ra2.at[it, block(g)],
                        send_sem.at[it, 4], recv_sem.at[it, 4], device_id=group(g2),
                    ).start()

                @pl.when(g2 == g)
                def _(src=src):
                    ra2[it, block(g), :] = sa2[it, src, :]

        pl.when(it + 1 < ITERS)(lambda: relay(it + 1))
        wait_rows(ra2.at[it, 0 : 31 * 16], 4)
        wide = split(jnp.transpose(ra2[it]))
        u[...] += dot3(wide, (vxt_h[...], vxt_l[...]))

        @pl.when(it + 1 < ITERS)
        def _():
            w[it + 1] = c[...] * u[...]
            rims(it + 1)

        return carry

    lax.fori_loop(0, ITERS, step, 0)
    last = pltpu.make_async_copy(u, u_out, load_sem.at[13])
    last.start()
    for it in range(ITERS):
        @pl.when(jnp.logical_not(top | bottom))
        def _(it=it):
            pltpu.make_async_remote_copy(
                hr.at[it, 0:144], hr.at[it, 0:144], send_sem.at[it, 0], recv_sem.at[it, 0], device_id=near(1, 0)
            ).wait_send()
            pltpu.make_async_remote_copy(
                rl.at[it], rl.at[it], send_sem.at[it, 7], recv_sem.at[it, 0], device_id=near(1, 0)
            ).wait_send()

        @pl.when(top | bottom)
        def _(it=it):
            for stage, part in ((0, hr.at[it, 0:96]), (5, hr.at[it, 0:48])):
                pltpu.make_async_remote_copy(
                    part, part, send_sem.at[it, stage], recv_sem.at[it, stage], device_id=near(1, 0)
                ).wait_send()

        for stage, part in (
            (6, hc.at[it]),
            (1, s.at[it, 0:496]), (2, sb.at[it, 0:15]), (3, mb.at[it, 0:15]), (4, sa2.at[it, 0:496])):
            pltpu.make_async_remote_copy(
                part, part, send_sem.at[it, stage], recv_sem.at[it, stage], device_id=near(1, 0)
            ).wait_send()
    last.wait()
    pltpu.make_async_copy(r, r_out, load_sem.at[12]).wait()


def finish(u_in, r_in, u_out, r_out):
    u_out[...] = u_in[...]
    r_out[...] = r_in[...]


def shards(solution, right_side, span_index, coef_table, xaxis_bands, yaxis_bands, zaxis_bands,
           xaxis_vectors, yaxis_vectors, zaxis_vectors, xaxis_values, yaxis_values, zaxis_values):
    flat = (128, 512)
    hbm = pl.BlockSpec(memory_space=pl.ANY)
    vmem = pl.BlockSpec(memory_space=pltpu.VMEM)
    smem = pl.BlockSpec(memory_space=pltpu.SMEM)
    V = pltpu.VMEM
    big = V((ITERS, 512, 128), F32)
    ring = V((ITERS, 16, 32, 128), F32)
    scratch = [
        V(flat, F32), V(flat, F32), V(flat, jnp.int32), V((512, 512), F32), V((256, 256), F32), V((256, 256), F32),
        V((7, 2, 512), F32), V((7, 2, 8), F32), V((7, 2, 16), F32), V((1, 512), F32), V((1, 256), F32), V((1, 256), F32),
        V(flat, F32), V(flat, F32), V((ITERS, 2, 24, 512), F32), V((ITERS, 4, 40, 128), F32),
        V((ITERS, 4, 40, 128), F32), V((ITERS, 48, 128), F32),
        V((ITERS, 256, 512), F32), V((ITERS, 128, 512), F32), V((256, 512), F32),
        big, big, ring, ring, V((256, 256), F32), ring, ring, big, big,
        V((256, 384), BF16), V((256, 384), BF16), V((512, 512), BF16), V((512, 512), BF16),
        V((256, 256), BF16), V((256, 256), BF16), V((256, 256), BF16), V((256, 256), BF16),
        V((256, 256), BF16), V((256, 256), BF16), V((256, 256), F32),
        V((512, 512), BF16), V((512, 512), BF16), V((512, 512), BF16), V((512, 512), BF16),
        pltpu.SemaphoreType.DMA((14,)), pltpu.SemaphoreType.DMA((ITERS, 8)), pltpu.SemaphoreType.DMA((ITERS, 13)),
    ]
    updated, residual = pl.pallas_call(
        kernel,
        out_shape=(jax.ShapeDtypeStruct(flat, F32), jax.ShapeDtypeStruct(flat, F32)),
        in_specs=[hbm, hbm, hbm, smem] + [hbm] * 9,
        out_specs=(hbm, hbm),
        scratch_shapes=scratch,
        compiler_params=pltpu.CompilerParams(collective_id=0, has_side_effects=True),
        name="richardson",
    )(
        solution.reshape(flat), right_side.reshape(flat), span_index.reshape(flat), coef_table,
        jnp.swapaxes(xaxis_bands, 0, 1), jnp.swapaxes(yaxis_bands, 0, 1), jnp.swapaxes(zaxis_bands, 0, 1),
        xaxis_vectors, yaxis_vectors, zaxis_vectors,
        xaxis_values.reshape(1, 512), yaxis_values.reshape(1, 256), zaxis_values.reshape(1, 256),
    )
    updated, residual = pl.pallas_call(
        finish,
        out_shape=(jax.ShapeDtypeStruct(flat, F32), jax.ShapeDtypeStruct(flat, F32)),
        in_specs=[vmem, vmem],
        out_specs=(vmem, vmem),
        name="finish",
    )(updated, residual)
    return updated.reshape(solution.shape), residual.reshape(solution.shape)


def solution(mesh):
    grid = P("py", "pz", None)
    return jax.shard_map(
        shards,
        mesh=mesh,
        in_specs=(grid, grid, grid, P(), P(), P(None, None, "py"), P(None, None, "pz"), P(), P(), P(), P(), P(), P()),
        out_specs=(grid, grid),
        check_vma=False,
    )
```

```python
import jax
import jax.numpy as jnp
from jax import lax
from jax.experimental import pallas as pl
from jax.experimental.pallas import tpu as pltpu
from jax.sharding import PartitionSpec as P

ITERS = 2
F32 = jnp.float32
BF16 = jnp.bfloat16
PLACES = ((0, 1), (2, 3), (4, 5), (6, 7))
RING = (8, 7, 9, 6, 10, 5, 11, 4, 12, 3, 13, 2, 14, 1, 15)


def split(v):
    hi = v.astype(BF16)
    return hi, (v - hi.astype(F32)).astype(BF16)


def dot3(a, b, dims=((1,), (0,))):
    def one(p, q):
        return lax.dot_general(p, q, (dims, ((), ())), preferred_element_type=F32)

    return one(a[0], b[0]) + one(a[0], b[1]) + one(a[1], b[0])


def swap_blocks(v, lane):
    v = pltpu.roll(v, 0, 1, stride=16, stride_axis=0)
    for bit in (1, 2, 4):
        v = jnp.where((lane // (16 * bit)) % 2 == 1, pltpu.roll(v, 8 - bit, 0), v)
    return pltpu.roll(v, 0, 1, stride=16, stride_axis=0)


def kernel(
    u_in, b_in, span_in, coef, xb_in, yb_in, zb_in, vx_in, vy_in, vz_in, xv_in, yv_in, zv_in,
    u_out, r_out,
    u, b, span, vx, vy, vz, xb, yb, zb, xv, yv, zv, c, r, zs, cs, hc, rl, hr, w, acc,
    s, ra, sb, rb, rc, se, rd, m, mb, rb2, sa2, rm, sn, ra2,
    bm_h, bm_l, vxt_h, vxt_l, vy_h, vy_l, vyt_h, vyt_l, vz_h, vz_l, den,
    kx_h, kx_l, mx_h, mx_l, load_sem, send_sem, recv_sem,
):
    py, pz = lax.axis_index("py"), lax.axis_index("pz")
    zh, yc = py // 8, py % 8
    x, zl = pz // 4, pz % 4
    top, bottom = yc == 7, yc == 0
    edge = top | bottom
    core = yc % 2
    first, second = core == 0, core == 1
    g = yc * 4 + x
    mine = (yc // 2) * 4 + x
    q = zh * 4 + zl

    def device(py2, pz2):
        return {"py": py2, "pz": pz2}

    def group(g2):
        return device(zh * 8 + g2 // 4, (g2 % 4) * 4 + zl)

    def ring(q2):
        return device((q2 // 4) * 8 + yc, x * 4 + q2 % 4)

    def near(dy, dz):
        return device((py + 32 + dy) % 32, (pz + 16 + dz) % 16)

    loads = [
        pltpu.make_async_copy(src, dst, load_sem.at[i])
        for i, (src, dst) in enumerate(
            ((u_in, u), (span_in, span), (vx_in, vx), (vy_in, vy), (vz_in, vz), (b_in, b),
             (xb_in, xb), (yb_in, yb), (zb_in, zb), (xv_in, xv), (yv_in, yv), (zv_in, zv))
        )
    ]
    loads[0].start()
    loads[1].start()
    barrier = pltpu.get_barrier_semaphore()

    def greet(k, carry):
        pl.semaphore_signal(barrier, inc=1, device_id=group((g + k) % 32))
        return carry

    lax.fori_loop(1, 32, greet, 0)

    def greet_ring(k, carry):
        pl.semaphore_signal(barrier, inc=1, device_id=ring((q + k) % 16))
        return carry

    lax.fori_loop(1, 16, greet_ring, 0)
    sides = [(dy, dz) for dy in (-1, 0, 1) for dz in (-1, 0, 1) if dy or dz]
    for dy, dz in sides:
        pl.semaphore_signal(barrier, inc=1, device_id=near(dy, dz))
    above, below = ((zh + 1) % 4) * 8, ((zh + 3) % 4) * 8

    @pl.when(bottom)
    def _():
        for k in range(3):
            pl.semaphore_signal(barrier, inc=1, device_id=device(below + 2 * k + 1, pz))

    @pl.when(top)
    def _():
        for k in range(1, 4):
            pl.semaphore_signal(barrier, inc=1, device_id=device(above + 2 * k, pz))

    for load in loads[2:]:
        load.start()
    cs[...] = jnp.zeros_like(cs)
    for it in range(ITERS):
        hr[it, pl.ds(144, 112), :] = jnp.zeros((112, 512), F32)

    loads[0].wait()
    loads[1].wait()

    def weigh(i, carry):
        rows = pl.ds(pl.multiple_of(i * 8, 8), 8)
        at = span[rows, :]
        v = jnp.full((8, 512), coef[0], F32)
        for e in range(1, 8):
            v = jnp.where(at == e, coef[e], v)
        c[rows, :] = v
        w[0, rows, :] = v * u[rows, :]
        return carry

    lax.fori_loop(0, 16, weigh, 0)
    pl.semaphore_wait(barrier, 31 + 15 + 8 + jnp.where(top | bottom, 0, 1))

    sub = lax.broadcasted_iota(jnp.int32, (8, 128), 0)
    lane = lax.broadcasted_iota(jnp.int32, (8, 128), 1)

    def prepare():
        def coords(tile):
            if tile == 2:
                return lane // 16, lane % 16
            col = lane + tile * 128
            yy = jnp.where(col < 48, col // 16 - 3, 8 + (col - 48) // 16)
            zz = col % 16
            k = col - 96
            edge = col >= 96
            yy = jnp.where(edge, k % 8, yy)
            zz = jnp.where(edge, jnp.where(k < 24, k // 8 - 3, 16 + (k - 24) // 8), zz)
            k = col - 144
            corner = k >= 0
            cc = k % 16
            y3 = jnp.where(cc >= 6, 2, jnp.where(cc >= 3, 1, 0))
            z3 = cc - 3 * y3
            t = k // 16
            yy = jnp.where(corner, jnp.where(t < 2, y3 - 3, 8 + y3), yy)
            zz = jnp.where(corner, jnp.where(t % 2 == 0, z3 - 3, 16 + z3), zz)
            bad = (corner & (cc >= 9)) | (col >= 208)
            gy, gz = py * 8 + yy, pz * 16 + zz
            bad = bad | (gy < 0) | (gy > 255) | (gz < 0) | (gz > 255)
            return jnp.where(bad, 1000, yy), jnp.where(bad, 1000, zz)

        for i in (6, 7, 8):
            loads[i].wait()
        pick = lax.broadcasted_iota(jnp.int32, (8, 16), 1) - lax.broadcasted_iota(jnp.int32, (8, 16), 0)
        columns = {
            (kind, k, half): jnp.sum(
                jnp.where(pick == half * 8, zb[k, kind : kind + 1, :], 0.0), axis=1, keepdims=True
            )
            for kind in range(2) for k in range(7) for half in range(2)
        }
        for tile in range(3):
            yy, zz = coords(tile)
            ez = {}
            for half in range(2):
                dz = zz - (half * 8 + sub) + 3
                for kind in range(2):
                    total = jnp.zeros((8, 128), F32)
                    for k in range(7):
                        total = jnp.where(dz == k, columns[kind, k, half], total)
                    ez[kind, half] = total
            for y in range(8):
                dy = yy - y + 3
                ey = []
                for kind in range(2):
                    total = jnp.zeros((8, 128), F32)
                    for k in range(7):
                        total = jnp.where(dy == k, yb[k, kind : kind + 1, y : y + 1], total)
                    ey.append(total)
                mass = [ey[1] * ez[1, half] for half in range(2)]
                stiff = [ey[0] * ez[1, half] + ey[1] * ez[0, half] for half in range(2)]
                for base, pair in ((0, mass), (128, stiff)):
                    hi, lo = split(jnp.concatenate(pair, axis=0))
                    at = slice(base + y * 16, base + y * 16 + 16)
                    bm_h[at, tile * 128 : tile * 128 + 128] = hi
                    bm_l[at, tile * 128 : tile * 128 + 128] = lo
        for kind, (big, small) in enumerate(((kx_h, kx_l), (mx_h, mx_l))):
            for i in range(4):
                for j in range(4):
                    at = (slice(j * 128, j * 128 + 128), slice(i * 128, i * 128 + 128))
                    if abs(i - j) > 1:
                        big[at] = jnp.zeros((128, 128), BF16)
                        small[at] = jnp.zeros((128, 128), BF16)
                        continue
                    for part in range(0, 128, 16):
                        shape = (16, 128)
                        k_of = (j - i) * 128 + part + 3 + lax.broadcasted_iota(jnp.int32, shape, 0)
                        k_of = k_of - lax.broadcasted_iota(jnp.int32, shape, 1)
                        total = jnp.zeros(shape, F32)
                        for k in range(7):
                            total = jnp.where(k_of == k, xb[k, kind : kind + 1, at[1]], total)
                        hi, lo = split(total)
                        big[j * 128 + part : j * 128 + part + 16, at[1]] = hi
                        small[j * 128 + part : j * 128 + part + 16, at[1]] = lo
        loads[2].wait()
        for i in range(4):
            cols = slice(i * 128, i * 128 + 128)
            hi, lo = split(jnp.transpose(vx[:, cols]))
            vxt_h[cols, :] = hi
            vxt_l[cols, :] = lo
        loads[3].wait()
        vy_h[...], vy_l[...] = split(vy[...])
        vyt_h[...], vyt_l[...] = split(jnp.transpose(vy[...]))
        loads[4].wait()
        for p in range(2):
            for e in range(2):
                for xx in range(4):
                    to = p * 128 + e * 64 + xx * 16
                    at = xx * 64 + (2 * p + e) * 16
                    hi, lo = split(vz[at : at + 16, :])
                    vz_h[to : to + 16, :] = hi
                    vz_l[to : to + 16, :] = lo
        for i in (9, 10, 11):
            loads[i].wait()
        column = jnp.transpose(jnp.broadcast_to(yv[...], (128, 256)))
        j = jnp.where(first, mine * 16 + q, 256 + q * 16 + mine)
        row = lax.broadcasted_iota(jnp.int32, (1, 512), 1)
        shift = jnp.sum(jnp.where(row == j, xv[...], 0.0), axis=1, keepdims=True)
        for half in range(2):
            cols = slice(half * 128, half * 128 + 128)
            den[:, cols] = (column + zv[:, cols]) + shift
        loads[5].wait()

    quarter = [slice(k * 128, k * 128 + 128) for k in range(4)]

    def push(it, src, dst, stage, where, out=None):
        pltpu.make_async_remote_copy(
            src, dst, send_sem.at[it, stage if out is None else out], recv_sem.at[it, stage], device_id=where
        ).start()

    def rims(it):
        for i in range(3):
            for side, first in enumerate((0, 13)):
                for t in range(4):
                    cols = slice(t * 128, t * 128 + 128)
                    full = w[it, :, cols].reshape(8, 16, 128)
                    zs[it, side, i * 8 : i * 8 + 8, cols] = full[:, first + i, :]
        for cy in range(2):
            for cz in range(2):
                for i in range(3):
                    row = (cy * 5 + i) * 16 + cz * 13
                    three = w[it, row : row + 3, :]
                    for t in range(4):
                        at = t * 9 + i * 3
                        cs[it, cy * 2 + cz, at : at + 3, :] = three[:, t * 128 : t * 128 + 128]
        own = w.at[it]

        @pl.when(top)
        def _():
            for k in range(3):
                push(it, own.at[80:128, quarter[k]], rl.at[it], 5, device(zh * 8 + 2 * k + 1, pz))
            push(it, own.at[80:128, quarter[3]], hr.at[it, 0:48, quarter[3]], 0, near(1, 0), 5)

        @pl.when(bottom)
        def _():
            for k in range(1, 4):
                push(it, own.at[0:48, quarter[k]], rl.at[it], 5, device(zh * 8 + 2 * k, pz))
            push(it, own.at[0:48, quarter[0]], hr.at[it, 48:96, quarter[0]], 0, near(-1, 0), 5)

        push(it, cs.at[it, 3], hc.at[it, 0], 6, near(1, 1))
        push(it, cs.at[it, 2], hc.at[it, 1], 6, near(1, -1))
        push(it, cs.at[it, 1], hc.at[it, 2], 6, near(-1, 1))
        push(it, cs.at[it, 0], hc.at[it, 3], 6, near(-1, -1))

        @pl.when(jnp.logical_not(top))
        def _():
            push(it, own.at[80:128], hr.at[it, 0:48], 0, near(1, 0))

        @pl.when(jnp.logical_not(bottom))
        def _():
            push(it, own.at[0:48], hr.at[it, 48:96], 0, near(-1, 0))

        push(it, zs.at[it, 1], hr.at[it, 96:120], 0, near(0, 1))
        push(it, zs.at[it, 0], hr.at[it, 120:144], 0, near(0, -1))

    def relay(it):
        @pl.when(jnp.logical_not(top | bottom))
        def _():
            pltpu.make_async_remote_copy(
                rl.at[it], rl.at[it], send_sem.at[it, 5], recv_sem.at[it, 5], device_id=near(1, 0)
            ).wait_recv()
            odd = yc % 2 == 1
            start = pl.multiple_of(jnp.where(odd, 0, 48), 8)
            cols = pl.ds(pl.multiple_of((yc // 2) * 128, 128), 128)
            push(it, rl.at[it], hr.at[it, pl.ds(start, 48), cols], 0,
                 device(jnp.where(odd, above, below + 7), pz), 7)

    rims(0)
    relay(0)
    prepare()

    def step(it, carry):
        wide = split(w[it])
        acc[...] = dot3((bm_h[:, 256:384], bm_l[:, 256:384]), wide)
        pltpu.make_async_remote_copy(
            hr.at[it, 0:144], hr.at[it, 0:144], send_sem.at[it, 0], recv_sem.at[it, 0],
            device_id=near(1, 0),
        ).wait_recv()
        pltpu.make_async_remote_copy(
            hc.at[it], hc.at[it], send_sem.at[it, 6], recv_sem.at[it, 6], device_id=near(1, 0)
        ).wait_recv()
        for corner in range(4):
            for t in range(4):
                at = 144 + corner * 16
                hr[it, at : at + 9, quarter[t]] = hc[it, corner, t * 9 : t * 9 + 9, :]
        wide = split(hr[it])
        acc[...] += dot3((bm_h[:, 0:256], bm_l[:, 0:256]), wide)

        total = dot3(split(acc[0:128, :]), (kx_h[...], kx_l[...]))
        total = total + dot3(split(acc[128:256, :]), (mx_h[...], mx_l[...]))
        r[...] = b[...] - c[...] * total

        @pl.when(it == ITERS - 1)
        def _():
            pltpu.make_async_copy(r, r_out, load_sem.at[12]).start()

        turned = [r[((8 - i) % 8) * 16 : ((8 - i) % 8) * 16 + 16, :] for i in range(8)]
        wide = split(jnp.concatenate(turned, axis=0))
        def block(i):
            return pl.ds(pl.multiple_of(i * 16, 16), 16)

        def modes(i):
            rows = slice(i * 128, i * 128 + 128)
            s[it, rows, :] = dot3((vxt_h[rows, :], vxt_l[rows, :]), wide, ((1,), (1,)))

        def wait_rows(part, stage):
            pltpu.make_async_remote_copy(
                part, part, send_sem.at[it, 0], recv_sem.at[it, stage], device_id=near(1, 0)
            ).wait_recv()

        modes(2)
        modes(3)
        for k in RING:
            q2 = (q + k) % 16
            push(it, s.at[it, block(16 + q2)], rc.at[it, block(q)], 2, ring(q2))
        rc[it, block(q), :] = s[it, block(16 + q), :]
        modes(0)
        modes(1)

        def send_some(src, dst, stage, where, count, own, source=lambda i: i):
            def one(k, carry):
                i = (mine + k) % count if count == 16 else (g + k) % 32

                @pl.when(i != own)
                def _():
                    push(it, src.at[it, block(source(i))], dst, stage, where(i))

                return carry

            lax.fori_loop(0, count, one, 0)

        def first_core(i):
            return device(zh * 8 + (i // 4) * 2, (i % 4) * 4 + zl)

        def second_core(i):
            return device(zh * 8 + (i // 4) * 2 + 1, (i % 4) * 4 + zl)

        none = 99
        send_some(s, ra.at[it, block(g)], 1, first_core, 16, jnp.where(first, mine, none))

        @pl.when(first)
        def _():
            ra[it, block(g), :] = s[it, block(mine), :]
            wait_rows(ra.at[it, 0 : 31 * 16], 1)
            for k in range(16):
                sb[it, k] = ra[it, pl.ds(k, 32, stride=16), :]
            for k in RING:
                q2 = (q + k) % 16
                push(it, sb.at[it, q2], rb.at[it, q], 3, ring(q2))
            rb[it, q] = sb[it, q]

        wait_rows(rc.at[it, 0 : 15 * 16], 2)
        for k in range(16):
            se[it, k * 16 : k * 16 + 16, :] = rc[it, pl.ds(k, 16, stride=16), :]
        send_some(se, rd.at[it, block(g)], 4, second_core, 16, jnp.where(second, mine, none))

        @pl.when(first)
        def _():
            wait_rows(rb.at[it, 0:15], 3)

        @pl.when(second)
        def _():
            rd[it, block(g), :] = se[it, block(mine), :]
            wait_rows(rd.at[it, 0 : 31 * 16], 4)
            for k in range(16):
                rb[it, k] = rd[it, pl.ds(k, 32, stride=16), :]

        for h in range(4):
            for t in range(4):
                rows = slice(t * 8, t * 8 + 8)
                one, two = ((h * 8 + yy) * 8 for yy in PLACES[t])
                for p in range(2):
                    a = swap_blocks(rb[it, h * 4 + 2 * p, rows, :], lane)
                    e = swap_blocks(rb[it, h * 4 + 2 * p + 1, rows, :], lane)
                    m[one : one + 8, quarter[p]] = jnp.where(lane < 64, a, pltpu.roll(e, 64, 1))
                    m[two : two + 8, quarter[p]] = jnp.where(lane < 64, pltpu.roll(a, 64, 1), e)
        vzs = (vz_h[...], vz_l[...])
        m[...] = dot3(split(m[...]), vzs)
        m[...] = dot3((vyt_h[...], vyt_l[...]), split(m[...])) / den[...]
        m[...] = dot3((vy_h[...], vy_l[...]), split(m[...]))
        m[...] = dot3(split(m[...]), vzs, ((1,), (1,)))

        for t in range(4):
            rows = slice(t * 8, t * 8 + 8)
            for h in range(4):
                one, two = ((h * 8 + yy) * 8 for yy in PLACES[t])
                for p in range(2):
                    low, high = m[one : one + 8, quarter[p]], m[two : two + 8, quarter[p]]
                    a = jnp.where(lane < 64, low, pltpu.roll(high, 64, 1))
                    e = jnp.where(lane < 64, pltpu.roll(low, 64, 1), high)
                    mb[it, h * 4 + 2 * p, rows, :] = swap_blocks(a, lane)
                    mb[it, h * 4 + 2 * p + 1, rows, :] = swap_blocks(e, lane)

        def turn(i):
            return (i // 8) * 8 + (8 - i % 8) % 8

        def by_group(src, dst):
            for k in range(16):
                for h in range(4):
                    dst[it, pl.ds(h * 128 + k, 8, stride=16), :] = src[it, k, h * 8 : h * 8 + 8, :]

        @pl.when(first)
        def _():
            for k in RING:
                q2 = (q + k) % 16
                push(it, mb.at[it, q2], rb2.at[it, q], 8, ring(q2))
            rb2[it, q] = mb[it, q]

        @pl.when(second)
        def _():
            by_group(mb, sa2)
            send_some(sa2, rm.at[it, block(mine)], 10, group, 32, g, turn)
            rm[it, block(mine), :] = sa2[it, block(turn(g)), :]
            wait_rows(rm.at[it, 0 : 15 * 16], 10)

        @pl.when(first)
        def _():
            wait_rows(rm.at[it, 0 : 16 * 16], 10)

        for k in range(16):
            sn[it, k * 16 : k * 16 + 16, :] = rm[it, pl.ds(k, 16, stride=16), :]
        for k in RING:
            q2 = (q + k) % 16
            push(it, sn.at[it, block(q2)], ra2.at[it, block(16 + q)], 11, ring(q2))
        ra2[it, block(16 + q), :] = sn[it, block(q), :]

        @pl.when(first)
        def _():
            wait_rows(rb2.at[it, 0:15], 8)
            by_group(rb2, sa2)
            send_some(sa2, ra2.at[it, block(mine)], 9, group, 32, g, turn)
            ra2[it, block(mine), :] = sa2[it, block(turn(g)), :]
            wait_rows(ra2.at[it, 0 : 15 * 16], 9)

        @pl.when(second)
        def _():
            wait_rows(ra2.at[it, 0 : 16 * 16], 9)

        wait_rows(ra2.at[it, 0 : 15 * 16], 11)
        wide = split(jnp.transpose(ra2[it]))
        u[...] += dot3(wide, (vxt_h[...], vxt_l[...]))

        @pl.when(it + 1 < ITERS)
        def _():
            w[it + 1] = c[...] * u[...]
            rims(it + 1)
            relay(it + 1)

        return carry

    lax.fori_loop(0, ITERS, step, 0)
    last = pltpu.make_async_copy(u, u_out, load_sem.at[13])
    last.start()
    for it in range(ITERS):
        @pl.when(jnp.logical_not(top | bottom))
        def _(it=it):
            pltpu.make_async_remote_copy(
                hr.at[it, 0:144], hr.at[it, 0:144], send_sem.at[it, 0], recv_sem.at[it, 0], device_id=near(1, 0)
            ).wait_send()
            pltpu.make_async_remote_copy(
                rl.at[it], rl.at[it], send_sem.at[it, 7], recv_sem.at[it, 0], device_id=near(1, 0)
            ).wait_send()

        @pl.when(top | bottom)
        def _(it=it):
            for stage, part in ((0, hr.at[it, 0:96]), (5, hr.at[it, 0:48])):
                pltpu.make_async_remote_copy(
                    part, part, send_sem.at[it, stage], recv_sem.at[it, stage], device_id=near(1, 0)
                ).wait_send()

        def sent(stage, part, it=it):
            pltpu.make_async_remote_copy(
                part, part, send_sem.at[it, stage], recv_sem.at[it, stage], device_id=near(1, 0)
            ).wait_send()

        sent(6, hc.at[it])
        sent(2, ra.at[it, 0 : 15 * 16])
        sent(11, ra.at[it, 0 : 15 * 16])

        @pl.when(first)
        def _(it=it, sent=sent):
            sent(1, ra.at[it, 0 : 15 * 16])
            sent(3, sb.at[it, 0:15])
            sent(4, ra.at[it, 0 : 16 * 16])
            sent(8, sb.at[it, 0:15])
            sent(9, ra.at[it, 0 : 31 * 16])

        @pl.when(second)
        def _(it=it, sent=sent):
            sent(1, ra.at[it, 0 : 16 * 16])
            sent(4, ra.at[it, 0 : 15 * 16])
            sent(10, ra.at[it, 0 : 31 * 16])

    last.wait()
    pltpu.make_async_copy(r, r_out, load_sem.at[12]).wait()


def finish(u_in, r_in, u_out, r_out):
    u_out[...] = u_in[...]
    r_out[...] = r_in[...]


def shards(solution, right_side, span_index, coef_table, xaxis_bands, yaxis_bands, zaxis_bands,
           xaxis_vectors, yaxis_vectors, zaxis_vectors, xaxis_values, yaxis_values, zaxis_values):
    flat = (128, 512)
    hbm = pl.BlockSpec(memory_space=pl.ANY)
    vmem = pl.BlockSpec(memory_space=pltpu.VMEM)
    smem = pl.BlockSpec(memory_space=pltpu.SMEM)
    V = pltpu.VMEM
    big = V((ITERS, 512, 128), F32)
    half = V((ITERS, 256, 128), F32)
    ring = V((ITERS, 16, 32, 128), F32)
    scratch = [
        V(flat, F32), V(flat, F32), V(flat, jnp.int32), V((512, 512), F32), V((256, 256), F32), V((256, 256), F32),
        V((7, 2, 512), F32), V((7, 2, 8), F32), V((7, 2, 16), F32), V((1, 512), F32), V((1, 256), F32), V((1, 256), F32),
        V(flat, F32), V(flat, F32), V((ITERS, 2, 24, 512), F32), V((ITERS, 4, 40, 128), F32),
        V((ITERS, 4, 40, 128), F32), V((ITERS, 48, 128), F32),
        V((ITERS, 256, 512), F32), V((ITERS, 128, 512), F32), V((256, 512), F32),
        big, big, ring, ring, half, half, big, V((256, 256), F32), ring, ring, big, half, half, big,
        V((256, 384), BF16), V((256, 384), BF16), V((512, 512), BF16), V((512, 512), BF16),
        V((256, 256), BF16), V((256, 256), BF16), V((256, 256), BF16), V((256, 256), BF16),
        V((256, 256), BF16), V((256, 256), BF16), V((256, 256), F32),
        V((512, 512), BF16), V((512, 512), BF16), V((512, 512), BF16), V((512, 512), BF16),
        pltpu.SemaphoreType.DMA((14,)), pltpu.SemaphoreType.DMA((ITERS, 12)), pltpu.SemaphoreType.DMA((ITERS, 12)),
    ]
    updated, residual = pl.pallas_call(
        kernel,
        out_shape=(jax.ShapeDtypeStruct(flat, F32), jax.ShapeDtypeStruct(flat, F32)),
        in_specs=[hbm, hbm, hbm, smem] + [hbm] * 9,
        out_specs=(hbm, hbm),
        scratch_shapes=scratch,
        compiler_params=pltpu.CompilerParams(collective_id=0, has_side_effects=True),
        name="richardson",
    )(
        solution.reshape(flat), right_side.reshape(flat), span_index.reshape(flat), coef_table,
        jnp.swapaxes(xaxis_bands, 0, 1), jnp.swapaxes(yaxis_bands, 0, 1), jnp.swapaxes(zaxis_bands, 0, 1),
        xaxis_vectors, yaxis_vectors, zaxis_vectors,
        xaxis_values.reshape(1, 512), yaxis_values.reshape(1, 256), zaxis_values.reshape(1, 256),
    )
    updated, residual = pl.pallas_call(
        finish,
        out_shape=(jax.ShapeDtypeStruct(flat, F32), jax.ShapeDtypeStruct(flat, F32)),
        in_specs=[vmem, vmem],
        out_specs=(vmem, vmem),
        name="finish",
    )(updated, residual)
    return updated.reshape(solution.shape), residual.reshape(solution.shape)


def solution(mesh):
    grid = P("py", "pz", None)
    return jax.shard_map(
        shards,
        mesh=mesh,
        in_specs=(grid, grid, grid, P(), P(), P(None, None, "py"), P(None, None, "pz"), P(), P(), P(), P(), P(), P()),
        out_specs=(grid, grid),
        check_vma=False,
    )
```

```python
import jax
import jax.numpy as jnp
from jax import lax
from jax.experimental import pallas as pl
from jax.experimental.pallas import tpu as pltpu
from jax.sharding import PartitionSpec as P

ITERS = 2
F32 = jnp.float32
BF16 = jnp.bfloat16
PLACES = ((0, 1), (2, 3), (4, 5), (6, 7))
RING = (8, 7, 9, 6, 10, 5, 11, 4, 12, 3, 13, 2, 14, 1, 15)


def split(v):
    hi = v.astype(BF16)
    return hi, (v - hi.astype(F32)).astype(BF16)


def dot3(a, b, dims=((1,), (0,))):
    def one(p, q):
        return lax.dot_general(p, q, (dims, ((), ())), preferred_element_type=F32)

    return one(a[0], b[0]) + one(a[0], b[1]) + one(a[1], b[0])


def swap_blocks(v, lane):
    v = pltpu.roll(v, 0, 1, stride=16, stride_axis=0)
    for bit in (1, 2, 4):
        v = jnp.where((lane // (16 * bit)) % 2 == 1, pltpu.roll(v, 8 - bit, 0), v)
    return pltpu.roll(v, 0, 1, stride=16, stride_axis=0)


def kernel(
    u_in, b_in, span_in, coef_in, xb_in, yb_in, zb_in, vx_in, vy_in, vz_in, xv_in, yv_in, zv_in,
    u_out, r_out,
    u, b, span, vx, vy, vz, xb, yb, zb, xv, yv, zv, coef, c, r, zs, cs, hc, rl, hr, w, acc,
    s, ra, sb, rb, rc, se, rd, m, mz, mg, rz, rg, sg, ry, sz, rx, ra2,
    bm_h, bm_l, vxt_h, vxt_l, vy_h, vy_l, vyt_h, vyt_l, vz_h, vz_l, den,
    kx_h, kx_l, mx_h, mx_l, load_sem, send_sem, recv_sem,
):
    py, pz = lax.axis_index("py"), lax.axis_index("pz")
    zh, yc = py // 8, py % 8
    x, zl = pz // 4, pz % 4
    top, bottom = yc == 7, yc == 0
    edge = top | bottom
    core = yc % 2
    first, second = core == 0, core == 1
    g = yc * 4 + x
    mine = (yc // 2) * 4 + x
    q = zh * 4 + zl

    def device(py2, pz2):
        return {"py": py2, "pz": pz2}

    def group(g2):
        return device(zh * 8 + g2 // 4, (g2 % 4) * 4 + zl)

    def ring(q2):
        return device((q2 // 4) * 8 + yc, x * 4 + q2 % 4)

    def near(dy, dz):
        return device((py + 32 + dy) % 32, (pz + 16 + dz) % 16)

    loads = [
        pltpu.make_async_copy(src, dst, load_sem.at[i])
        for i, (src, dst) in enumerate(
            ((u_in, u), (span_in, span), (vx_in, vx), (vy_in, vy), (vz_in, vz), (b_in, b),
             (xb_in, xb), (yb_in, yb), (zb_in, zb), (xv_in, xv), (yv_in, yv), (zv_in, zv), (coef_in, coef))
        )
    ]
    for i in (0, 1, 12):
        loads[i].start()
    barrier = pltpu.get_barrier_semaphore()

    def greet(k, carry):
        pl.semaphore_signal(barrier, inc=1, device_id=group((g + k) % 32))
        return carry

    lax.fori_loop(1, 32, greet, 0)

    def greet_ring(k, carry):
        pl.semaphore_signal(barrier, inc=1, device_id=ring((q + k) % 16))
        return carry

    lax.fori_loop(1, 16, greet_ring, 0)
    sides = [(dy, dz) for dy in (-1, 0, 1) for dz in (-1, 0, 1) if dy or dz]
    for dy, dz in sides:
        pl.semaphore_signal(barrier, inc=1, device_id=near(dy, dz))
    above, below = ((zh + 1) % 4) * 8, ((zh + 3) % 4) * 8

    @pl.when(bottom)
    def _():
        for k in range(3):
            pl.semaphore_signal(barrier, inc=1, device_id=device(below + 2 * k + 1, pz))

    @pl.when(top)
    def _():
        for k in range(1, 4):
            pl.semaphore_signal(barrier, inc=1, device_id=device(above + 2 * k, pz))

    for load in loads[2:12]:
        load.start()
    cs[...] = jnp.zeros_like(cs)
    for it in range(ITERS):
        hr[it, pl.ds(144, 112), :] = jnp.zeros((112, 512), F32)

    loads[0].wait()
    loads[1].wait()
    loads[12].wait()
    table = [coef[:, e : e + 1] for e in range(8)]

    def weigh(i, carry):
        rows = pl.ds(pl.multiple_of(i * 8, 8), 8)
        at = span[rows, :]
        v = jnp.broadcast_to(table[0], (8, 512))
        for e in range(1, 8):
            v = jnp.where(at == e, table[e], v)
        c[rows, :] = v
        w[0, rows, :] = v * u[rows, :]
        return carry

    lax.fori_loop(0, 16, weigh, 0)
    pl.semaphore_wait(barrier, 31 + 15 + 8 + jnp.where(top | bottom, 0, 1))

    sub = lax.broadcasted_iota(jnp.int32, (8, 128), 0)
    lane = lax.broadcasted_iota(jnp.int32, (8, 128), 1)

    def prepare():
        def coords(tile):
            if tile == 2:
                return lane // 16, lane % 16
            col = lane + tile * 128
            yy = jnp.where(col < 48, col // 16 - 3, 8 + (col - 48) // 16)
            zz = col % 16
            k = col - 96
            edge = col >= 96
            yy = jnp.where(edge, k % 8, yy)
            zz = jnp.where(edge, jnp.where(k < 24, k // 8 - 3, 16 + (k - 24) // 8), zz)
            k = col - 144
            corner = k >= 0
            cc = k % 16
            y3 = jnp.where(cc >= 6, 2, jnp.where(cc >= 3, 1, 0))
            z3 = cc - 3 * y3
            t = k // 16
            yy = jnp.where(corner, jnp.where(t < 2, y3 - 3, 8 + y3), yy)
            zz = jnp.where(corner, jnp.where(t % 2 == 0, z3 - 3, 16 + z3), zz)
            bad = (corner & (cc >= 9)) | (col >= 208)
            gy, gz = py * 8 + yy, pz * 16 + zz
            bad = bad | (gy < 0) | (gy > 255) | (gz < 0) | (gz > 255)
            return jnp.where(bad, 1000, yy), jnp.where(bad, 1000, zz)

        for i in (6, 7, 8):
            loads[i].wait()
        pick = lax.broadcasted_iota(jnp.int32, (8, 16), 1) - lax.broadcasted_iota(jnp.int32, (8, 16), 0)
        columns = {
            (kind, k, half): jnp.sum(
                jnp.where(pick == half * 8, zb[k, kind : kind + 1, :], 0.0), axis=1, keepdims=True
            )
            for kind in range(2) for k in range(7) for half in range(2)
        }
        for tile in range(3):
            yy, zz = coords(tile)
            ez = {}
            for half in range(2):
                dz = zz - (half * 8 + sub) + 3
                for kind in range(2):
                    total = jnp.zeros((8, 128), F32)
                    for k in range(7):
                        total = jnp.where(dz == k, columns[kind, k, half], total)
                    ez[kind, half] = total
            for y in range(8):
                dy = yy - y + 3
                ey = []
                for kind in range(2):
                    total = jnp.zeros((8, 128), F32)
                    for k in range(7):
                        total = jnp.where(dy == k, yb[k, kind : kind + 1, y : y + 1], total)
                    ey.append(total)
                mass = [ey[1] * ez[1, half] for half in range(2)]
                stiff = [ey[0] * ez[1, half] + ey[1] * ez[0, half] for half in range(2)]
                for base, pair in ((0, mass), (128, stiff)):
                    hi, lo = split(jnp.concatenate(pair, axis=0))
                    at = slice(base + y * 16, base + y * 16 + 16)
                    bm_h[at, tile * 128 : tile * 128 + 128] = hi
                    bm_l[at, tile * 128 : tile * 128 + 128] = lo
        for kind, (big, small) in enumerate(((kx_h, kx_l), (mx_h, mx_l))):
            for i in range(4):
                for j in range(4):
                    at = (slice(j * 128, j * 128 + 128), slice(i * 128, i * 128 + 128))
                    if abs(i - j) > 1:
                        big[at] = jnp.zeros((128, 128), BF16)
                        small[at] = jnp.zeros((128, 128), BF16)
                        continue
                    for part in range(0, 128, 16):
                        shape = (16, 128)
                        k_of = (j - i) * 128 + part + 3 + lax.broadcasted_iota(jnp.int32, shape, 0)
                        k_of = k_of - lax.broadcasted_iota(jnp.int32, shape, 1)
                        total = jnp.zeros(shape, F32)
                        for k in range(7):
                            total = jnp.where(k_of == k, xb[k, kind : kind + 1, at[1]], total)
                        hi, lo = split(total)
                        big[j * 128 + part : j * 128 + part + 16, at[1]] = hi
                        small[j * 128 + part : j * 128 + part + 16, at[1]] = lo
        loads[2].wait()
        for i in range(4):
            cols = slice(i * 128, i * 128 + 128)
            hi, lo = split(jnp.transpose(vx[:, cols]))
            vxt_h[cols, :] = hi
            vxt_l[cols, :] = lo
        loads[3].wait()
        vy_h[...], vy_l[...] = split(vy[...])
        vyt_h[...], vyt_l[...] = split(jnp.transpose(vy[...]))
        loads[4].wait()
        for p in range(2):
            for e in range(2):
                for xx in range(4):
                    to = p * 128 + e * 64 + xx * 16
                    at = xx * 64 + (2 * p + e) * 16
                    hi, lo = split(vz[at : at + 16, :])
                    vz_h[to : to + 16, :] = hi
                    vz_l[to : to + 16, :] = lo
        for i in (9, 10, 11):
            loads[i].wait()
        column = jnp.transpose(jnp.broadcast_to(yv[...], (128, 256)))
        j = jnp.where(first, mine * 16 + q, 256 + q * 16 + mine)
        row = lax.broadcasted_iota(jnp.int32, (1, 512), 1)
        shift = jnp.sum(jnp.where(row == j, xv[...], 0.0), axis=1, keepdims=True)
        for half in range(2):
            cols = slice(half * 128, half * 128 + 128)
            den[:, cols] = (column + zv[:, cols]) + shift
        loads[5].wait()

    quarter = [slice(k * 128, k * 128 + 128) for k in range(4)]

    def push(it, src, dst, stage, where, out=None):
        pltpu.make_async_remote_copy(
            src, dst, send_sem.at[it, stage if out is None else out], recv_sem.at[it, stage], device_id=where
        ).start()

    def rims(it):
        for i in range(3):
            for side, first in enumerate((0, 13)):
                for t in range(4):
                    cols = slice(t * 128, t * 128 + 128)
                    full = w[it, :, cols].reshape(8, 16, 128)
                    zs[it, side, i * 8 : i * 8 + 8, cols] = full[:, first + i, :]
        for cy in range(2):
            for cz in range(2):
                for i in range(3):
                    row = (cy * 5 + i) * 16 + cz * 13
                    three = w[it, row : row + 3, :]
                    for t in range(4):
                        at = t * 9 + i * 3
                        cs[it, cy * 2 + cz, at : at + 3, :] = three[:, t * 128 : t * 128 + 128]
        own = w.at[it]

        @pl.when(top)
        def _():
            for k in range(3):
                push(it, own.at[80:128, quarter[k]], rl.at[it], 5, device(zh * 8 + 2 * k + 1, pz))
            push(it, own.at[80:128, quarter[3]], hr.at[it, 0:48, quarter[3]], 0, near(1, 0), 5)

        @pl.when(bottom)
        def _():
            for k in range(1, 4):
                push(it, own.at[0:48, quarter[k]], rl.at[it], 5, device(zh * 8 + 2 * k, pz))
            push(it, own.at[0:48, quarter[0]], hr.at[it, 48:96, quarter[0]], 0, near(-1, 0), 5)

        push(it, cs.at[it, 3], hc.at[it, 0], 6, near(1, 1))
        push(it, cs.at[it, 2], hc.at[it, 1], 6, near(1, -1))
        push(it, cs.at[it, 1], hc.at[it, 2], 6, near(-1, 1))
        push(it, cs.at[it, 0], hc.at[it, 3], 6, near(-1, -1))

        @pl.when(jnp.logical_not(top))
        def _():
            push(it, own.at[80:128], hr.at[it, 0:48], 0, near(1, 0))

        @pl.when(jnp.logical_not(bottom))
        def _():
            push(it, own.at[0:48], hr.at[it, 48:96], 0, near(-1, 0))

        push(it, zs.at[it, 1], hr.at[it, 96:120], 0, near(0, 1))
        push(it, zs.at[it, 0], hr.at[it, 120:144], 0, near(0, -1))

    def relay(it):
        @pl.when(jnp.logical_not(top | bottom))
        def _():
            pltpu.make_async_remote_copy(
                rl.at[it], rl.at[it], send_sem.at[it, 5], recv_sem.at[it, 5], device_id=near(1, 0)
            ).wait_recv()
            odd = yc % 2 == 1
            start = pl.multiple_of(jnp.where(odd, 0, 48), 8)
            cols = pl.ds(pl.multiple_of((yc // 2) * 128, 128), 128)
            push(it, rl.at[it], hr.at[it, pl.ds(start, 48), cols], 0,
                 device(jnp.where(odd, above, below + 7), pz), 7)

    rims(0)
    relay(0)
    prepare()

    def step(it, carry):
        wide = split(w[it])
        acc[...] = dot3((bm_h[:, 256:384], bm_l[:, 256:384]), wide)
        pltpu.make_async_remote_copy(
            hr.at[it, 0:144], hr.at[it, 0:144], send_sem.at[it, 0], recv_sem.at[it, 0],
            device_id=near(1, 0),
        ).wait_recv()
        pltpu.make_async_remote_copy(
            hc.at[it], hc.at[it], send_sem.at[it, 6], recv_sem.at[it, 6], device_id=near(1, 0)
        ).wait_recv()
        for corner in range(4):
            for t in range(4):
                at = 144 + corner * 16
                hr[it, at : at + 9, quarter[t]] = hc[it, corner, t * 9 : t * 9 + 9, :]
        wide = split(hr[it])
        acc[...] += dot3((bm_h[:, 0:256], bm_l[:, 0:256]), wide)

        total = dot3(split(acc[0:128, :]), (kx_h[...], kx_l[...]))
        total = total + dot3(split(acc[128:256, :]), (mx_h[...], mx_l[...]))
        r[...] = b[...] - c[...] * total

        @pl.when(it == ITERS - 1)
        def _():
            pltpu.make_async_copy(r, r_out, load_sem.at[13]).start()

        turned = [r[((8 - i) % 8) * 16 : ((8 - i) % 8) * 16 + 16, :] for i in range(8)]
        wide = split(jnp.concatenate(turned, axis=0))
        def block(i):
            return pl.ds(pl.multiple_of(i * 16, 16), 16)

        def modes(i):
            rows = slice(i * 128, i * 128 + 128)
            s[it, rows, :] = dot3((vxt_h[rows, :], vxt_l[rows, :]), wide, ((1,), (1,)))

        def wait_rows(part, stage):
            pltpu.make_async_remote_copy(
                part, part, send_sem.at[it, 0], recv_sem.at[it, stage], device_id=near(1, 0)
            ).wait_recv()

        modes(2)
        modes(3)
        for k in RING:
            q2 = (q + k) % 16
            push(it, s.at[it, block(16 + q2)], rc.at[it, block(q)], 2, ring(q2))
        rc[it, block(q), :] = s[it, block(16 + q), :]
        modes(0)
        modes(1)

        def send_some(src, dst, stage, where, own, source=lambda i: i):
            def one(k, carry):
                i = (mine + k) % 16

                @pl.when(i != own)
                def _():
                    push(it, src.at[it, block(source(i))], dst, stage, where(i))

                return carry

            lax.fori_loop(0, 16, one, 0)

        def first_core(i):
            return device(zh * 8 + (i // 4) * 2, (i % 4) * 4 + zl)

        def second_core(i):
            return device(zh * 8 + (i // 4) * 2 + 1, (i % 4) * 4 + zl)

        none = 99
        send_some(s, ra.at[it, block(g)], 1, first_core, jnp.where(first, mine, none))

        @pl.when(first)
        def _():
            ra[it, block(g), :] = s[it, block(mine), :]
            wait_rows(ra.at[it, 0 : 31 * 16], 1)
            for k in range(16):
                sb[it, k] = ra[it, pl.ds(k, 32, stride=16), :]
            for k in RING:
                q2 = (q + k) % 16
                push(it, sb.at[it, q2], rb.at[it, q], 3, ring(q2))
            rb[it, q] = sb[it, q]

        wait_rows(rc.at[it, 0 : 15 * 16], 2)
        for k in range(16):
            se[it, k * 16 : k * 16 + 16, :] = rc[it, pl.ds(k, 16, stride=16), :]
        send_some(se, rd.at[it, block(g)], 4, second_core, jnp.where(second, mine, none))

        @pl.when(first)
        def _():
            wait_rows(rb.at[it, 0:15], 3)

        @pl.when(second)
        def _():
            rd[it, block(g), :] = se[it, block(mine), :]
            wait_rows(rd.at[it, 0 : 31 * 16], 4)
            for k in range(16):
                rb[it, k] = rd[it, pl.ds(k, 32, stride=16), :]

        for h in range(4):
            for t in range(4):
                rows = slice(t * 8, t * 8 + 8)
                one, two = ((h * 8 + yy) * 8 for yy in PLACES[t])
                for p in range(2):
                    a = swap_blocks(rb[it, h * 4 + 2 * p, rows, :], lane)
                    e = swap_blocks(rb[it, h * 4 + 2 * p + 1, rows, :], lane)
                    m[one : one + 8, quarter[p]] = jnp.where(lane < 64, a, pltpu.roll(e, 64, 1))
                    m[two : two + 8, quarter[p]] = jnp.where(lane < 64, pltpu.roll(a, 64, 1), e)
        vzs = (vz_h[...], vz_l[...])
        m[...] = dot3(split(m[...]), vzs)
        m[...] = dot3((vyt_h[...], vyt_l[...]), split(m[...])) / den[...]
        m[...] = dot3((vy_h[...], vy_l[...]), split(m[...]))
        m[...] = dot3(split(m[...]), vzs, ((1,), (1,)))

        for t in range(4):
            for h in range(4):
                one, two = ((h * 8 + yy) * 8 for yy in PLACES[t])
                for p in range(2):
                    low, high = m[one : one + 8, quarter[p]], m[two : two + 8, quarter[p]]
                    pair = (
                        jnp.where(lane < 64, low, pltpu.roll(high, 64, 1)),
                        jnp.where(lane < 64, pltpu.roll(low, 64, 1), high),
                    )
                    for e, v in enumerate(pair):
                        v = pltpu.roll(swap_blocks(v, lane), 3, 0)
                        k = h * 4 + 2 * p + e
                        mz[it, k * 16 + t * 4 : k * 16 + t * 4 + 4, :] = v[0:4]
                        mg[it, pl.ds(t * 64 + k, 4, stride=16), :] = v[4:8]
        for k in RING:
            q2 = (q + k) % 16
            push(it, mz.at[it, block(q2)], rz.at[it, block(q)], 8, ring(q2))
        rz[it, block(q), :] = mz[it, block(q), :]

        def turn(i):
            return (i // 4) * 4 + 3 - i % 4

        slot = core * 16 + mine
        send_some(mg, rg.at[it, block(slot)], 10, second_core, jnp.where(second, mine, none), turn)

        @pl.when(second)
        def _():
            rg[it, block(slot), :] = mg[it, block(turn(mine)), :]
            wait_rows(rg.at[it, 0 : 31 * 16], 10)
            for k in range(16):
                sg[it, k] = rg[it, pl.ds(k, 32, stride=16), :]
            for k in RING:
                q2 = (q + k) % 16
                push(it, sg.at[it, q2], ry.at[it, q], 11, ring(q2))
            ry[it, q] = sg[it, q]

        wait_rows(rz.at[it, 0 : 15 * 16], 8)
        for k in range(16):
            sz[it, k * 16 : k * 16 + 16, :] = rz[it, pl.ds(k, 16, stride=16), :]
        send_some(sz, rx.at[it, block(slot)], 9, first_core, jnp.where(first, mine, none), turn)

        @pl.when(first)
        def _():
            rx[it, block(slot), :] = sz[it, block(turn(mine)), :]
            wait_rows(rx.at[it, 0 : 31 * 16], 9)
            ra2[0:256, :] = rx[it, 0:256, :]
            for k in range(16):
                ra2[256 + k * 16 : 272 + k * 16, :] = rx[it, pl.ds(256 + k, 16, stride=16), :]

        @pl.when(second)
        def _():
            wait_rows(ry.at[it, 0:15], 11)
            for k in range(16):
                ra2[256 + k * 16 : 272 + k * 16, :] = ry[it, k, 16:32, :]
                ra2[pl.ds(k, 16, stride=16), :] = ry[it, k, 0:16, :]

        wide = split(jnp.transpose(ra2[...]))
        u[...] += dot3(wide, (vxt_h[...], vxt_l[...]))

        @pl.when(it + 1 < ITERS)
        def _():
            w[it + 1] = c[...] * u[...]
            rims(it + 1)
            relay(it + 1)

        return carry

    lax.fori_loop(0, ITERS, step, 0)
    last = pltpu.make_async_copy(u, u_out, load_sem.at[14])
    last.start()
    for it in range(ITERS):
        @pl.when(jnp.logical_not(top | bottom))
        def _(it=it):
            pltpu.make_async_remote_copy(
                hr.at[it, 0:144], hr.at[it, 0:144], send_sem.at[it, 0], recv_sem.at[it, 0], device_id=near(1, 0)
            ).wait_send()
            pltpu.make_async_remote_copy(
                rl.at[it], rl.at[it], send_sem.at[it, 7], recv_sem.at[it, 0], device_id=near(1, 0)
            ).wait_send()

        @pl.when(top | bottom)
        def _(it=it):
            for stage, part in ((0, hr.at[it, 0:96]), (5, hr.at[it, 0:48])):
                pltpu.make_async_remote_copy(
                    part, part, send_sem.at[it, stage], recv_sem.at[it, stage], device_id=near(1, 0)
                ).wait_send()

        def sent(stage, part, it=it):
            pltpu.make_async_remote_copy(
                part, part, send_sem.at[it, stage], recv_sem.at[it, stage], device_id=near(1, 0)
            ).wait_send()

        sent(6, hc.at[it])
        sent(2, ra.at[it, 0 : 15 * 16])
        sent(8, ra.at[it, 0 : 15 * 16])

        @pl.when(first)
        def _(it=it, sent=sent):
            sent(1, ra.at[it, 0 : 15 * 16])
            sent(3, sb.at[it, 0:15])
            sent(4, ra.at[it, 0 : 16 * 16])
            sent(10, ra.at[it, 0 : 16 * 16])
            sent(9, ra.at[it, 0 : 15 * 16])

        @pl.when(second)
        def _(it=it, sent=sent):
            sent(1, ra.at[it, 0 : 16 * 16])
            sent(4, ra.at[it, 0 : 15 * 16])
            sent(10, ra.at[it, 0 : 15 * 16])
            sent(11, sb.at[it, 0:15])
            sent(9, ra.at[it, 0 : 16 * 16])

    last.wait()
    pltpu.make_async_copy(r, r_out, load_sem.at[13]).wait()


def finish(u_in, r_in, u_out, r_out):
    u_out[...] = u_in[...]
    r_out[...] = r_in[...]


def shards(solution, right_side, span_index, coef_table, xaxis_bands, yaxis_bands, zaxis_bands,
           xaxis_vectors, yaxis_vectors, zaxis_vectors, xaxis_values, yaxis_values, zaxis_values):
    flat = (128, 512)
    hbm = pl.BlockSpec(memory_space=pl.ANY)
    vmem = pl.BlockSpec(memory_space=pltpu.VMEM)
    V = pltpu.VMEM
    big = V((ITERS, 512, 128), F32)
    half = V((ITERS, 256, 128), F32)
    ring = V((ITERS, 16, 32, 128), F32)
    scratch = [
        V(flat, F32), V(flat, F32), V(flat, jnp.int32), V((512, 512), F32), V((256, 256), F32), V((256, 256), F32),
        V((7, 2, 512), F32), V((7, 2, 8), F32), V((7, 2, 16), F32), V((1, 512), F32), V((1, 256), F32), V((1, 256), F32), V((1, 8), F32),
        V(flat, F32), V(flat, F32), V((ITERS, 2, 24, 512), F32), V((ITERS, 4, 40, 128), F32),
        V((ITERS, 4, 40, 128), F32), V((ITERS, 48, 128), F32),
        V((ITERS, 256, 512), F32), V((ITERS, 128, 512), F32), V((256, 512), F32),
        big, big, ring, ring, half, half, big, V((256, 256), F32), half, half, half, big, ring, ring, half, big, V((512, 128), F32),
        V((256, 384), BF16), V((256, 384), BF16), V((512, 512), BF16), V((512, 512), BF16),
        V((256, 256), BF16), V((256, 256), BF16), V((256, 256), BF16), V((256, 256), BF16),
        V((256, 256), BF16), V((256, 256), BF16), V((256, 256), F32),
        V((512, 512), BF16), V((512, 512), BF16), V((512, 512), BF16), V((512, 512), BF16),
        pltpu.SemaphoreType.DMA((15,)), pltpu.SemaphoreType.DMA((ITERS, 12)), pltpu.SemaphoreType.DMA((ITERS, 12)),
    ]
    updated, residual = pl.pallas_call(
        kernel,
        out_shape=(jax.ShapeDtypeStruct(flat, F32), jax.ShapeDtypeStruct(flat, F32)),
        in_specs=[hbm] * 13,
        out_specs=(hbm, hbm),
        scratch_shapes=scratch,
        compiler_params=pltpu.CompilerParams(collective_id=0, has_side_effects=True),
        name="richardson",
    )(
        solution.reshape(flat), right_side.reshape(flat), span_index.reshape(flat), coef_table.reshape(1, 8),
        jnp.swapaxes(xaxis_bands, 0, 1), jnp.swapaxes(yaxis_bands, 0, 1), jnp.swapaxes(zaxis_bands, 0, 1),
        xaxis_vectors, yaxis_vectors, zaxis_vectors,
        xaxis_values.reshape(1, 512), yaxis_values.reshape(1, 256), zaxis_values.reshape(1, 256),
    )
    updated, residual = pl.pallas_call(
        finish,
        out_shape=(jax.ShapeDtypeStruct(flat, F32), jax.ShapeDtypeStruct(flat, F32)),
        in_specs=[vmem, vmem],
        out_specs=(vmem, vmem),
        name="finish",
    )(updated, residual)
    return updated.reshape(solution.shape), residual.reshape(solution.shape)


def solution(mesh):
    grid = P("py", "pz", None)
    return jax.shard_map(
        shards,
        mesh=mesh,
        in_specs=(grid, grid, grid, P(), P(), P(None, None, "py"), P(None, None, "pz"), P(), P(), P(), P(), P(), P()),
        out_specs=(grid, grid),
        check_vma=False,
    )
```

```python
import jax
import jax.numpy as jnp
from jax import lax
from jax.experimental import pallas as pl
from jax.experimental.pallas import tpu as pltpu
from jax.sharding import PartitionSpec as P

ITERS = 2
F32 = jnp.float32
BF16 = jnp.bfloat16
PLACES = ((0, 1), (2, 3), (4, 5), (6, 7))
RING = (8, 7, 9, 6, 10, 5, 11, 4, 12, 3, 13, 2, 14, 1, 15)


def split(v):
    hi = v.astype(BF16)
    return hi, (v - hi.astype(F32)).astype(BF16)


def dot3(a, b, dims=((1,), (0,))):
    def one(p, q):
        return lax.dot_general(p, q, (dims, ((), ())), preferred_element_type=F32)

    return one(a[0], b[0]) + one(a[0], b[1]) + one(a[1], b[0])


def swap_blocks(v, lane):
    v = pltpu.roll(v, 0, 1, stride=16, stride_axis=0)
    for bit in (1, 2, 4):
        v = jnp.where((lane // (16 * bit)) % 2 == 1, pltpu.roll(v, 8 - bit, 0), v)
    return pltpu.roll(v, 0, 1, stride=16, stride_axis=0)


def kernel(
    u_in, b_in, span_in, coef_in, xb_in, yb_in, zb_in, vx_in, vy_in, vz_in, xv_in, yv_in, zv_in,
    u_out, r_out,
    u, b, span, vx, vy, vz, xb, yb, zb, xv, yv, zv, coef, c, r, zs, cs, hc, rl, hr, w, acc,
    s, ra, sb, rb, rc, se, rd, m, mz, mg, rz, rg, sg, ry, sz, rx, ra2,
    bm_h, bm_l, vxt_h, vxt_l, vy_h, vy_l, vyt_h, vyt_l, vz_h, vz_l, den,
    kx_h, kx_l, mx_h, mx_l, load_sem, send_sem, recv_sem,
):
    py, pz = lax.axis_index("py"), lax.axis_index("pz")
    zh, yc = py // 8, py % 8
    x, zl = pz // 4, pz % 4
    top, bottom = yc == 7, yc == 0
    edge = top | bottom
    core = yc % 2
    first, second = core == 0, core == 1
    g = yc * 4 + x
    mine = (yc // 2) * 4 + x
    q = zh * 4 + zl

    def device(py2, pz2):
        return {"py": py2, "pz": pz2}

    def group(g2):
        return device(zh * 8 + g2 // 4, (g2 % 4) * 4 + zl)

    def ring(q2):
        return device((q2 // 4) * 8 + yc, x * 4 + q2 % 4)

    def near(dy, dz):
        return device((py + 32 + dy) % 32, (pz + 16 + dz) % 16)

    loads = [
        pltpu.make_async_copy(src, dst, load_sem.at[i])
        for i, (src, dst) in enumerate(
            ((u_in, u), (span_in, span), (vx_in, vx), (vy_in, vy), (vz_in, vz), (b_in, b),
             (xb_in, xb), (yb_in, yb), (zb_in, zb), (xv_in, xv), (yv_in, yv), (zv_in, zv), (coef_in, coef))
        )
    ]
    barrier = pltpu.get_barrier_semaphore()
    for k in RING:
        pl.semaphore_signal(barrier, inc=1, device_id=ring((q + k) % 16))
    for i in (0, 1, 12):
        loads[i].start()
    sides = [(dy, dz) for dy in (-1, 0, 1) for dz in (-1, 0, 1) if dy or dz]
    for dy, dz in sides:
        pl.semaphore_signal(barrier, inc=1, device_id=near(dy, dz))
    above, below = ((zh + 1) % 4) * 8, ((zh + 3) % 4) * 8

    @pl.when(bottom)
    def _():
        pl.semaphore_signal(barrier, inc=1, device_id=device(below + 1, pz))

    @pl.when(top)
    def _():
        pl.semaphore_signal(barrier, inc=1, device_id=device(above + 6, pz))

    def greet(k, carry):
        pl.semaphore_signal(barrier, inc=1, device_id=group((g + k) % 32))
        return carry

    lax.fori_loop(1, 32, greet, 0)
    for load in loads[2:12]:
        load.start()
    cs[...] = jnp.zeros_like(cs)
    for it in range(ITERS):
        hr[it, pl.ds(144, 112), :] = jnp.zeros((112, 512), F32)

    loads[0].wait()
    loads[1].wait()
    loads[12].wait()
    table = [coef[:, e : e + 1] for e in range(8)]

    def weigh(i, carry):
        rows = pl.ds(pl.multiple_of(i * 8, 8), 8)
        at = span[rows, :]
        v = jnp.broadcast_to(table[0], (8, 512))
        for e in range(1, 8):
            v = jnp.where(at == e, table[e], v)
        c[rows, :] = v
        w[0, rows, :] = v * u[rows, :]
        return carry

    lax.fori_loop(0, 16, weigh, 0)
    pl.semaphore_wait(barrier, 31 + 15 + 8 + jnp.where((yc == 1) | (yc == 6), 1, 0))

    sub = lax.broadcasted_iota(jnp.int32, (8, 128), 0)
    lane = lax.broadcasted_iota(jnp.int32, (8, 128), 1)

    def prepare():
        def coords(tile):
            if tile == 2:
                return lane // 16, lane % 16
            col = lane + tile * 128
            yy = jnp.where(col < 48, col // 16 - 3, 8 + (col - 48) // 16)
            zz = col % 16
            k = col - 96
            edge = col >= 96
            yy = jnp.where(edge, k % 8, yy)
            zz = jnp.where(edge, jnp.where(k < 24, k // 8 - 3, 16 + (k - 24) // 8), zz)
            k = col - 144
            corner = k >= 0
            cc = k % 16
            y3 = jnp.where(cc >= 6, 2, jnp.where(cc >= 3, 1, 0))
            z3 = cc - 3 * y3
            t = k // 16
            yy = jnp.where(corner, jnp.where(t < 2, y3 - 3, 8 + y3), yy)
            zz = jnp.where(corner, jnp.where(t % 2 == 0, z3 - 3, 16 + z3), zz)
            bad = (corner & (cc >= 9)) | (col >= 208)
            gy, gz = py * 8 + yy, pz * 16 + zz
            bad = bad | (gy < 0) | (gy > 255) | (gz < 0) | (gz > 255)
            return jnp.where(bad, 1000, yy), jnp.where(bad, 1000, zz)

        for i in (6, 7, 8):
            loads[i].wait()
        pick = lax.broadcasted_iota(jnp.int32, (8, 16), 1) - lax.broadcasted_iota(jnp.int32, (8, 16), 0)
        columns = {
            (kind, k, half): jnp.sum(
                jnp.where(pick == half * 8, zb[k, kind : kind + 1, :], 0.0), axis=1, keepdims=True
            )
            for kind in range(2) for k in range(7) for half in range(2)
        }
        for tile in range(3):
            yy, zz = coords(tile)
            ez = {}
            for half in range(2):
                dz = zz - (half * 8 + sub) + 3
                for kind in range(2):
                    total = jnp.zeros((8, 128), F32)
                    for k in range(7):
                        total = jnp.where(dz == k, columns[kind, k, half], total)
                    ez[kind, half] = total
            for y in range(8):
                dy = yy - y + 3
                ey = []
                for kind in range(2):
                    total = jnp.zeros((8, 128), F32)
                    for k in range(7):
                        total = jnp.where(dy == k, yb[k, kind : kind + 1, y : y + 1], total)
                    ey.append(total)
                mass = [ey[1] * ez[1, half] for half in range(2)]
                stiff = [ey[0] * ez[1, half] + ey[1] * ez[0, half] for half in range(2)]
                for base, pair in ((0, mass), (128, stiff)):
                    hi, lo = split(jnp.concatenate(pair, axis=0))
                    at = slice(base + y * 16, base + y * 16 + 16)
                    bm_h[at, tile * 128 : tile * 128 + 128] = hi
                    bm_l[at, tile * 128 : tile * 128 + 128] = lo
        for kind, (big, small) in enumerate(((kx_h, kx_l), (mx_h, mx_l))):
            for i in range(4):
                for j in range(4):
                    at = (slice(j * 128, j * 128 + 128), slice(i * 128, i * 128 + 128))
                    if abs(i - j) > 1:
                        big[at] = jnp.zeros((128, 128), BF16)
                        small[at] = jnp.zeros((128, 128), BF16)
                        continue
                    for part in range(0, 128, 16):
                        shape = (16, 128)
                        k_of = (j - i) * 128 + part + 3 + lax.broadcasted_iota(jnp.int32, shape, 0)
                        k_of = k_of - lax.broadcasted_iota(jnp.int32, shape, 1)
                        total = jnp.zeros(shape, F32)
                        for k in range(7):
                            total = jnp.where(k_of == k, xb[k, kind : kind + 1, at[1]], total)
                        hi, lo = split(total)
                        big[j * 128 + part : j * 128 + part + 16, at[1]] = hi
                        small[j * 128 + part : j * 128 + part + 16, at[1]] = lo
        loads[2].wait()
        for i in range(4):
            cols = slice(i * 128, i * 128 + 128)
            hi, lo = split(jnp.transpose(vx[:, cols]))
            vxt_h[cols, :] = hi
            vxt_l[cols, :] = lo
        loads[3].wait()
        vy_h[...], vy_l[...] = split(vy[...])
        vyt_h[...], vyt_l[...] = split(jnp.transpose(vy[...]))
        loads[4].wait()
        for p in range(2):
            for e in range(2):
                for xx in range(4):
                    to = p * 128 + e * 64 + xx * 16
                    at = xx * 64 + (2 * p + e) * 16
                    hi, lo = split(vz[at : at + 16, :])
                    vz_h[to : to + 16, :] = hi
                    vz_l[to : to + 16, :] = lo
        for i in (9, 10, 11):
            loads[i].wait()
        column = jnp.transpose(jnp.broadcast_to(yv[...], (128, 256)))
        j = jnp.where(first, mine * 16 + q, 256 + q * 16 + mine)
        row = lax.broadcasted_iota(jnp.int32, (1, 512), 1)
        shift = jnp.sum(jnp.where(row == j, xv[...], 0.0), axis=1, keepdims=True)
        for half in range(2):
            cols = slice(half * 128, half * 128 + 128)
            den[:, cols] = (column + zv[:, cols]) + shift
        loads[5].wait()

    quarter = [slice(k * 128, k * 128 + 128) for k in range(4)]

    def push(it, src, dst, stage, where, out=None):
        pltpu.make_async_remote_copy(
            src, dst, send_sem.at[it, stage if out is None else out], recv_sem.at[it, stage], device_id=where
        ).start()

    def rims(it):
        for i in range(3):
            for side, first in enumerate((0, 13)):
                for t in range(4):
                    cols = slice(t * 128, t * 128 + 128)
                    full = w[it, :, cols].reshape(8, 16, 128)
                    zs[it, side, i * 8 : i * 8 + 8, cols] = full[:, first + i, :]
        for cy in range(2):
            for cz in range(2):
                for i in range(3):
                    row = (cy * 5 + i) * 16 + cz * 13
                    three = w[it, row : row + 3, :]
                    for t in range(4):
                        at = t * 9 + i * 3
                        cs[it, cy * 2 + cz, at : at + 3, :] = three[:, t * 128 : t * 128 + 128]
        own = w.at[it]
        left, right = slice(0, 256), slice(256, 512)

        @pl.when(top)
        def _():
            push(it, own.at[80:128, left], rl.at[it], 5, device(zh * 8 + 1, pz))

        @pl.when(bottom)
        def _():
            push(it, own.at[0:48, right], rl.at[it], 5, device(zh * 8 + 6, pz))

        push(it, zs.at[it, 1], hr.at[it, 96:120], 0, near(0, 1))
        push(it, zs.at[it, 0], hr.at[it, 120:144], 0, near(0, -1))

        @pl.when(top)
        def _():
            push(it, own.at[80:128, right], hr.at[it, 0:48, right], 0, near(1, 0), 5)

        @pl.when(bottom)
        def _():
            push(it, own.at[0:48, left], hr.at[it, 48:96, left], 0, near(-1, 0), 5)

        @pl.when(jnp.logical_not(top))
        def _():
            push(it, own.at[80:128], hr.at[it, 0:48], 0, near(1, 0))

        @pl.when(jnp.logical_not(bottom))
        def _():
            push(it, own.at[0:48], hr.at[it, 48:96], 0, near(-1, 0))

        push(it, cs.at[it, 3], hc.at[it, 0], 6, near(1, 1))
        push(it, cs.at[it, 2], hc.at[it, 1], 6, near(1, -1))
        push(it, cs.at[it, 1], hc.at[it, 2], 6, near(-1, 1))
        push(it, cs.at[it, 0], hc.at[it, 3], 6, near(-1, -1))

    def relay(it):
        def passed():
            pltpu.make_async_remote_copy(
                rl.at[it], rl.at[it], send_sem.at[it, 5], recv_sem.at[it, 5], device_id=near(1, 0)
            ).wait_recv()

        @pl.when(yc == 1)
        def _():
            passed()
            push(it, rl.at[it], hr.at[it, 0:48, 0:256], 0, device(above, pz), 7)

        @pl.when(yc == 6)
        def _():
            passed()
            push(it, rl.at[it], hr.at[it, 48:96, 256:512], 0, device(below + 7, pz), 7)

    rims(0)
    relay(0)
    prepare()

    def step(it, carry):
        wide = split(w[it])
        acc[...] = dot3((bm_h[:, 256:384], bm_l[:, 256:384]), wide)
        pltpu.make_async_remote_copy(
            hr.at[it, 0:144], hr.at[it, 0:144], send_sem.at[it, 0], recv_sem.at[it, 0],
            device_id=near(1, 0),
        ).wait_recv()
        pltpu.make_async_remote_copy(
            hc.at[it], hc.at[it], send_sem.at[it, 6], recv_sem.at[it, 6], device_id=near(1, 0)
        ).wait_recv()
        for corner in range(4):
            for t in range(4):
                at = 144 + corner * 16
                hr[it, at : at + 9, quarter[t]] = hc[it, corner, t * 9 : t * 9 + 9, :]
        wide = split(hr[it])
        acc[...] += dot3((bm_h[:, 0:256], bm_l[:, 0:256]), wide)

        total = dot3(split(acc[0:128, :]), (kx_h[...], kx_l[...]))
        total = total + dot3(split(acc[128:256, :]), (mx_h[...], mx_l[...]))
        r[...] = b[...] - c[...] * total

        @pl.when(it == ITERS - 1)
        def _():
            r_out[...] = r[...]

        turned = [r[((8 - i) % 8) * 16 : ((8 - i) % 8) * 16 + 16, :] for i in range(8)]
        wide = split(jnp.concatenate(turned, axis=0))
        def block(i):
            return pl.ds(pl.multiple_of(i * 16, 16), 16)

        def modes(i):
            rows = slice(i * 128, i * 128 + 128)
            s[it, rows, :] = dot3((vxt_h[rows, :], vxt_l[rows, :]), wide, ((1,), (1,)))

        def wait_rows(part, stage):
            pltpu.make_async_remote_copy(
                part, part, send_sem.at[it, 0], recv_sem.at[it, stage], device_id=near(1, 0)
            ).wait_recv()

        def send_some(src, dst, stage, where, own, source=lambda i: i):
            def one(k, carry):
                i = (mine + k) % 16

                @pl.when(i != own)
                def _():
                    push(it, src.at[it, block(source(i))], dst, stage, where(i))

                return carry

            lax.fori_loop(0, 16, one, 0)

        def first_core(i):
            return device(zh * 8 + (i // 4) * 2, (i % 4) * 4 + zl)

        def second_core(i):
            return device(zh * 8 + (i // 4) * 2 + 1, (i % 4) * 4 + zl)

        none = 99
        modes(0)
        modes(1)
        send_some(s, ra.at[it, block(g)], 1, first_core, jnp.where(first, mine, none))
        modes(2)
        modes(3)
        for k in RING:
            q2 = (q + k) % 16
            push(it, s.at[it, block(16 + q2)], rc.at[it, block(q)], 2, ring(q2))
        rc[it, block(q), :] = s[it, block(16 + q), :]

        @pl.when(first)
        def _():
            ra[it, block(g), :] = s[it, block(mine), :]
            wait_rows(ra.at[it, 0 : 31 * 16], 1)
            for k in range(16):
                sb[it, k] = ra[it, pl.ds(k, 32, stride=16), :]
            for k in RING:
                q2 = (q + k) % 16
                push(it, sb.at[it, q2], rb.at[it, q], 3, ring(q2))
            rb[it, q] = sb[it, q]

        wait_rows(rc.at[it, 0 : 15 * 16], 2)
        for k in range(16):
            se[it, k * 16 : k * 16 + 16, :] = rc[it, pl.ds(k, 16, stride=16), :]
        send_some(se, rd.at[it, block(g)], 4, second_core, jnp.where(second, mine, none))

        @pl.when(first)
        def _():
            wait_rows(rb.at[it, 0:15], 3)

        @pl.when(second)
        def _():
            rd[it, block(g), :] = se[it, block(mine), :]
            wait_rows(rd.at[it, 0 : 31 * 16], 4)
            for k in range(16):
                rb[it, k] = rd[it, pl.ds(k, 32, stride=16), :]

        for h in range(4):
            for t in range(4):
                rows = slice(t * 8, t * 8 + 8)
                one, two = ((h * 8 + yy) * 8 for yy in PLACES[t])
                for p in range(2):
                    a = swap_blocks(rb[it, h * 4 + 2 * p, rows, :], lane)
                    e = swap_blocks(rb[it, h * 4 + 2 * p + 1, rows, :], lane)
                    m[one : one + 8, quarter[p]] = jnp.where(lane < 64, a, pltpu.roll(e, 64, 1))
                    m[two : two + 8, quarter[p]] = jnp.where(lane < 64, pltpu.roll(a, 64, 1), e)
        vzs = (vz_h[...], vz_l[...])
        m[...] = dot3(split(m[...]), vzs)
        m[...] = dot3((vyt_h[...], vyt_l[...]), split(m[...])) / den[...]
        m[...] = dot3((vy_h[...], vy_l[...]), split(m[...]))
        m[...] = dot3(split(m[...]), vzs, ((1,), (1,)))

        for t in range(4):
            for h in range(4):
                one, two = ((h * 8 + yy) * 8 for yy in PLACES[t])
                for p in range(2):
                    low, high = m[one : one + 8, quarter[p]], m[two : two + 8, quarter[p]]
                    pair = (
                        jnp.where(lane < 64, low, pltpu.roll(high, 64, 1)),
                        jnp.where(lane < 64, pltpu.roll(low, 64, 1), high),
                    )
                    for e, v in enumerate(pair):
                        v = pltpu.roll(swap_blocks(v, lane), 3, 0)
                        k = h * 4 + 2 * p + e
                        mz[it, k * 16 + t * 4 : k * 16 + t * 4 + 4, :] = v[0:4]
                        mg[it, pl.ds(t * 64 + k, 4, stride=16), :] = v[4:8]
        def turn(i):
            return (i // 4) * 4 + 3 - i % 4

        slot = core * 16 + mine
        send_some(mg, rg.at[it, block(slot)], 10, second_core, jnp.where(second, mine, none), turn)
        for k in RING:
            q2 = (q + k) % 16
            push(it, mz.at[it, block(q2)], rz.at[it, block(q)], 8, ring(q2))
        rz[it, block(q), :] = mz[it, block(q), :]

        @pl.when(second)
        def _():
            rg[it, block(slot), :] = mg[it, block(turn(mine)), :]
            wait_rows(rg.at[it, 0 : 31 * 16], 10)
            for k in range(16):
                sg[it, k] = rg[it, pl.ds(k, 32, stride=16), :]
            for k in RING:
                q2 = (q + k) % 16
                push(it, sg.at[it, q2], ry.at[it, q], 11, ring(q2))
            ry[it, q] = sg[it, q]

        wait_rows(rz.at[it, 0 : 15 * 16], 8)
        for k in range(16):
            sz[it, k * 16 : k * 16 + 16, :] = rz[it, pl.ds(k, 16, stride=16), :]
        send_some(sz, rx.at[it, block(slot)], 9, first_core, jnp.where(first, mine, none), turn)

        @pl.when(first)
        def _():
            rx[it, block(slot), :] = sz[it, block(turn(mine)), :]
            wait_rows(rx.at[it, 0 : 31 * 16], 9)
            ra2[0:256, :] = rx[it, 0:256, :]
            for k in range(16):
                ra2[256 + k * 16 : 272 + k * 16, :] = rx[it, pl.ds(256 + k, 16, stride=16), :]

        @pl.when(second)
        def _():
            wait_rows(ry.at[it, 0:15], 11)
            for k in range(16):
                ra2[256 + k * 16 : 272 + k * 16, :] = ry[it, k, 16:32, :]
                ra2[pl.ds(k, 16, stride=16), :] = ry[it, k, 0:16, :]

        wide = split(jnp.transpose(ra2[...]))
        u[...] += dot3(wide, (vxt_h[...], vxt_l[...]))

        @pl.when(it == ITERS - 1)
        def _():
            u_out[...] = u[...]

        @pl.when(it + 1 < ITERS)
        def _():
            w[it + 1] = c[...] * u[...]
            rims(it + 1)
            relay(it + 1)

        return carry

    lax.fori_loop(0, ITERS, step, 0)
    for it in range(ITERS):
        @pl.when(jnp.logical_not(top | bottom))
        def _(it=it):
            pltpu.make_async_remote_copy(
                hr.at[it, 0:144], hr.at[it, 0:144], send_sem.at[it, 0], recv_sem.at[it, 0], device_id=near(1, 0)
            ).wait_send()

        @pl.when((yc == 1) | (yc == 6))
        def _(it=it):
            pltpu.make_async_remote_copy(
                rl.at[it], rl.at[it], send_sem.at[it, 7], recv_sem.at[it, 0], device_id=near(1, 0)
            ).wait_send()

        @pl.when(top | bottom)
        def _(it=it):
            for stage, part in ((0, hr.at[it, 0:96]), (5, hr.at[it, 0:48])):
                pltpu.make_async_remote_copy(
                    part, part, send_sem.at[it, stage], recv_sem.at[it, stage], device_id=near(1, 0)
                ).wait_send()

        def sent(stage, part, it=it):
            pltpu.make_async_remote_copy(
                part, part, send_sem.at[it, stage], recv_sem.at[it, stage], device_id=near(1, 0)
            ).wait_send()

        sent(6, hc.at[it])
        sent(2, ra.at[it, 0 : 15 * 16])
        sent(8, ra.at[it, 0 : 15 * 16])

        @pl.when(first)
        def _(it=it, sent=sent):
            sent(1, ra.at[it, 0 : 15 * 16])
            sent(3, sb.at[it, 0:15])
            sent(4, ra.at[it, 0 : 16 * 16])
            sent(10, ra.at[it, 0 : 16 * 16])
            sent(9, ra.at[it, 0 : 15 * 16])

        @pl.when(second)
        def _(it=it, sent=sent):
            sent(1, ra.at[it, 0 : 16 * 16])
            sent(4, ra.at[it, 0 : 15 * 16])
            sent(10, ra.at[it, 0 : 15 * 16])
            sent(11, sb.at[it, 0:15])
            sent(9, ra.at[it, 0 : 16 * 16])


def finish(u_in, r_in, u_out, r_out):
    u_out[...] = u_in[...]
    r_out[...] = r_in[...]


def shards(solution, right_side, span_index, coef_table, xaxis_bands, yaxis_bands, zaxis_bands,
           xaxis_vectors, yaxis_vectors, zaxis_vectors, xaxis_values, yaxis_values, zaxis_values):
    flat = (128, 512)
    hbm = pl.BlockSpec(memory_space=pltpu.HBM)
    vmem = pl.BlockSpec(memory_space=pltpu.VMEM)
    V = pltpu.VMEM
    big = V((ITERS, 512, 128), F32)
    half = V((ITERS, 256, 128), F32)
    ring = V((ITERS, 16, 32, 128), F32)
    scratch = [
        V(flat, F32), V(flat, F32), V(flat, jnp.int32), V((512, 512), F32), V((256, 256), F32), V((256, 256), F32),
        V((7, 2, 512), F32), V((7, 2, 8), F32), V((7, 2, 16), F32), V((1, 512), F32), V((1, 256), F32), V((1, 256), F32), V((1, 8), F32),
        V(flat, F32), V(flat, F32), V((ITERS, 2, 24, 512), F32), V((ITERS, 4, 40, 128), F32),
        V((ITERS, 4, 40, 128), F32), V((ITERS, 48, 256), F32),
        V((ITERS, 256, 512), F32), V((ITERS, 128, 512), F32), V((256, 512), F32),
        big, big, ring, ring, half, half, big, V((256, 256), F32), half, half, half, big, ring, ring, half, big, V((512, 128), F32),
        V((256, 384), BF16), V((256, 384), BF16), V((512, 512), BF16), V((512, 512), BF16),
        V((256, 256), BF16), V((256, 256), BF16), V((256, 256), BF16), V((256, 256), BF16),
        V((256, 256), BF16), V((256, 256), BF16), V((256, 256), F32),
        V((512, 512), BF16), V((512, 512), BF16), V((512, 512), BF16), V((512, 512), BF16),
        pltpu.SemaphoreType.DMA((13,)), pltpu.SemaphoreType.DMA((ITERS, 12)), pltpu.SemaphoreType.DMA((ITERS, 12)),
    ]
    updated, residual = pl.pallas_call(
        kernel,
        out_shape=(jax.ShapeDtypeStruct(flat, F32), jax.ShapeDtypeStruct(flat, F32)),
        in_specs=[hbm] * 13,
        out_specs=(vmem, vmem),
        scratch_shapes=scratch,
        compiler_params=pltpu.CompilerParams(collective_id=0, has_side_effects=True, vmem_limit_bytes=24 * 1024 * 1024),
        name="richardson",
    )(*(pltpu.with_memory_space_constraint(a, pltpu.HBM) for a in (
        solution.reshape(flat), right_side.reshape(flat), span_index.reshape(flat), coef_table.reshape(1, 8),
        jnp.swapaxes(xaxis_bands, 0, 1), jnp.swapaxes(yaxis_bands, 0, 1), jnp.swapaxes(zaxis_bands, 0, 1),
        xaxis_vectors, yaxis_vectors, zaxis_vectors,
        xaxis_values.reshape(1, 512), yaxis_values.reshape(1, 256), zaxis_values.reshape(1, 256),
    )))
    updated, residual = pl.pallas_call(
        finish,
        out_shape=(jax.ShapeDtypeStruct(flat, F32), jax.ShapeDtypeStruct(flat, F32)),
        in_specs=[vmem, vmem],
        out_specs=(vmem, vmem),
        compiler_params=pltpu.CompilerParams(vmem_limit_bytes=8 * 1024 * 1024),
        name="finish",
    )(updated, residual)
    return updated.reshape(solution.shape), residual.reshape(solution.shape)


def solution(mesh):
    grid = P("py", "pz", None)
    return jax.shard_map(
        shards,
        mesh=mesh,
        in_specs=(grid, grid, grid, P(), P(), P(None, None, "py"), P(None, None, "pz"), P(), P(), P(), P(), P(), P()),
        out_specs=(grid, grid),
        check_vma=False,
    )
```

```python
import jax
import jax.numpy as jnp
from jax import lax
from jax.experimental import pallas as pl
from jax.experimental.pallas import tpu as pltpu
from jax.sharding import PartitionSpec as P

ITERS = 2
F32 = jnp.float32
BF16 = jnp.bfloat16
PLACES = ((0, 1), (2, 3), (4, 5), (6, 7))
FAR = ((2, 2), (2, 1), (1, 2), (2, 3), (3, 2), (0, 2), (2, 0), (1, 1), (1, 3), (3, 1), (3, 3), (0, 1), (1, 0), (0, 3), (3, 0))
RING = (8, 7, 9, 6, 10, 5, 11, 4, 12, 3, 13, 2, 14, 1, 15)


def split(v):
    hi = v.astype(BF16)
    return hi, (v - hi.astype(F32)).astype(BF16)


def dot3(a, b, dims=((1,), (0,))):
    def one(p, q):
        return lax.dot_general(p, q, (dims, ((), ())), preferred_element_type=F32)

    return one(a[0], b[0]) + one(a[0], b[1]) + one(a[1], b[0])


def swap_blocks(v, lane):
    v = pltpu.roll(v, 0, 1, stride=16, stride_axis=0)
    for bit in (1, 2, 4):
        v = jnp.where((lane // (16 * bit)) % 2 == 1, pltpu.roll(v, 8 - bit, 0), v)
    return pltpu.roll(v, 0, 1, stride=16, stride_axis=0)


def kernel(
    u_in, b_in, span_in, coef_in, xb_in, yb_in, zb_in, vx_in, vy_in, vz_in, xv_in, yv_in, zv_in,
    u_out, r_out,
    u, b, span, vx, vy, vz, xb, yb, zb, xv, yv, zv, coef, c, r, zs, cs, hc, rl, hr, w, acc,
    s, ra, sb, rb, rc, se, rd, m, mz, mg, rz, rg, sg, ry, sz, rx, ra2,
    bm_h, bm_l, vxt_h, vxt_l, vy_h, vy_l, vyt_h, vyt_l, vz_h, vz_l, den,
    kx_h, kx_l, mx_h, mx_l, load_sem, send_sem, recv_sem,
):
    py, pz = lax.axis_index("py"), lax.axis_index("pz")
    zh, yc = py // 8, py % 8
    x, zl = pz // 4, pz % 4
    top, bottom = yc == 7, yc == 0
    edge = top | bottom
    core = yc % 2
    first, second = core == 0, core == 1
    g = yc * 4 + x
    mine = (yc // 2) * 4 + x
    q = zh * 4 + zl

    def device(py2, pz2):
        return {"py": py2, "pz": pz2}

    def group(g2):
        return device(zh * 8 + g2 // 4, (g2 % 4) * 4 + zl)

    def ring(q2):
        return device((q2 // 4) * 8 + yc, x * 4 + q2 % 4)

    def near(dy, dz):
        return device((py + 32 + dy) % 32, (pz + 16 + dz) % 16)

    loads = [
        pltpu.make_async_copy(src, dst, load_sem.at[i])
        for i, (src, dst) in enumerate(
            ((u_in, u), (span_in, span), (vx_in, vx), (vy_in, vy), (vz_in, vz), (b_in, b),
             (xb_in, xb), (yb_in, yb), (zb_in, zb), (xv_in, xv), (yv_in, yv), (zv_in, zv), (coef_in, coef))
        )
    ]
    barrier = pltpu.get_barrier_semaphore()
    for k in RING:
        pl.semaphore_signal(barrier, inc=1, device_id=ring((q + k) % 16))
    for i in (0, 1, 12):
        loads[i].start()
    sides = [(dy, dz) for dy in (-1, 0, 1) for dz in (-1, 0, 1) if dy or dz]
    for dy, dz in sides:
        pl.semaphore_signal(barrier, inc=1, device_id=near(dy, dz))
    above, below = ((zh + 1) % 4) * 8, ((zh + 3) % 4) * 8

    @pl.when(bottom)
    def _():
        for k in range(3):
            pl.semaphore_signal(barrier, inc=1, device_id=device(below + 2 * k + 1, pz))

    @pl.when(top)
    def _():
        for k in range(1, 4):
            pl.semaphore_signal(barrier, inc=1, device_id=device(above + 2 * k, pz))

    def greet(k, carry):
        pl.semaphore_signal(barrier, inc=1, device_id=group((g + k) % 32))
        return carry

    lax.fori_loop(1, 32, greet, 0)
    for load in loads[2:12]:
        load.start()
    cs[...] = jnp.zeros_like(cs)
    for it in range(ITERS):
        hr[it, pl.ds(144, 112), :] = jnp.zeros((112, 512), F32)

    loads[0].wait()
    loads[1].wait()
    loads[12].wait()
    table = [coef[:, e : e + 1] for e in range(8)]

    def weigh(i, carry):
        rows = pl.ds(pl.multiple_of(i * 8, 8), 8)
        at = span[rows, :]
        v = jnp.broadcast_to(table[0], (8, 512))
        for e in range(1, 8):
            v = jnp.where(at == e, table[e], v)
        c[rows, :] = v
        w[0, rows, :] = v * u[rows, :]
        return carry

    lax.fori_loop(0, 16, weigh, 0)
    pl.semaphore_wait(barrier, 31 + 15 + 8 + jnp.where(top | bottom, 0, 1))

    sub = lax.broadcasted_iota(jnp.int32, (8, 128), 0)
    lane = lax.broadcasted_iota(jnp.int32, (8, 128), 1)

    def prepare():
        def coords(tile):
            if tile == 2:
                return lane // 16, lane % 16
            col = lane + tile * 128
            yy = jnp.where(col < 48, col // 16 - 3, 8 + (col - 48) // 16)
            zz = col % 16
            k = col - 96
            edge = col >= 96
            yy = jnp.where(edge, k % 8, yy)
            zz = jnp.where(edge, jnp.where(k < 24, k // 8 - 3, 16 + (k - 24) // 8), zz)
            k = col - 144
            corner = k >= 0
            cc = k % 16
            y3 = jnp.where(cc >= 6, 2, jnp.where(cc >= 3, 1, 0))
            z3 = cc - 3 * y3
            t = k // 16
            yy = jnp.where(corner, jnp.where(t < 2, y3 - 3, 8 + y3), yy)
            zz = jnp.where(corner, jnp.where(t % 2 == 0, z3 - 3, 16 + z3), zz)
            bad = (corner & (cc >= 9)) | (col >= 208)
            gy, gz = py * 8 + yy, pz * 16 + zz
            bad = bad | (gy < 0) | (gy > 255) | (gz < 0) | (gz > 255)
            return jnp.where(bad, 1000, yy), jnp.where(bad, 1000, zz)

        for i in (6, 7, 8):
            loads[i].wait()
        pick = lax.broadcasted_iota(jnp.int32, (8, 16), 1) - lax.broadcasted_iota(jnp.int32, (8, 16), 0)
        columns = {
            (kind, k, half): jnp.sum(
                jnp.where(pick == half * 8, zb[k, kind : kind + 1, :], 0.0), axis=1, keepdims=True
            )
            for kind in range(2) for k in range(7) for half in range(2)
        }
        for tile in range(3):
            yy, zz = coords(tile)
            ez = {}
            for half in range(2):
                dz = zz - (half * 8 + sub) + 3
                for kind in range(2):
                    total = jnp.zeros((8, 128), F32)
                    for k in range(7):
                        total = jnp.where(dz == k, columns[kind, k, half], total)
                    ez[kind, half] = total
            for y in range(8):
                dy = yy - y + 3
                ey = []
                for kind in range(2):
                    total = jnp.zeros((8, 128), F32)
                    for k in range(7):
                        total = jnp.where(dy == k, yb[k, kind : kind + 1, y : y + 1], total)
                    ey.append(total)
                mass = [ey[1] * ez[1, half] for half in range(2)]
                stiff = [ey[0] * ez[1, half] + ey[1] * ez[0, half] for half in range(2)]
                for base, pair in ((0, mass), (128, stiff)):
                    hi, lo = split(jnp.concatenate(pair, axis=0))
                    at = slice(base + y * 16, base + y * 16 + 16)
                    bm_h[at, tile * 128 : tile * 128 + 128] = hi
                    bm_l[at, tile * 128 : tile * 128 + 128] = lo
        for kind, (big, small) in enumerate(((kx_h, kx_l), (mx_h, mx_l))):
            for i in range(4):
                for j in range(4):
                    at = (slice(j * 128, j * 128 + 128), slice(i * 128, i * 128 + 128))
                    if abs(i - j) > 1:
                        big[at] = jnp.zeros((128, 128), BF16)
                        small[at] = jnp.zeros((128, 128), BF16)
                        continue
                    for part in range(0, 128, 16):
                        shape = (16, 128)
                        k_of = (j - i) * 128 + part + 3 + lax.broadcasted_iota(jnp.int32, shape, 0)
                        k_of = k_of - lax.broadcasted_iota(jnp.int32, shape, 1)
                        total = jnp.zeros(shape, F32)
                        for k in range(7):
                            total = jnp.where(k_of == k, xb[k, kind : kind + 1, at[1]], total)
                        hi, lo = split(total)
                        big[j * 128 + part : j * 128 + part + 16, at[1]] = hi
                        small[j * 128 + part : j * 128 + part + 16, at[1]] = lo
        loads[2].wait()
        for i in range(4):
            cols = slice(i * 128, i * 128 + 128)
            hi, lo = split(jnp.transpose(vx[:, cols]))
            vxt_h[cols, :] = hi
            vxt_l[cols, :] = lo
        loads[3].wait()
        vy_h[...], vy_l[...] = split(vy[...])
        vyt_h[...], vyt_l[...] = split(jnp.transpose(vy[...]))
        loads[4].wait()
        for p in range(2):
            for e in range(2):
                for xx in range(4):
                    to = p * 128 + e * 64 + xx * 16
                    at = xx * 64 + (2 * p + e) * 16
                    hi, lo = split(vz[at : at + 16, :])
                    vz_h[to : to + 16, :] = hi
                    vz_l[to : to + 16, :] = lo
        for i in (9, 10, 11):
            loads[i].wait()
        column = jnp.transpose(jnp.broadcast_to(yv[...], (128, 256)))
        j = jnp.where(first, mine * 16 + q, 256 + q * 16 + mine)
        row = lax.broadcasted_iota(jnp.int32, (1, 512), 1)
        shift = jnp.sum(jnp.where(row == j, xv[...], 0.0), axis=1, keepdims=True)
        for half in range(2):
            cols = slice(half * 128, half * 128 + 128)
            den[:, cols] = (column + zv[:, cols]) + shift
        loads[5].wait()

    quarter = [slice(k * 128, k * 128 + 128) for k in range(4)]

    def push(it, src, dst, stage, where, out=None):
        pltpu.make_async_remote_copy(
            src, dst, send_sem.at[it, stage if out is None else out], recv_sem.at[it, stage], device_id=where
        ).start()

    def rims(it):
        for i in range(3):
            for side, first in enumerate((0, 13)):
                for t in range(4):
                    cols = slice(t * 128, t * 128 + 128)
                    full = w[it, :, cols].reshape(8, 16, 128)
                    zs[it, side, i * 8 : i * 8 + 8, cols] = full[:, first + i, :]
        for cy in range(2):
            for cz in range(2):
                for i in range(3):
                    row = (cy * 5 + i) * 16 + cz * 13
                    three = w[it, row : row + 3, :]
                    for t in range(4):
                        at = t * 9 + i * 3
                        cs[it, cy * 2 + cz, at : at + 3, :] = three[:, t * 128 : t * 128 + 128]
        own = w.at[it]

        @pl.when(top)
        def _():
            for k in range(3):
                push(it, own.at[80:128, quarter[k]], rl.at[it], 5, device(zh * 8 + 2 * k + 1, pz))
            push(it, own.at[80:128, quarter[3]], hr.at[it, 0:48, quarter[3]], 0, near(1, 0), 5)

        @pl.when(bottom)
        def _():
            for k in range(1, 4):
                push(it, own.at[0:48, quarter[k]], rl.at[it], 5, device(zh * 8 + 2 * k, pz))
            push(it, own.at[0:48, quarter[0]], hr.at[it, 48:96, quarter[0]], 0, near(-1, 0), 5)

        push(it, cs.at[it, 3], hc.at[it, 0], 6, near(1, 1))
        push(it, cs.at[it, 2], hc.at[it, 1], 6, near(1, -1))
        push(it, cs.at[it, 1], hc.at[it, 2], 6, near(-1, 1))
        push(it, cs.at[it, 0], hc.at[it, 3], 6, near(-1, -1))

        @pl.when(jnp.logical_not(top))
        def _():
            push(it, own.at[80:128], hr.at[it, 0:48], 0, near(1, 0))

        @pl.when(jnp.logical_not(bottom))
        def _():
            push(it, own.at[0:48], hr.at[it, 48:96], 0, near(-1, 0))

        push(it, zs.at[it, 1], hr.at[it, 96:120], 0, near(0, 1))
        push(it, zs.at[it, 0], hr.at[it, 120:144], 0, near(0, -1))

    def relay(it):
        @pl.when(jnp.logical_not(top | bottom))
        def _():
            pltpu.make_async_remote_copy(
                rl.at[it], rl.at[it], send_sem.at[it, 5], recv_sem.at[it, 5], device_id=near(1, 0)
            ).wait_recv()
            odd = yc % 2 == 1
            start = pl.multiple_of(jnp.where(odd, 0, 48), 8)
            cols = pl.ds(pl.multiple_of((yc // 2) * 128, 128), 128)
            push(it, rl.at[it], hr.at[it, pl.ds(start, 48), cols], 0,
                 device(jnp.where(odd, above, below + 7), pz), 7)

    rims(0)
    relay(0)
    prepare()

    def step(it, carry):
        wide = split(w[it])
        acc[...] = dot3((bm_h[:, 256:384], bm_l[:, 256:384]), wide)
        pltpu.make_async_remote_copy(
            hr.at[it, 0:144], hr.at[it, 0:144], send_sem.at[it, 0], recv_sem.at[it, 0],
            device_id=near(1, 0),
        ).wait_recv()
        pltpu.make_async_remote_copy(
            hc.at[it], hc.at[it], send_sem.at[it, 6], recv_sem.at[it, 6], device_id=near(1, 0)
        ).wait_recv()
        for corner in range(4):
            for t in range(4):
                at = 144 + corner * 16
                hr[it, at : at + 9, quarter[t]] = hc[it, corner, t * 9 : t * 9 + 9, :]
        wide = split(hr[it])
        acc[...] += dot3((bm_h[:, 0:256], bm_l[:, 0:256]), wide)

        total = dot3(split(acc[0:128, :]), (kx_h[...], kx_l[...]))
        total = total + dot3(split(acc[128:256, :]), (mx_h[...], mx_l[...]))
        r[...] = b[...] - c[...] * total

        @pl.when(it == ITERS - 1)
        def _():
            r_out[...] = r[...]

        turned = [r[((8 - i) % 8) * 16 : ((8 - i) % 8) * 16 + 16, :] for i in range(8)]
        wide = split(jnp.concatenate(turned, axis=0))
        def block(i):
            return pl.ds(pl.multiple_of(i * 16, 16), 16)

        def modes(i):
            rows = slice(i * 128, i * 128 + 128)
            s[it, rows, :] = dot3((vxt_h[rows, :], vxt_l[rows, :]), wide, ((1,), (1,)))

        def wait_rows(part, stage):
            pltpu.make_async_remote_copy(
                part, part, send_sem.at[it, 0], recv_sem.at[it, stage], device_id=near(1, 0)
            ).wait_recv()

        modes(2)
        modes(3)
        for k in RING:
            q2 = (q + k) % 16
            push(it, s.at[it, block(16 + q2)], rc.at[it, block(q)], 2, ring(q2))
        rc[it, block(q), :] = s[it, block(16 + q), :]
        modes(0)
        modes(1)

        def send_some(src, dst, stage, where, own, source=lambda i: i):
            for dy, dx in FAR:
                i = ((mine // 4 + dy) % 4) * 4 + (mine % 4 + dx) % 4
                push(it, src.at[it, block(source(i))], dst, stage, where(i))

            @pl.when(mine != own)
            def _():
                push(it, src.at[it, block(source(mine))], dst, stage, where(mine))

        def first_core(i):
            return device(zh * 8 + (i // 4) * 2, (i % 4) * 4 + zl)

        def second_core(i):
            return device(zh * 8 + (i // 4) * 2 + 1, (i % 4) * 4 + zl)

        none = 99
        send_some(s, ra.at[it, block(g)], 1, first_core, jnp.where(first, mine, none))

        @pl.when(first)
        def _():
            ra[it, block(g), :] = s[it, block(mine), :]
            wait_rows(ra.at[it, 0 : 31 * 16], 1)
            for k in range(16):
                sb[it, k] = ra[it, pl.ds(k, 32, stride=16), :]
            for k in RING:
                q2 = (q + k) % 16
                push(it, sb.at[it, q2], rb.at[it, q], 3, ring(q2))
            rb[it, q] = sb[it, q]

        wait_rows(rc.at[it, 0 : 15 * 16], 2)
        for k in range(16):
            se[it, k * 16 : k * 16 + 16, :] = rc[it, pl.ds(k, 16, stride=16), :]
        send_some(se, rd.at[it, block(g)], 4, second_core, jnp.where(second, mine, none))

        @pl.when(first)
        def _():
            wait_rows(rb.at[it, 0:15], 3)

        @pl.when(second)
        def _():
            rd[it, block(g), :] = se[it, block(mine), :]
            wait_rows(rd.at[it, 0 : 31 * 16], 4)
            for k in range(16):
                rb[it, k] = rd[it, pl.ds(k, 32, stride=16), :]

        for h in range(4):
            for t in range(4):
                rows = slice(t * 8, t * 8 + 8)
                one, two = ((h * 8 + yy) * 8 for yy in PLACES[t])
                for p in range(2):
                    a = swap_blocks(rb[it, h * 4 + 2 * p, rows, :], lane)
                    e = swap_blocks(rb[it, h * 4 + 2 * p + 1, rows, :], lane)
                    m[one : one + 8, quarter[p]] = jnp.where(lane < 64, a, pltpu.roll(e, 64, 1))
                    m[two : two + 8, quarter[p]] = jnp.where(lane < 64, pltpu.roll(a, 64, 1), e)
        vzs = (vz_h[...], vz_l[...])
        m[...] = dot3(split(m[...]), vzs)
        m[...] = dot3((vyt_h[...], vyt_l[...]), split(m[...])) / den[...]
        m[...] = dot3((vy_h[...], vy_l[...]), split(m[...]))
        m[...] = dot3(split(m[...]), vzs, ((1,), (1,)))

        for t in range(4):
            for h in range(4):
                one, two = ((h * 8 + yy) * 8 for yy in PLACES[t])
                for p in range(2):
                    low, high = m[one : one + 8, quarter[p]], m[two : two + 8, quarter[p]]
                    pair = (
                        jnp.where(lane < 64, low, pltpu.roll(high, 64, 1)),
                        jnp.where(lane < 64, pltpu.roll(low, 64, 1), high),
                    )
                    for e, v in enumerate(pair):
                        v = pltpu.roll(swap_blocks(v, lane), 3, 0)
                        k = h * 4 + 2 * p + e
                        mz[it, k * 16 + t * 4 : k * 16 + t * 4 + 4, :] = v[0:4]
                        mg[it, pl.ds(t * 64 + k, 4, stride=16), :] = v[4:8]
        for k in RING:
            q2 = (q + k) % 16
            push(it, mz.at[it, block(q2)], rz.at[it, block(q)], 8, ring(q2))
        rz[it, block(q), :] = mz[it, block(q), :]

        def turn(i):
            return (i // 4) * 4 + 3 - i % 4

        slot = core * 16 + mine
        send_some(mg, rg.at[it, block(slot)], 10, second_core, jnp.where(second, mine, none), turn)

        @pl.when(second)
        def _():
            rg[it, block(slot), :] = mg[it, block(turn(mine)), :]
            wait_rows(rg.at[it, 0 : 31 * 16], 10)
            for k in range(16):
                sg[it, k] = rg[it, pl.ds(k, 32, stride=16), :]
            for k in RING:
                q2 = (q + k) % 16
                push(it, sg.at[it, q2], ry.at[it, q], 11, ring(q2))
            ry[it, q] = sg[it, q]

        wait_rows(rz.at[it, 0 : 15 * 16], 8)
        for k in range(16):
            sz[it, k * 16 : k * 16 + 16, :] = rz[it, pl.ds(k, 16, stride=16), :]
        send_some(sz, rx.at[it, block(slot)], 9, first_core, jnp.where(first, mine, none), turn)

        @pl.when(first)
        def _():
            rx[it, block(slot), :] = sz[it, block(turn(mine)), :]
            wait_rows(rx.at[it, 0 : 31 * 16], 9)
            ra2[0:256, :] = rx[it, 0:256, :]
            for k in range(16):
                ra2[256 + k * 16 : 272 + k * 16, :] = rx[it, pl.ds(256 + k, 16, stride=16), :]

        @pl.when(second)
        def _():
            wait_rows(ry.at[it, 0:15], 11)
            for k in range(16):
                ra2[256 + k * 16 : 272 + k * 16, :] = ry[it, k, 16:32, :]
                ra2[pl.ds(k, 16, stride=16), :] = ry[it, k, 0:16, :]

        wide = split(jnp.transpose(ra2[...]))
        u[...] += dot3(wide, (vxt_h[...], vxt_l[...]))

        @pl.when(it == ITERS - 1)
        def _():
            u_out[...] = u[...]

        @pl.when(it + 1 < ITERS)
        def _():
            w[it + 1] = c[...] * u[...]
            rims(it + 1)
            relay(it + 1)

        return carry

    lax.fori_loop(0, ITERS, step, 0)
    for it in range(ITERS):
        @pl.when(jnp.logical_not(top | bottom))
        def _(it=it):
            pltpu.make_async_remote_copy(
                hr.at[it, 0:144], hr.at[it, 0:144], send_sem.at[it, 0], recv_sem.at[it, 0], device_id=near(1, 0)
            ).wait_send()
            pltpu.make_async_remote_copy(
                rl.at[it], rl.at[it], send_sem.at[it, 7], recv_sem.at[it, 0], device_id=near(1, 0)
            ).wait_send()

        @pl.when(top | bottom)
        def _(it=it):
            for stage, part in ((0, hr.at[it, 0:96]), (5, hr.at[it, 0:48])):
                pltpu.make_async_remote_copy(
                    part, part, send_sem.at[it, stage], recv_sem.at[it, stage], device_id=near(1, 0)
                ).wait_send()

        def sent(stage, part, it=it):
            pltpu.make_async_remote_copy(
                part, part, send_sem.at[it, stage], recv_sem.at[it, stage], device_id=near(1, 0)
            ).wait_send()

        sent(6, hc.at[it])
        sent(2, ra.at[it, 0 : 15 * 16])
        sent(8, ra.at[it, 0 : 15 * 16])

        @pl.when(first)
        def _(it=it, sent=sent):
            sent(1, ra.at[it, 0 : 15 * 16])
            sent(3, sb.at[it, 0:15])
            sent(4, ra.at[it, 0 : 16 * 16])
            sent(10, ra.at[it, 0 : 16 * 16])
            sent(9, ra.at[it, 0 : 15 * 16])

        @pl.when(second)
        def _(it=it, sent=sent):
            sent(1, ra.at[it, 0 : 16 * 16])
            sent(4, ra.at[it, 0 : 15 * 16])
            sent(10, ra.at[it, 0 : 15 * 16])
            sent(11, sb.at[it, 0:15])
            sent(9, ra.at[it, 0 : 16 * 16])


def finish(u_in, r_in, u_out, r_out):
    u_out[...] = u_in[...]
    r_out[...] = r_in[...]


def shards(solution, right_side, span_index, coef_table, xaxis_bands, yaxis_bands, zaxis_bands,
           xaxis_vectors, yaxis_vectors, zaxis_vectors, xaxis_values, yaxis_values, zaxis_values):
    flat = (128, 512)
    hbm = pl.BlockSpec(memory_space=pl.ANY)
    vmem = pl.BlockSpec(memory_space=pltpu.VMEM)
    V = pltpu.VMEM
    big = V((ITERS, 512, 128), F32)
    half = V((ITERS, 256, 128), F32)
    ring = V((ITERS, 16, 32, 128), F32)
    scratch = [
        V(flat, F32), V(flat, F32), V(flat, jnp.int32), V((512, 512), F32), V((256, 256), F32), V((256, 256), F32),
        V((7, 2, 512), F32), V((7, 2, 8), F32), V((7, 2, 16), F32), V((1, 512), F32), V((1, 256), F32), V((1, 256), F32), V((1, 8), F32),
        V(flat, F32), V(flat, F32), V((ITERS, 2, 24, 512), F32), V((ITERS, 4, 40, 128), F32),
        V((ITERS, 4, 40, 128), F32), V((ITERS, 48, 128), F32),
        V((ITERS, 256, 512), F32), V((ITERS, 128, 512), F32), V((256, 512), F32),
        big, big, ring, ring, half, half, big, V((256, 256), F32), half, half, half, big, ring, ring, half, big, V((512, 128), F32),
        V((256, 384), BF16), V((256, 384), BF16), V((512, 512), BF16), V((512, 512), BF16),
        V((256, 256), BF16), V((256, 256), BF16), V((256, 256), BF16), V((256, 256), BF16),
        V((256, 256), BF16), V((256, 256), BF16), V((256, 256), F32),
        V((512, 512), BF16), V((512, 512), BF16), V((512, 512), BF16), V((512, 512), BF16),
        pltpu.SemaphoreType.DMA((13,)), pltpu.SemaphoreType.DMA((ITERS, 12)), pltpu.SemaphoreType.DMA((ITERS, 12)),
    ]
    updated, residual = pl.pallas_call(
        kernel,
        out_shape=(jax.ShapeDtypeStruct(flat, F32), jax.ShapeDtypeStruct(flat, F32)),
        in_specs=[hbm] * 13,
        out_specs=(vmem, vmem),
        scratch_shapes=scratch,
        compiler_params=pltpu.CompilerParams(collective_id=0, has_side_effects=True, vmem_limit_bytes=24 * 1024 * 1024),
        name="richardson",
    )(*(pltpu.with_memory_space_constraint(a, pltpu.HBM) for a in (
        solution.reshape(flat), right_side.reshape(flat), span_index.reshape(flat), coef_table.reshape(1, 8),
        jnp.swapaxes(xaxis_bands, 0, 1), jnp.swapaxes(yaxis_bands, 0, 1), jnp.swapaxes(zaxis_bands, 0, 1),
        xaxis_vectors, yaxis_vectors, zaxis_vectors,
        xaxis_values.reshape(1, 512), yaxis_values.reshape(1, 256), zaxis_values.reshape(1, 256),
    )))
    updated, residual = pl.pallas_call(
        finish,
        out_shape=(jax.ShapeDtypeStruct(flat, F32), jax.ShapeDtypeStruct(flat, F32)),
        in_specs=[vmem, vmem],
        out_specs=(vmem, vmem),
        compiler_params=pltpu.CompilerParams(vmem_limit_bytes=8 * 1024 * 1024),
        name="finish",
    )(updated, residual)
    return updated.reshape(solution.shape), residual.reshape(solution.shape)


def solution(mesh):
    grid = P("py", "pz", None)
    return jax.shard_map(
        shards,
        mesh=mesh,
        in_specs=(grid, grid, grid, P(), P(), P(None, None, "py"), P(None, None, "pz"), P(), P(), P(), P(), P(), P()),
        out_specs=(grid, grid),
        check_vma=False,
    )
```

```python
import jax
import jax.numpy as jnp
from jax import lax
from jax.experimental import pallas as pl
from jax.experimental.pallas import tpu as pltpu
from jax.sharding import PartitionSpec as P

ITERS = 2
F32 = jnp.float32
BF16 = jnp.bfloat16
PLACES = ((0, 1), (2, 3), (4, 5), (6, 7))
FAR = ((2, 2), (2, 1), (1, 2), (2, 3), (3, 2), (0, 2), (2, 0), (1, 1), (1, 3), (3, 1), (3, 3), (0, 1), (1, 0), (0, 3), (3, 0))
RING = (8, 7, 9, 6, 10, 5, 11, 4, 12, 3, 13, 2, 14, 1, 15)


def split(v):
    hi = v.astype(BF16)
    return hi, (v - hi.astype(F32)).astype(BF16)


def dot3(a, b, dims=((1,), (0,))):
    def one(p, q):
        return lax.dot_general(p, q, (dims, ((), ())), preferred_element_type=F32)

    return one(a[0], b[0]) + one(a[0], b[1]) + one(a[1], b[0])


def swap_blocks(v, lane):
    v = pltpu.roll(v, 0, 1, stride=16, stride_axis=0)
    for bit in (1, 2, 4):
        v = jnp.where((lane // (16 * bit)) % 2 == 1, pltpu.roll(v, 8 - bit, 0), v)
    return pltpu.roll(v, 0, 1, stride=16, stride_axis=0)


def kernel(
    u_in, b_in, span_in, coef_in, xb_in, yb_in, zb_in, vx_in, vy_in, vz_in, xv_in, yv_in, zv_in,
    u_out, r_out,
    u, b, span, vx, vy, vz, xb, yb, zb, xv, yv, zv, coef, c, r, zs, cs, hc, rl, hr, w, acc,
    s, ra, sb, rb, rc, se, rd, m, mz, mg, rz, rg, sg, ry, sz, rx, ra2,
    bm_h, bm_l, vxt_h, vxt_l, vy_h, vy_l, vyt_h, vyt_l, vz_h, vz_l, den,
    kx_h, kx_l, mx_h, mx_l, load_sem, send_sem, recv_sem,
):
    py, pz = lax.axis_index("py"), lax.axis_index("pz")
    zh, yc = py // 8, py % 8
    x, zl = pz // 4, pz % 4
    top, bottom = yc == 7, yc == 0
    edge = top | bottom
    core = yc % 2
    first, second = core == 0, core == 1
    g = yc * 4 + x
    mine = (yc // 2) * 4 + x
    q = zh * 4 + zl

    def device(py2, pz2):
        return {"py": py2, "pz": pz2}

    def group(g2):
        return device(zh * 8 + g2 // 4, (g2 % 4) * 4 + zl)

    def ring(q2):
        return device((q2 // 4) * 8 + yc, x * 4 + q2 % 4)

    def near(dy, dz):
        return device((py + 32 + dy) % 32, (pz + 16 + dz) % 16)

    loads = [
        pltpu.make_async_copy(src, dst, load_sem.at[i])
        for i, (src, dst) in enumerate(
            ((u_in, u), (span_in, span), (vx_in, vx), (vy_in, vy), (vz_in, vz), (b_in, b),
             (xb_in, xb), (yb_in, yb), (zb_in, zb), (xv_in, xv), (yv_in, yv), (zv_in, zv), (coef_in, coef))
        )
    ]
    barrier = pltpu.get_barrier_semaphore()
    for k in RING:
        pl.semaphore_signal(barrier, inc=1, device_id=ring((q + k) % 16))
    for i in (0, 1, 12):
        loads[i].start()
    sides = [(dy, dz) for dy in (-1, 0, 1) for dz in (-1, 0, 1) if dy or dz]
    for dy, dz in sides:
        pl.semaphore_signal(barrier, inc=1, device_id=near(dy, dz))
    above, below = ((zh + 1) % 4) * 8, ((zh + 3) % 4) * 8

    @pl.when(bottom)
    def _():
        for k in range(3):
            pl.semaphore_signal(barrier, inc=1, device_id=device(below + 2 * k + 1, pz))

    @pl.when(top)
    def _():
        for k in range(1, 4):
            pl.semaphore_signal(barrier, inc=1, device_id=device(above + 2 * k, pz))

    def greet(k, carry):
        pl.semaphore_signal(barrier, inc=1, device_id=group((g + k) % 32))
        return carry

    lax.fori_loop(1, 32, greet, 0)
    for load in loads[2:12]:
        load.start()
    cs[...] = jnp.zeros_like(cs)
    for it in range(ITERS):
        hr[it, pl.ds(144, 112), :] = jnp.zeros((112, 512), F32)

    loads[0].wait()
    loads[1].wait()
    loads[12].wait()
    table = [coef[:, e : e + 1] for e in range(8)]

    def weigh(i, carry):
        rows = pl.ds(pl.multiple_of(i * 8, 8), 8)
        at = span[rows, :]
        v = jnp.broadcast_to(table[0], (8, 512))
        for e in range(1, 8):
            v = jnp.where(at == e, table[e], v)
        c[rows, :] = v
        w[0, rows, :] = v * u[rows, :]
        return carry

    lax.fori_loop(0, 16, weigh, 0)
    pl.semaphore_wait(barrier, 31 + 15 + 8 + jnp.where(top | bottom, 0, 1))

    sub = lax.broadcasted_iota(jnp.int32, (8, 128), 0)
    lane = lax.broadcasted_iota(jnp.int32, (8, 128), 1)

    def prepare():
        def coords(tile):
            if tile == 2:
                return lane // 16, lane % 16
            col = lane + tile * 128
            yy = jnp.where(col < 48, col // 16 - 3, 8 + (col - 48) // 16)
            zz = col % 16
            k = col - 96
            edge = col >= 96
            yy = jnp.where(edge, k % 8, yy)
            zz = jnp.where(edge, jnp.where(k < 24, k // 8 - 3, 16 + (k - 24) // 8), zz)
            k = col - 144
            corner = k >= 0
            cc = k % 16
            y3 = jnp.where(cc >= 6, 2, jnp.where(cc >= 3, 1, 0))
            z3 = cc - 3 * y3
            t = k // 16
            yy = jnp.where(corner, jnp.where(t < 2, y3 - 3, 8 + y3), yy)
            zz = jnp.where(corner, jnp.where(t % 2 == 0, z3 - 3, 16 + z3), zz)
            bad = (corner & (cc >= 9)) | (col >= 208)
            gy, gz = py * 8 + yy, pz * 16 + zz
            bad = bad | (gy < 0) | (gy > 255) | (gz < 0) | (gz > 255)
            return jnp.where(bad, 1000, yy), jnp.where(bad, 1000, zz)

        for i in (6, 7, 8):
            loads[i].wait()
        pick = lax.broadcasted_iota(jnp.int32, (8, 16), 1) - lax.broadcasted_iota(jnp.int32, (8, 16), 0)
        columns = {
            (kind, k, half): jnp.sum(
                jnp.where(pick == half * 8, zb[k, kind : kind + 1, :], 0.0), axis=1, keepdims=True
            )
            for kind in range(2) for k in range(7) for half in range(2)
        }
        for tile in range(3):
            yy, zz = coords(tile)
            ez = {}
            for half in range(2):
                dz = zz - (half * 8 + sub) + 3
                for kind in range(2):
                    total = jnp.zeros((8, 128), F32)
                    for k in range(7):
                        total = jnp.where(dz == k, columns[kind, k, half], total)
                    ez[kind, half] = total
            for y in range(8):
                dy = yy - y + 3
                ey = []
                for kind in range(2):
                    total = jnp.zeros((8, 128), F32)
                    for k in range(7):
                        total = jnp.where(dy == k, yb[k, kind : kind + 1, y : y + 1], total)
                    ey.append(total)
                mass = [ey[1] * ez[1, half] for half in range(2)]
                stiff = [ey[0] * ez[1, half] + ey[1] * ez[0, half] for half in range(2)]
                for base, pair in ((0, mass), (128, stiff)):
                    hi, lo = split(jnp.concatenate(pair, axis=0))
                    at = slice(base + y * 16, base + y * 16 + 16)
                    bm_h[at, tile * 128 : tile * 128 + 128] = hi
                    bm_l[at, tile * 128 : tile * 128 + 128] = lo
        for kind, (big, small) in enumerate(((kx_h, kx_l), (mx_h, mx_l))):
            for i in range(4):
                for j in range(4):
                    at = (slice(j * 128, j * 128 + 128), slice(i * 128, i * 128 + 128))
                    if abs(i - j) > 1:
                        big[at] = jnp.zeros((128, 128), BF16)
                        small[at] = jnp.zeros((128, 128), BF16)
                        continue
                    for part in range(0, 128, 16):
                        shape = (16, 128)
                        k_of = (j - i) * 128 + part + 3 + lax.broadcasted_iota(jnp.int32, shape, 0)
                        k_of = k_of - lax.broadcasted_iota(jnp.int32, shape, 1)
                        total = jnp.zeros(shape, F32)
                        for k in range(7):
                            total = jnp.where(k_of == k, xb[k, kind : kind + 1, at[1]], total)
                        hi, lo = split(total)
                        big[j * 128 + part : j * 128 + part + 16, at[1]] = hi
                        small[j * 128 + part : j * 128 + part + 16, at[1]] = lo
        loads[2].wait()
        for i in range(4):
            cols = slice(i * 128, i * 128 + 128)
            hi, lo = split(jnp.transpose(vx[:, cols]))
            vxt_h[cols, :] = hi
            vxt_l[cols, :] = lo
        loads[3].wait()
        vy_h[...], vy_l[...] = split(vy[...])
        vyt_h[...], vyt_l[...] = split(jnp.transpose(vy[...]))
        loads[4].wait()
        for p in range(2):
            for e in range(2):
                for xx in range(4):
                    to = p * 128 + e * 64 + xx * 16
                    at = xx * 64 + (2 * p + e) * 16
                    hi, lo = split(vz[at : at + 16, :])
                    vz_h[to : to + 16, :] = hi
                    vz_l[to : to + 16, :] = lo
        for i in (9, 10, 11):
            loads[i].wait()
        column = jnp.transpose(jnp.broadcast_to(yv[...], (128, 256)))
        j = jnp.where(first, mine * 16 + q, 256 + q * 16 + mine)
        row = lax.broadcasted_iota(jnp.int32, (1, 512), 1)
        shift = jnp.sum(jnp.where(row == j, xv[...], 0.0), axis=1, keepdims=True)
        for half in range(2):
            cols = slice(half * 128, half * 128 + 128)
            den[:, cols] = (column + zv[:, cols]) + shift
        loads[5].wait()

    quarter = [slice(k * 128, k * 128 + 128) for k in range(4)]

    def push(it, src, dst, stage, where, out=None):
        pltpu.make_async_remote_copy(
            src, dst, send_sem.at[it, stage if out is None else out], recv_sem.at[it, stage], device_id=where
        ).start()

    def rims(it):
        for i in range(3):
            for side, first in enumerate((0, 13)):
                for t in range(4):
                    cols = slice(t * 128, t * 128 + 128)
                    full = w[it, :, cols].reshape(8, 16, 128)
                    zs[it, side, i * 8 : i * 8 + 8, cols] = full[:, first + i, :]
        for cy in range(2):
            for cz in range(2):
                for i in range(3):
                    row = (cy * 5 + i) * 16 + cz * 13
                    three = w[it, row : row + 3, :]
                    for t in range(4):
                        at = t * 9 + i * 3
                        cs[it, cy * 2 + cz, at : at + 3, :] = three[:, t * 128 : t * 128 + 128]
        own = w.at[it]

        @pl.when(top)
        def _():
            for k in range(3):
                push(it, own.at[80:128, quarter[k]], rl.at[it], 5, device(zh * 8 + 2 * k + 1, pz))
            push(it, own.at[80:128, quarter[3]], hr.at[it, 0:48, quarter[3]], 0, near(1, 0), 5)

        @pl.when(bottom)
        def _():
            for k in range(1, 4):
                push(it, own.at[0:48, quarter[k]], rl.at[it], 5, device(zh * 8 + 2 * k, pz))
            push(it, own.at[0:48, quarter[0]], hr.at[it, 48:96, quarter[0]], 0, near(-1, 0), 5)

        push(it, cs.at[it, 3], hc.at[it, 0], 6, near(1, 1))
        push(it, cs.at[it, 2], hc.at[it, 1], 6, near(1, -1))
        push(it, cs.at[it, 1], hc.at[it, 2], 6, near(-1, 1))
        push(it, cs.at[it, 0], hc.at[it, 3], 6, near(-1, -1))
        push(it, zs.at[it, 1], hr.at[it, 96:120], 0, near(0, 1))
        push(it, zs.at[it, 0], hr.at[it, 120:144], 0, near(0, -1))

        @pl.when(jnp.logical_not(top))
        def _():
            push(it, own.at[80:128], hr.at[it, 0:48], 0, near(1, 0))

        @pl.when(jnp.logical_not(bottom))
        def _():
            push(it, own.at[0:48], hr.at[it, 48:96], 0, near(-1, 0))


    def relay(it):
        @pl.when(jnp.logical_not(top | bottom))
        def _():
            pltpu.make_async_remote_copy(
                rl.at[it], rl.at[it], send_sem.at[it, 5], recv_sem.at[it, 5], device_id=near(1, 0)
            ).wait_recv()
            odd = yc % 2 == 1
            start = pl.multiple_of(jnp.where(odd, 0, 48), 8)
            cols = pl.ds(pl.multiple_of((yc // 2) * 128, 128), 128)
            push(it, rl.at[it], hr.at[it, pl.ds(start, 48), cols], 0,
                 device(jnp.where(odd, above, below + 7), pz), 7)

    rims(0)
    relay(0)
    prepare()

    def step(it, carry):
        wide = split(w[it])
        acc[...] = dot3((bm_h[:, 256:384], bm_l[:, 256:384]), wide)
        pltpu.make_async_remote_copy(
            hr.at[it, 0:144], hr.at[it, 0:144], send_sem.at[it, 0], recv_sem.at[it, 0],
            device_id=near(1, 0),
        ).wait_recv()
        pltpu.make_async_remote_copy(
            hc.at[it], hc.at[it], send_sem.at[it, 6], recv_sem.at[it, 6], device_id=near(1, 0)
        ).wait_recv()
        for corner in range(4):
            for t in range(4):
                at = 144 + corner * 16
                hr[it, at : at + 9, quarter[t]] = hc[it, corner, t * 9 : t * 9 + 9, :]
        wide = split(hr[it])
        acc[...] += dot3((bm_h[:, 0:256], bm_l[:, 0:256]), wide)

        total = dot3(split(acc[0:128, :]), (kx_h[...], kx_l[...]))
        total = total + dot3(split(acc[128:256, :]), (mx_h[...], mx_l[...]))
        r[...] = b[...] - c[...] * total

        @pl.when(it == ITERS - 1)
        def _():
            r_out[...] = r[...]

        turned = [r[((8 - i) % 8) * 16 : ((8 - i) % 8) * 16 + 16, :] for i in range(8)]
        wide = split(jnp.concatenate(turned, axis=0))
        def block(i):
            return pl.ds(pl.multiple_of(i * 16, 16), 16)

        def modes(i):
            rows = slice(i * 128, i * 128 + 128)
            s[it, rows, :] = dot3((vxt_h[rows, :], vxt_l[rows, :]), wide, ((1,), (1,)))

        def wait_rows(part, stage):
            pltpu.make_async_remote_copy(
                part, part, send_sem.at[it, 0], recv_sem.at[it, stage], device_id=near(1, 0)
            ).wait_recv()

        modes(2)
        modes(3)
        for k in RING:
            q2 = (q + k) % 16
            push(it, s.at[it, block(16 + q2)], rc.at[it, block(q)], 2, ring(q2))
        rc[it, block(q), :] = s[it, block(16 + q), :]
        modes(0)
        modes(1)

        def send_some(src, dst, stage, where, own, source=lambda i: i):
            for dy, dx in FAR:
                i = ((mine // 4 + dy) % 4) * 4 + (mine % 4 + dx) % 4
                push(it, src.at[it, block(source(i))], dst, stage, where(i))

            @pl.when(mine != own)
            def _():
                push(it, src.at[it, block(source(mine))], dst, stage, where(mine))

        def first_core(i):
            return device(zh * 8 + (i // 4) * 2, (i % 4) * 4 + zl)

        def second_core(i):
            return device(zh * 8 + (i // 4) * 2 + 1, (i % 4) * 4 + zl)

        none = 99
        send_some(s, ra.at[it, block(g)], 1, first_core, jnp.where(first, mine, none))

        @pl.when(first)
        def _():
            ra[it, block(g), :] = s[it, block(mine), :]
            wait_rows(ra.at[it, 0 : 31 * 16], 1)
            for k in range(16):
                sb[it, k] = ra[it, pl.ds(k, 32, stride=16), :]
            for k in RING:
                q2 = (q + k) % 16
                push(it, sb.at[it, q2], rb.at[it, q], 3, ring(q2))
            rb[it, q] = sb[it, q]

        wait_rows(rc.at[it, 0 : 15 * 16], 2)
        for k in range(16):
            se[it, k * 16 : k * 16 + 16, :] = rc[it, pl.ds(k, 16, stride=16), :]
        send_some(se, rd.at[it, block(g)], 4, second_core, jnp.where(second, mine, none))

        @pl.when(first)
        def _():
            wait_rows(rb.at[it, 0:15], 3)

        @pl.when(second)
        def _():
            rd[it, block(g), :] = se[it, block(mine), :]
            wait_rows(rd.at[it, 0 : 31 * 16], 4)
            for k in range(16):
                rb[it, k] = rd[it, pl.ds(k, 32, stride=16), :]

        for h in range(4):
            for t in range(4):
                rows = slice(t * 8, t * 8 + 8)
                one, two = ((h * 8 + yy) * 8 for yy in PLACES[t])
                for p in range(2):
                    a = swap_blocks(rb[it, h * 4 + 2 * p, rows, :], lane)
                    e = swap_blocks(rb[it, h * 4 + 2 * p + 1, rows, :], lane)
                    m[one : one + 8, quarter[p]] = jnp.where(lane < 64, a, pltpu.roll(e, 64, 1))
                    m[two : two + 8, quarter[p]] = jnp.where(lane < 64, pltpu.roll(a, 64, 1), e)
        vzs = (vz_h[...], vz_l[...])
        m[...] = dot3(split(m[...]), vzs)
        m[...] = dot3((vyt_h[...], vyt_l[...]), split(m[...])) / den[...]
        m[...] = dot3((vy_h[...], vy_l[...]), split(m[...]))
        m[...] = dot3(split(m[...]), vzs, ((1,), (1,)))

        for t in range(4):
            for h in range(4):
                one, two = ((h * 8 + yy) * 8 for yy in PLACES[t])
                for p in range(2):
                    low, high = m[one : one + 8, quarter[p]], m[two : two + 8, quarter[p]]
                    pair = (
                        jnp.where(lane < 64, low, pltpu.roll(high, 64, 1)),
                        jnp.where(lane < 64, pltpu.roll(low, 64, 1), high),
                    )
                    for e, v in enumerate(pair):
                        v = pltpu.roll(swap_blocks(v, lane), 3, 0)
                        k = h * 4 + 2 * p + e
                        mz[it, k * 16 + t * 4 : k * 16 + t * 4 + 4, :] = v[0:4]
                        mg[it, pl.ds(t * 64 + k, 4, stride=16), :] = v[4:8]
        for k in RING:
            q2 = (q + k) % 16
            push(it, mz.at[it, block(q2)], rz.at[it, block(q)], 8, ring(q2))
        rz[it, block(q), :] = mz[it, block(q), :]

        def turn(i):
            return (i // 4) * 4 + 3 - i % 4

        slot = core * 16 + mine
        send_some(mg, rg.at[it, block(slot)], 10, second_core, jnp.where(second, mine, none), turn)

        @pl.when(second)
        def _():
            rg[it, block(slot), :] = mg[it, block(turn(mine)), :]
            wait_rows(rg.at[it, 0 : 31 * 16], 10)
            for k in range(16):
                sg[it, k] = rg[it, pl.ds(k, 32, stride=16), :]
            for k in RING:
                q2 = (q + k) % 16
                push(it, sg.at[it, q2], ry.at[it, q], 11, ring(q2))
            ry[it, q] = sg[it, q]

        wait_rows(rz.at[it, 0 : 15 * 16], 8)
        for k in range(16):
            sz[it, k * 16 : k * 16 + 16, :] = rz[it, pl.ds(k, 16, stride=16), :]
        send_some(sz, rx.at[it, block(slot)], 9, first_core, jnp.where(first, mine, none), turn)

        @pl.when(first)
        def _():
            rx[it, block(slot), :] = sz[it, block(turn(mine)), :]
            wait_rows(rx.at[it, 0 : 31 * 16], 9)
            ra2[0:256, :] = rx[it, 0:256, :]
            for k in range(16):
                ra2[256 + k * 16 : 272 + k * 16, :] = rx[it, pl.ds(256 + k, 16, stride=16), :]

        @pl.when(second)
        def _():
            wait_rows(ry.at[it, 0:15], 11)
            for k in range(16):
                ra2[256 + k * 16 : 272 + k * 16, :] = ry[it, k, 16:32, :]
                ra2[pl.ds(k, 16, stride=16), :] = ry[it, k, 0:16, :]

        wide = split(jnp.transpose(ra2[...]))
        u[...] += dot3(wide, (vxt_h[...], vxt_l[...]))

        @pl.when(it == ITERS - 1)
        def _():
            u_out[...] = u[...]

        @pl.when(it + 1 < ITERS)
        def _():
            w[it + 1] = c[...] * u[...]
            rims(it + 1)
            relay(it + 1)

        return carry

    lax.fori_loop(0, ITERS, step, 0)
    for it in range(ITERS):
        @pl.when(jnp.logical_not(top | bottom))
        def _(it=it):
            pltpu.make_async_remote_copy(
                hr.at[it, 0:144], hr.at[it, 0:144], send_sem.at[it, 0], recv_sem.at[it, 0], device_id=near(1, 0)
            ).wait_send()
            pltpu.make_async_remote_copy(
                rl.at[it], rl.at[it], send_sem.at[it, 7], recv_sem.at[it, 0], device_id=near(1, 0)
            ).wait_send()

        @pl.when(top | bottom)
        def _(it=it):
            for stage, part in ((0, hr.at[it, 0:96]), (5, hr.at[it, 0:48])):
                pltpu.make_async_remote_copy(
                    part, part, send_sem.at[it, stage], recv_sem.at[it, stage], device_id=near(1, 0)
                ).wait_send()

        def sent(stage, part, it=it):
            pltpu.make_async_remote_copy(
                part, part, send_sem.at[it, stage], recv_sem.at[it, stage], device_id=near(1, 0)
            ).wait_send()

        sent(6, hc.at[it])
        sent(2, ra.at[it, 0 : 15 * 16])
        sent(8, ra.at[it, 0 : 15 * 16])

        @pl.when(first)
        def _(it=it, sent=sent):
            sent(1, ra.at[it, 0 : 15 * 16])
            sent(3, sb.at[it, 0:15])
            sent(4, ra.at[it, 0 : 16 * 16])
            sent(10, ra.at[it, 0 : 16 * 16])
            sent(9, ra.at[it, 0 : 15 * 16])

        @pl.when(second)
        def _(it=it, sent=sent):
            sent(1, ra.at[it, 0 : 16 * 16])
            sent(4, ra.at[it, 0 : 15 * 16])
            sent(10, ra.at[it, 0 : 15 * 16])
            sent(11, sb.at[it, 0:15])
            sent(9, ra.at[it, 0 : 16 * 16])


def finish(u_in, r_in, u_out, r_out):
    u_out[...] = u_in[...]
    r_out[...] = r_in[...]


def shards(solution, right_side, span_index, coef_table, xaxis_bands, yaxis_bands, zaxis_bands,
           xaxis_vectors, yaxis_vectors, zaxis_vectors, xaxis_values, yaxis_values, zaxis_values):
    flat = (128, 512)
    hbm = pl.BlockSpec(memory_space=pl.ANY)
    vmem = pl.BlockSpec(memory_space=pltpu.VMEM)
    V = pltpu.VMEM
    big = V((ITERS + 1, 512, 128), F32)
    half = V((ITERS + 1, 256, 128), F32)
    ring = V((ITERS, 16, 32, 128), F32)
    scratch = [
        V(flat, F32), V(flat, F32), V(flat, jnp.int32), V((512, 512), F32), V((256, 256), F32), V((256, 256), F32),
        V((7, 2, 512), F32), V((7, 2, 8), F32), V((7, 2, 16), F32), V((1, 512), F32), V((1, 256), F32), V((1, 256), F32), V((1, 8), F32),
        V(flat, F32), V(flat, F32), V((ITERS, 2, 24, 512), F32), V((ITERS + 1, 4, 40, 128), F32),
        V((ITERS + 1, 4, 40, 128), F32), V((ITERS, 48, 128), F32),
        V((ITERS, 256, 512), F32), V((ITERS + 1, 128, 512), F32), V((256, 512), F32),
        big, big, ring, ring, half, half, big, V((256, 256), F32), half, half, half, big, ring, ring, half, big, V((512, 128), F32),
        V((256, 384), BF16), V((256, 384), BF16), V((512, 512), BF16), V((512, 512), BF16),
        V((256, 256), BF16), V((256, 256), BF16), V((256, 256), BF16), V((256, 256), BF16),
        V((256, 256), BF16), V((256, 256), BF16), V((256, 256), F32),
        V((512, 512), BF16), V((512, 512), BF16), V((512, 512), BF16), V((512, 512), BF16),
        pltpu.SemaphoreType.DMA((13,)), pltpu.SemaphoreType.DMA((ITERS, 12)), pltpu.SemaphoreType.DMA((ITERS, 12)),
    ]
    updated, residual = pl.pallas_call(
        kernel,
        out_shape=(jax.ShapeDtypeStruct(flat, F32), jax.ShapeDtypeStruct(flat, F32)),
        in_specs=[hbm] * 13,
        out_specs=(vmem, vmem),
        scratch_shapes=scratch,
        compiler_params=pltpu.CompilerParams(collective_id=0, has_side_effects=True, vmem_limit_bytes=24 * 1024 * 1024),
        name="richardson",
    )(*(pltpu.with_memory_space_constraint(a, pltpu.HBM) for a in (
        solution.reshape(flat), right_side.reshape(flat), span_index.reshape(flat), coef_table.reshape(1, 8),
        jnp.swapaxes(xaxis_bands, 0, 1), jnp.swapaxes(yaxis_bands, 0, 1), jnp.swapaxes(zaxis_bands, 0, 1),
        xaxis_vectors, yaxis_vectors, zaxis_vectors,
        xaxis_values.reshape(1, 512), yaxis_values.reshape(1, 256), zaxis_values.reshape(1, 256),
    )))
    updated, residual = pl.pallas_call(
        finish,
        out_shape=(jax.ShapeDtypeStruct(flat, F32), jax.ShapeDtypeStruct(flat, F32)),
        in_specs=[vmem, vmem],
        out_specs=(vmem, vmem),
        compiler_params=pltpu.CompilerParams(vmem_limit_bytes=8 * 1024 * 1024),
        name="finish",
    )(updated, residual)
    return updated.reshape(solution.shape), residual.reshape(solution.shape)


def solution(mesh):
    grid = P("py", "pz", None)
    return jax.shard_map(
        shards,
        mesh=mesh,
        in_specs=(grid, grid, grid, P(), P(), P(None, None, "py"), P(None, None, "pz"), P(), P(), P(), P(), P(), P()),
        out_specs=(grid, grid),
        check_vma=False,
    )
```
